32 devices in a mesh: dp: 16 (over z, y, x), mp: 2 (over core).
Axes of the slice: x: 2, y: 2, z: 4, core: 2. Of those that a mesh axis runs over, the one named last changes fastest.
Arguments:
- mask_features: bfloat16 [16, 32, 128, 256], P('dp', None, None, 'mp'), may hold values from -6 to 6
- grid_features: bfloat16 [16, 40, 40, 256], P('dp', None, None, 'mp'), may hold values from -6 to 6
- instance_cells: int32 [16, 100], P('dp'), may hold values from 0 to 1599, as said below
- instance_counts: int32 [16], replicated, may hold values from 1 to 100, as said below
- instance_labels: int32 [16, 100], P('dp'), may hold values from 0 to 79
- instance_masks: int32 [16, 100, 4096], P('dp'), may hold values 0 or 1
- mask_convs: float32 [2, 9, 256, 256], P(None, None, 'dp', 'mp'), may hold values from -0.125 to 0.125
- mask_convs_moment: float32 [2, 9, 256, 256], P(None, None, 'dp', 'mp'), may hold values from -1.7881393e-07 to 1.7881393e-07
- mask_convs_square: float32 [2, 9, 256, 256], P(None, None, 'dp', 'mp'), may hold values from 2.762352e-15 to 1.1049408e-14
- grid_first: float32 [9, 256, 512], P(None, 'dp', 'mp'), may hold values from -0.125 to 0.125
- grid_first_moment: float32 [9, 256, 512], P(None, 'dp', 'mp'), may hold values from -2.3841858e-07 to 2.3841858e-07
- grid_first_square: float32 [9, 256, 512], P(None, 'dp', 'mp'), may hold values from 4.9108476e-15 to 1.964339e-14
- grid_second: float32 [9, 512, 256], P(None, 'dp', 'mp'), may hold values from -0.0234375 to 0.0234375
- grid_second_moment: float32 [9, 512, 256], P(None, 'dp', 'mp'), may hold values from -3.8146973e-06 to 3.8146973e-06
- grid_second_square: float32 [9, 512, 256], P(None, 'dp', 'mp'), may hold values from 1.1049407e-12 to 4.4197627e-12
- class_conv: float32 [9, 512, 80], P(None, 'dp', 'mp'), may hold values from -0.09375 to 0.09375
- class_conv_moment: float32 [9, 512, 80], P(None, 'dp', 'mp'), may hold values from -4.7683716e-06 to 4.7683716e-06
- class_conv_square: float32 [9, 512, 80], P(None, 'dp', 'mp'), may hold values from 1.7264699e-12 to 6.9058795e-12
- mask_norms: float32 [4, 256], P(None, 'mp'), may hold values from 0.2 to 1.4
- mask_norms_moment: float32 [4, 256], P(None, 'mp'), may hold values from -2.9802322e-07 to 2.9802322e-07
- mask_norms_square: float32 [4, 256], P(None, 'mp'), may hold values from 7.6731995e-15 to 3.0692798e-14
- grid_norms: float32 [2, 512], P(None, 'mp'), may hold values from 0.2 to 1.4
- grid_norms_moment: float32 [2, 512], P(None, 'mp'), may hold values from -9.536743e-06 to 9.536743e-06
- grid_norms_square: float32 [2, 512], P(None, 'mp'), may hold values from 6.9058795e-12 to 2.7623518e-11
- class_bias: float32 [80], P('mp'), may hold values from -4.6 to -2
- class_bias_moment: float32 [80], P('mp'), may hold values from -6.1035156e-05 to 6.1035156e-05
- class_bias_square: float32 [80], P('mp'), may hold values from 3.0692798e-10 to 1.2277119e-09
Outputs:
- step_loss: float32 [], replicated
- gradient_norm: float32 [], replicated
- mask_convs_new: float32 [2, 9, 256, 256], P(None, None, 'dp', 'mp')
- mask_convs_moment_new: float32 [2, 9, 256, 256], P(None, None, 'dp', 'mp')
- mask_convs_square_new: float32 [2, 9, 256, 256], P(None, None, 'dp', 'mp')
- grid_first_new: float32 [9, 256, 512], P(None, 'dp', 'mp')
- grid_first_moment_new: float32 [9, 256, 512], P(None, 'dp', 'mp')
- grid_first_square_new: float32 [9, 256, 512], P(None, 'dp', 'mp')
- grid_second_new: float32 [9, 512, 256], P(None, 'dp', 'mp')
- grid_second_moment_new: float32 [9, 512, 256], P(None, 'dp', 'mp')
- grid_second_square_new: float32 [9, 512, 256], P(None, 'dp', 'mp')
- class_conv_new: float32 [9, 512, 80], P(None, 'dp', 'mp')
- class_conv_moment_new: float32 [9, 512, 80], P(None, 'dp', 'mp')
- class_conv_square_new: float32 [9, 512, 80], P(None, 'dp', 'mp')
- mask_norms_new: float32 [4, 256], P(None, 'mp')
- mask_norms_moment_new: float32 [4, 256], P(None, 'mp')
- mask_norms_square_new: float32 [4, 256], P(None, 'mp')
- grid_norms_new: float32 [2, 512], P(None, 'mp')
- grid_norms_moment_new: float32 [2, 512], P(None, 'mp')
- grid_norms_square_new: float32 [2, 512], P(None, 'mp')
- class_bias_new: float32 [80], P('mp')
- class_bias_moment_new: float32 [80], P('mp')
- class_bias_square_new: float32 [80], P('mp')
The draws below stay inside these ranges and needn't reach their ends.
Inputs may be any that keep to these rules, and one draw needn't show every extreme that they name: `instance_cells`: within an image the cells of the 100 slots are distinct. `instance_counts`: some image has 100 live instances in every draw.
All inputs are finite; a program needn't handle non-finite values. No bound on the sum of `instance_masks` on one device may be relied on, other than what follows from the above.
Results may differ from the reference program's by a relative error of at most 0.007.
The reference program's roundings to bfloat16 on the way (of `mask_low`, `hidden_mask`, `feature_map` and `kernel_rows`) count: a program that leaves them out, or rounds other values in their place, can miss the bound.
Values may be sent and summed in bfloat16 or wider, within the bound.
A program may use at most 192 MiB of HBM per device.

```python
import math
import jax
import jax.numpy as jnp
from jax import lax

C = 256
CK = 512
K = 80
GROUPS = 32
G = 40
NI = 100
HM = 32
WM = 128
PIX = 4096
IMAGES = 16
NPARAM = 3909712


def draw_instance_cells(key, part):
    sub_keys = jax.random.split(key, IMAGES)

    def one_image(sub_key):
        return jax.random.permutation(sub_key, G * G)[:NI].astype(jnp.int32)
    return jax.vmap(one_image)(sub_keys)


def draw_instance_counts(key, part):
    counts = jax.random.randint(key, (IMAGES,), 1, NI + 1, dtype=jnp.int32)
    full_image = jax.random.randint(jax.random.fold_in(key, 7), (), 0, IMAGES, dtype=jnp.int32)
    return jnp.where(jnp.arange(IMAGES) == full_image, NI, counts).astype(jnp.int32)


def touch_ends(array, stream_key, smallest, top_value):
    shape = array.shape
    place = [jax.random.randint(jax.random.fold_in(stream_key, axis), (), 0, shape[axis]) for axis in range(len(shape))]
    array = array.at[tuple(place)].set(smallest)
    longest = shape.index(max(shape))
    place[longest] = (place[longest] + 1) % shape[longest]
    return array.at[tuple(place)].set(top_value)


def steps_of(rng, shape, cuts, low, largest):
    gain, own = 1.0, jax.random.fold_in(rng, 6)
    for axis_at, blocks in cuts:
        draws = jnp.exp(jax.random.uniform(jax.random.fold_in(own, axis_at), (blocks,), jnp.float32, low / len(cuts), largest / len(cuts)))
        gain = gain * jnp.repeat(draws, shape[axis_at] // blocks).reshape([-1 if axis == axis_at else 1 for axis in range(len(shape))])
    return gain


def gaussian(rng, shape, width, most, cuts=(), kind=jnp.bfloat16):
    array = jax.random.normal(rng, shape, jnp.float32) * width
    if len(cuts) > 0:
        array = steps_of(rng, shape, cuts, -0.22, 0.18) * array
    return jnp.clip(array, min=-most, max=most).astype(kind)


def setup_inputs(seed: int = 0) -> dict:
    key_list = jax.random.split(jax.random.key(seed), 28)
    mask_features = gaussian(key_list[0], (IMAGES, HM, WM, C), 1.0, 6.0, ((0, 16), (3, 2)))
    grid_features = gaussian(key_list[1], (IMAGES, G, G, C), 1.0, 6.0, ((0, 16), (3, 2)))
    instance_cells = draw_instance_cells(jax.random.fold_in(key_list[27], 71), 0)
    instance_counts = draw_instance_counts(jax.random.fold_in(key_list[27], 71), 0)
    instance_labels = touch_ends(jax.random.randint(key_list[4], (IMAGES, NI), 0, K), jax.random.fold_in(key_list[4], 1), 0, K - 1).astype(jnp.int32)
    instance_masks = touch_ends((jax.random.randint(key_list[5], (IMAGES, NI, PIX), 0, 3) < 1).astype(jnp.int32), jax.random.fold_in(key_list[5], 1), 0, 1)
    mask_convs = gaussian(key_list[6], (2, 9, C, C), (9 * C) ** -0.5, 0.125, ((2, 16), (3, 2)), jnp.float32)
    mask_convs_moment = gaussian(key_list[7], (2, 9, C, C), (0.00006 * NPARAM ** -0.5), 1.7881393432617188e-07, ((2, 16), (3, 2)), jnp.float32)
    mask_convs_square = jnp.clip(jnp.exp(math.log(1.1049407577594893e-14) - 1.3862944 * jax.random.uniform(key_list[8], (2, 9, C, C), jnp.float32) ** steps_of(key_list[8], (2, 9, C, C), ((2, 16), (3, 2)), -0.2, 0.2)), 2.762351894398723e-15, 1.1049407577594893e-14)
    grid_first = gaussian(key_list[9], (9, C, CK), (9 * C) ** -0.5, 0.125, ((1, 16), (2, 2)), jnp.float32)
    grid_first_moment = gaussian(key_list[10], (9, C, CK), (0.00008 * NPARAM ** -0.5), 2.384185791015625e-07, ((1, 16), (2, 2)), jnp.float32)
    grid_first_square = jnp.clip(jnp.exp(math.log(1.9643390307909868e-14) - 1.3862944 * jax.random.uniform(key_list[11], (9, C, CK), jnp.float32) ** steps_of(key_list[11], (9, C, CK), ((1, 16), (2, 2)), -0.2, 0.2)), 4.910847576977467e-15, 1.9643390307909868e-14)
    grid_second = gaussian(key_list[12], (9, CK, C), (144 * CK) ** -0.5, 0.0234375, ((1, 16), (2, 2)), jnp.float32)
    grid_second_moment = gaussian(key_list[13], (9, CK, C), (0.0012 * NPARAM ** -0.5), 3.814697265625e-06, ((1, 16), (2, 2)), jnp.float32)
    grid_second_square = jnp.clip(jnp.exp(math.log(4.41976273288236e-12) - 1.3862944 * jax.random.uniform(key_list[14], (9, CK, C), jnp.float32) ** steps_of(key_list[14], (9, CK, C), ((1, 16), (2, 2)), -0.2, 0.2)), 1.10494068322059e-12, 4.41976273288236e-12)
    class_conv = gaussian(key_list[15], (9, CK, K), (9 * CK) ** -0.5, 0.09375, ((1, 16), (2, 2)), jnp.float32)
    class_conv_moment = gaussian(key_list[16], (9, CK, K), (0.0015 * NPARAM ** -0.5), 4.76837158203125e-06, ((1, 16), (2, 2)), jnp.float32)
    class_conv_square = jnp.clip(jnp.exp(math.log(6.905879514074176e-12) - 1.3862944 * jax.random.uniform(key_list[17], (9, CK, K), jnp.float32) ** steps_of(key_list[17], (9, CK, K), ((1, 16), (2, 2)), -0.2, 0.2)), 1.726469878518544e-12, 6.905879514074176e-12)
    mask_norms = jnp.clip(0.2 + 1.19999997 * jax.random.uniform(key_list[18], (4, C), jnp.float32) ** steps_of(key_list[18], (4, C), ((1, 2),), -0.2, 0.2), 0.2, 1.4)
    mask_norms_moment = gaussian(key_list[19], (4, C), (0.0001 * NPARAM ** -0.5), 2.980232238769531e-07, ((1, 2),), jnp.float32)
    mask_norms_square = jnp.clip(jnp.exp(math.log(3.069279788550476e-14) - 1.3862944 * jax.random.uniform(key_list[20], (4, C), jnp.float32) ** steps_of(key_list[20], (4, C), ((1, 2),), -0.2, 0.2)), 7.67319947137619e-15, 3.069279788550476e-14)
    grid_norms = jnp.clip(0.2 + 1.19999997 * jax.random.uniform(key_list[21], (2, CK), jnp.float32) ** steps_of(key_list[21], (2, CK), ((1, 2),), -0.2, 0.2), 0.2, 1.4)
    grid_norms_moment = gaussian(key_list[22], (2, CK), (0.003 * NPARAM ** -0.5), 9.5367431640625e-06, ((1, 2),), jnp.float32)
    grid_norms_square = jnp.clip(jnp.exp(math.log(2.7623518056296703e-11) - 1.3862944 * jax.random.uniform(key_list[23], (2, CK), jnp.float32) ** steps_of(key_list[23], (2, CK), ((1, 2),), -0.2, 0.2)), 6.905879514074176e-12, 2.7623518056296703e-11)
    class_bias = jnp.clip(-4.6 + 2.6 * jax.random.uniform(key_list[24], (K,), jnp.float32) ** steps_of(key_list[24], (K,), ((0, 2),), -0.2, 0.2), -4.6, -2.0)
    class_bias_moment = gaussian(key_list[25], (K,), (0.02 * NPARAM ** -0.5), 6.103515625e-05, ((0, 2),), jnp.float32)
    class_bias_square = jnp.clip(jnp.exp(math.log(1.2277119321169039e-09) - 1.3862944 * jax.random.uniform(key_list[26], (K,), jnp.float32) ** steps_of(key_list[26], (K,), ((0, 2),), -0.2, 0.2)), 3.0692798302922597e-10, 1.2277119321169039e-09)
    return {"mask_features": mask_features, "grid_features": grid_features, "instance_cells": instance_cells, "instance_counts": instance_counts, "instance_labels": instance_labels, "instance_masks": instance_masks, "mask_convs": mask_convs, "mask_convs_moment": mask_convs_moment, "mask_convs_square": mask_convs_square, "grid_first": grid_first, "grid_first_moment": grid_first_moment, "grid_first_square": grid_first_square, "grid_second": grid_second, "grid_second_moment": grid_second_moment, "grid_second_square": grid_second_square, "class_conv": class_conv, "class_conv_moment": class_conv_moment, "class_conv_square": class_conv_square, "mask_norms": mask_norms, "mask_norms_moment": mask_norms_moment, "mask_norms_square": mask_norms_square, "grid_norms": grid_norms, "grid_norms_moment": grid_norms_moment, "grid_norms_square": grid_norms_square, "class_bias": class_bias, "class_bias_moment": class_bias_moment, "class_bias_square": class_bias_square}


GN_EPS = 1e-05
CLIP_LIMIT = 0.02
LEARN_RATE = 0.02
SMALL_RATE = 0.5
BETA_ONE = 0.9
BETA_TWO = 0.95
ADAM_EPS = 1e-08
WEIGHT_DECAY = 0.05
CONTRAST_TEMP = 0.05
FOCAL_ALPHA = 0.25
DICE_WEIGHT = 3.0
STEP_TIME = 10.0
HIGHEST = lax.Precision.HIGHEST

@jax.custom_vjp
def low(v):
    return lax.optimization_barrier(v.astype(jnp.bfloat16)).astype(jnp.float32)

@jax.custom_vjp
def low_back(v):
    return v

def low_keep(v):
    return (low(v), None)

def low_pass(kept, grad):
    return (grad,)

def back_keep(v):
    return (v, None)

def back_low(kept, grad):
    return (low(grad),)
low.defvjp(low_keep, low_pass)
low_back.defvjp(back_keep, back_low)

def shifted_view(padded, tap_index, height, columns):
    row_start = tap_index // 3
    col_start = tap_index % 3
    return padded[row_start:row_start + height, col_start:col_start + columns]

def convolve(values, weight):
    height, columns = (values.shape[0], values.shape[1])
    padded = jnp.pad(values, ((1, 1), (1, 1), (0, 0)))
    summed = jnp.zeros((height, columns, weight.shape[2]), jnp.float32)
    for tap_index in range(9):
        summed = summed + jnp.einsum('hwc,cd->hwd', shifted_view(padded, tap_index, height, columns), weight[tap_index], precision=HIGHEST)
    return summed

def norm_act(values, gain_row, bias_row):
    height, columns, channels = values.shape
    group_width = channels // GROUPS
    grouped = values.reshape(height * columns, GROUPS, group_width)
    group_mean = lax.optimization_barrier(jnp.mean(grouped, axis=(0, 2), keepdims=True))
    group_var = lax.optimization_barrier(jnp.mean(jnp.square(grouped - group_mean), axis=(0, 2), keepdims=True))
    normed = ((grouped - group_mean) * lax.rsqrt(group_var + GN_EPS)).reshape(height, columns, channels)
    return jax.nn.relu(normed * gain_row + bias_row)

def mask_losses(logits, class_logits, cell_ids, live_count, labels, mask_bits):
    live_slots = (jnp.arange(NI) < live_count).astype(jnp.float32)
    count_float = live_count.astype(jnp.float32)
    probability = jax.nn.sigmoid(logits)
    mask_float = mask_bits.astype(jnp.float32)
    intersection = lax.optimization_barrier(jnp.sum(probability * mask_float.T, axis=0))
    denominator = lax.optimization_barrier(jnp.sum(probability * probability, axis=0)) + lax.optimization_barrier(jnp.sum(mask_float, axis=1)) + 1.0
    dice_loss = jnp.sum(live_slots * (1.0 - 2.0 * intersection / denominator)) / count_float
    cell_hot = (cell_ids[:, None] == jnp.arange(G * G)[None, :]).astype(jnp.float32) * live_slots[:, None]
    class_hot = (labels[:, None] == jnp.arange(K)[None, :]).astype(jnp.float32)
    target = jnp.dot(cell_hot.T, class_hot, precision=HIGHEST)
    class_prob = jax.nn.sigmoid(class_logits)
    log_pos = -jax.nn.softplus(-class_logits)
    log_neg = -jax.nn.softplus(class_logits)
    focal_terms = FOCAL_ALPHA * target * jnp.square(1.0 - class_prob) * log_pos + (1.0 - FOCAL_ALPHA) * (1.0 - target) * jnp.square(class_prob) * log_neg
    focal_loss = -jnp.sum(focal_terms) / (count_float + 1.0)
    return (focal_loss, dice_loss)

def contrast_loss(unscaled_scores, norms_all, row_start, live_slots, live_count, live_all):
    reciprocal_norm = lax.rsqrt(norms_all + 1e-06)
    reciprocal_row_norms = lax.dynamic_slice_in_dim(reciprocal_norm, row_start, NI)
    similarity_scores = unscaled_scores * reciprocal_row_norms[:, None] * reciprocal_norm[None, :] / CONTRAST_TEMP
    key_index = jnp.arange(norms_all.shape[0])
    query_index = row_start + jnp.arange(NI)
    allowed = (live_all[None, :] > 0.5) & (key_index[None, :] != query_index[:, None])
    similarity_scores = jnp.where(allowed, similarity_scores, -1000000000.0)
    top_score = lax.optimization_barrier(jnp.max(similarity_scores, axis=1, keepdims=True))
    log_total = top_score[:, 0] + jnp.log(lax.optimization_barrier(jnp.sum(jnp.exp(similarity_scores - top_score), axis=1)))
    return jnp.sum(live_slots * log_total) / live_count.astype(jnp.float32)

def image_terms(item, mask_low, grid_first_low, grid_second_low, class_low, mask_norms, grid_norms, class_bias):
    mask_in, grid_in, cell_ids, live_count, labels, mask_bits = item
    first_mask = low_back(convolve(mask_in, mask_low[0]))
    hidden_mask = low(norm_act(first_mask, mask_norms[0], mask_norms[1]))
    second_mask = low_back(convolve(hidden_mask, mask_low[1]))
    feature_map = low(norm_act(second_mask, mask_norms[2], mask_norms[3])).reshape(-1, C)
    first_grid = low_back(convolve(grid_in, grid_first_low))
    hidden_grid = low(norm_act(first_grid, grid_norms[0], grid_norms[1]))
    kernels = low_back(convolve(hidden_grid, grid_second_low).reshape(G * G, C))
    class_logits = low_back(convolve(hidden_grid, class_low).reshape(G * G, K) + class_bias)
    kernel_rows = low(jnp.take(kernels, cell_ids, axis=0))
    logits = low_back(jnp.dot(feature_map, kernel_rows.T, precision=HIGHEST))
    focal_loss, dice_loss = mask_losses(logits, class_logits, cell_ids, live_count, labels, mask_bits)
    return (focal_loss + DICE_WEIGHT * dice_loss, kernel_rows)

def adam_update(weight, moment, square, gradient, rate):
    moment_new = BETA_ONE * moment + (1.0 - BETA_ONE) * gradient
    square_new = BETA_TWO * square + (1.0 - BETA_TWO) * gradient * gradient
    moment_hat = moment_new / (1.0 - BETA_ONE ** STEP_TIME)
    square_hat = square_new / (1.0 - BETA_TWO ** STEP_TIME)
    weight_new = weight - rate * (moment_hat / (jnp.sqrt(square_hat) + ADAM_EPS) + WEIGHT_DECAY * weight)
    return (weight_new, moment_new, square_new)

def reference(mask_features, grid_features, instance_cells, instance_counts, instance_labels, instance_masks, mask_convs, mask_convs_moment, mask_convs_square, grid_first, grid_first_moment, grid_first_square, grid_second, grid_second_moment, grid_second_square, class_conv, class_conv_moment, class_conv_square, mask_norms, mask_norms_moment, mask_norms_square, grid_norms, grid_norms_moment, grid_norms_square, class_bias, class_bias_moment, class_bias_square):
    mask_float = mask_features.astype(jnp.float32)
    grid_float = grid_features.astype(jnp.float32)
    live_all = (jnp.arange(NI)[None, :] < instance_counts[:, None]).astype(jnp.float32).reshape(-1)
    starts = (jnp.arange(IMAGES) * NI).astype(jnp.int32)

    def total_loss(params):
        mask_weight, first_w, second_w, class_w, mask_norm_w, grid_norm_weight, bias_w = params
        mask_low, first_low, second_low, class_low = (low(mask_weight), low(first_w), low(second_w), low(class_w))

        def per_image(item):
            return image_terms(item, mask_low, first_low, second_low, class_low, mask_norm_w, grid_norm_weight, bias_w)
        terms, kernel_sets = lax.map(jax.checkpoint(per_image), (mask_float, grid_float, instance_cells, instance_counts, instance_labels, instance_masks))
        kernel_all = kernel_sets.reshape(IMAGES * NI, C)
        norms_all = lax.optimization_barrier(jnp.sum(kernel_all * kernel_all, axis=1))

        def per_block(item):
            query_rows, row_start, live_count = item
            live_slots = (jnp.arange(NI) < live_count).astype(jnp.float32)
            unscaled_scores = low_back(jnp.dot(query_rows, kernel_all.T, precision=HIGHEST))
            return contrast_loss(unscaled_scores, norms_all, row_start, live_slots, live_count, live_all)
        contrasts = lax.map(jax.checkpoint(per_block), (kernel_sets, starts, instance_counts))
        return (jnp.sum(terms) + jnp.sum(contrasts)) / IMAGES
    params = (mask_convs, grid_first, grid_second, class_conv, mask_norms, grid_norms, class_bias)
    step_loss, back_fn = jax.vjp(total_loss, params)
    gradients = back_fn(jnp.ones_like(step_loss))[0]
    total_squares = sum((jnp.sum(jnp.square(entry)) for entry in gradients))
    gradient_norm = jnp.sqrt(total_squares)
    factor = jnp.minimum(1.0, CLIP_LIMIT / gradient_norm)
    moments = ((mask_convs_moment, mask_convs_square), (grid_first_moment, grid_first_square), (grid_second_moment, grid_second_square), (class_conv_moment, class_conv_square), (mask_norms_moment, mask_norms_square), (grid_norms_moment, grid_norms_square), (class_bias_moment, class_bias_square))
    rates = (LEARN_RATE,) * 4 + (SMALL_RATE,) * 3
    results = []
    for weight, state, gradient, rate in zip(params, moments, gradients, rates):
        results.extend(adam_update(weight, state[0], state[1], gradient * factor, rate))
    return (step_loss, gradient_norm, results[0], results[1], results[2], results[3], results[4], results[5], results[6], results[7], results[8], results[9], results[10], results[11], results[12], results[13], results[14], results[15], results[16], results[17], results[18], results[19], results[20])
```

```python
from functools import partial

import jax
import jax.numpy as jnp
from jax import lax
from jax.experimental import pallas as pl
from jax.experimental.pallas import tpu as pltpu
from jax.sharding import PartitionSpec as P

GROUPS = 32
G = 40
NI = 100


GN_EPS = 1e-05
CLIP_LIMIT = 0.02
LEARN_RATE = 0.02
SMALL_RATE = 0.5
BETA_ONE = 0.9
BETA_TWO = 0.95
ADAM_EPS = 1e-08
WEIGHT_DECAY = 0.05
CONTRAST_TEMP = 0.05
FOCAL_ALPHA = 0.25
DICE_WEIGHT = 3.0
STEP_TIME = 10.0
HIGHEST = lax.Precision.HIGHEST


MESH = pl.DeviceIdType.MESH
VMEM = pltpu.VMEM
ANY = pl.ANY
VMEM_LIMIT = 60 * 2**20
F32 = jnp.float32
BF16 = jnp.bfloat16


def line_lengths(total):
    if total & (total - 1):
        return (total, 1, 1)
    bits = total.bit_length() - 1
    last = bits // 3
    middle = (bits - last) // 2
    return (1 << (bits - last - middle), 1 << middle, 1 << last)


def place(dims):
    index = lax.axis_index("dp")
    return (index // (dims[1] * dims[2]), (index // dims[2]) % dims[1], index % dims[2])


def along(dims, axis, step):
    stride = (dims[1] * dims[2], dims[2], 1)[axis]
    return {"dp": lax.axis_index("dp") + step * stride}


def partner():
    return {"mp": 1 - lax.axis_index("mp")}


def greet_lines(dims, pair):
    sem = pltpu.get_barrier_semaphore()
    pos = place(dims)
    count = jnp.int32(0)
    for axis in range(3):
        for step in (-1, 1):
            there = (pos[axis] + step >= 0) & (pos[axis] + step < dims[axis])

            @pl.when(there)
            def _(axis=axis, step=step):
                pl.semaphore_signal(
                    sem, inc=1, device_id=along(dims, axis, step), device_id_type=MESH
                )

            count = count + there.astype(jnp.int32)
    if pair:
        pl.semaphore_signal(sem, inc=1, device_id=partner(), device_id_type=MESH)
        count = count + 1
    pl.semaphore_wait(sem, count)


def greet_partner():
    sem = pltpu.get_barrier_semaphore()
    pl.semaphore_signal(sem, inc=1, device_id=partner(), device_id_type=MESH)
    pl.semaphore_wait(sem, 1)


def ring_step(dims, pos, axis, offset):
    other = lax.rem(pos[axis] + offset, dims[axis])
    return along(dims, axis, other - pos[axis])


def greet_all_lines(dims):
    sem = pltpu.get_barrier_semaphore()
    pos = place(dims)
    count = 1
    for axis in range(3):
        for offset in range(1, dims[axis]):
            pl.semaphore_signal(
                sem, inc=1, device_id=ring_step(dims, pos, axis, offset), device_id_type=MESH
            )
            count += 1
    pl.semaphore_signal(sem, inc=1, device_id=partner(), device_id_type=MESH)
    pl.semaphore_wait(sem, count)


GATHER_ORDERS = ((2, 1, 0), (0, 2, 1), (0, 1, 2))
REDUCE_ORDERS = tuple(tuple(reversed(order)) for order in GATHER_ORDERS)


def rounds_of(dims, order):
    return [
        (stage, axis, step) for stage, axis in enumerate(order) for step in range(dims[axis] - 1)
    ]


def round_count(dims):
    return sum(n - 1 for n in dims)


def row_cuts(rows, unit=16):
    if rows % unit or rows < 3 * unit:
        return ((0, 0, rows),)
    tiles = rows // unit
    first = max(1, round(tiles * 0.2))
    second = (tiles - first) // 2
    sizes = (first, second, tiles - first - second)
    cuts, start = [], 0
    for order, size in enumerate(sizes):
        cuts.append((order, start * unit, size * unit))
        start += size
    return tuple(cuts)


class Flow:
    def __init__(self, rounds):
        self.rounds = rounds

    def start(self, r):
        for copy, sends, *_ in self.rounds[r]:

            @pl.when(sends)
            def _(copy=copy):
                copy.start()

    def finish(self, r):
        for copy, _, receives, land in self.rounds[r]:

            @pl.when(receives)
            def _(copy=copy, land=land):
                copy.wait_recv()
                if land is not None:
                    land()

    def drain(self):
        for copies in self.rounds:
            for copy, sends, *_ in copies:

                @pl.when(sends)
                def _(copy=copy):
                    copy.wait_send()


def gather_flow(dims, out, send_sems, recv_sems, base, rows, order):
    pos = place(dims)
    result = []
    for r, (stage, axis, step) in enumerate(rounds_of(dims, order)):
        n, done = dims[axis], set(order[:stage])
        copies = []
        for side, delta in ((0, 1), (1, -1)):
            block = pos[axis] - delta * step
            sends = (
                (pos[axis] + delta >= 0)
                & (pos[axis] + delta < n)
                & (block >= 0)
                & (block < n)
            )
            block = jnp.clip(block, 0, n - 1)
            source = pos[axis] - delta * (1 + step)
            receives = (source >= 0) & (source < n)
            view = out.at[
                tuple(
                    pl.ds(0, dims[k]) if k in done else (block if k == axis else pos[k])
                    for k in range(3)
                )
                + (rows,)
            ]
            copy = pltpu.make_async_remote_copy(
                src_ref=view,
                dst_ref=view,
                send_sem=send_sems.at[base + 2 * r + side],
                recv_sem=recv_sems.at[base + 2 * r + side],
                device_id=along(dims, axis, delta),
                device_id_type=MESH,
            )
            copies.append((copy, sends, receives, None))
        result.append(copies)
    return Flow(result)


def landing_shapes(dims, rows, width, order):
    shapes, left = [], {0, 1, 2}
    for axis in order:
        left = left - {axis}
        n = dims[axis]
        slots = max(1, n - 1) * (1 if n <= 2 else 2)
        shapes.append((slots,) + tuple(dims[k] for k in sorted(left)) + (rows, width))
    return shapes


def reduce_flow(dims, total, staged, lands, send_sems, recv_sems, base, rows, order):
    pos = place(dims)
    result = []
    for r, (stage, axis, step) in enumerate(rounds_of(dims, order)):
        n, reduced = dims[axis], set(order[:stage])
        free = [k for k in range(3) if k not in reduced and k != axis]

        def view(block, lead=None, axis=axis, reduced=reduced):
            lead = iter(lead) if lead is not None else None
            index = []
            for k in range(3):
                if k == axis:
                    index.append(block)
                elif k in reduced:
                    index.append(pos[k])
                else:
                    index.append(pl.ds(0, dims[k]) if lead is None else next(lead))
            return tuple(index) + (rows,)

        copies = []
        for side, delta in ((0, 1), (1, -1)):
            place_in_flow = pos[axis] if delta == 1 else n - 1 - pos[axis]
            sends = place_in_flow <= step
            block = n - 1 - step + place_in_flow
            block = jnp.clip(block if delta == 1 else n - 1 - block, 0, n - 1)
            receives = (place_in_flow >= 1) & (place_in_flow - 1 <= step)
            taken = n - 1 - step + place_in_flow - 1
            taken = jnp.clip(taken if delta == 1 else n - 1 - taken, 0, n - 1)
            land_ref = lands[stage].at[step if n <= 2 else side * (n - 1) + step]
            copy = pltpu.make_async_remote_copy(
                src_ref=staged.at[view(block)],
                dst_ref=land_ref,
                send_sem=send_sems.at[base + 2 * r + side],
                recv_sem=recv_sems.at[base + 2 * r + side],
                device_id=along(dims, axis, delta),
                device_id_type=MESH,
            )

            def land(taken=taken, land_ref=land_ref, free=free, view=view):
                sizes = [dims[k] for k in free]
                blocks = 1
                for size in sizes:
                    blocks *= size

                def add(i, carry):
                    lead, rest = [], i
                    for size in reversed(sizes):
                        lead.append(lax.rem(rest, size))
                        rest = rest // size
                    lead = lead[::-1]
                    index = view(taken, lead)
                    value = total[index] + land_ref[tuple(lead)].astype(F32)
                    total[index] = value
                    staged[index] = value.astype(BF16)
                    return carry

                if blocks == 1:
                    add(jnp.int32(0), 0)
                else:
                    lax.fori_loop(0, blocks, add, 0)

            copies.append((copy, sends, receives, land))
        result.append(copies)
    return Flow(result)


def run_flows(flows, count):
    for r in range(count + 1):
        for flow in flows:
            if r > 0:
                flow.finish(r - 1)
            if r < count:
                flow.start(r)
    for flow in flows:
        flow.drain()


def params(collective_id):
    return pltpu.CompilerParams(
        collective_id=collective_id, has_side_effects=True, vmem_limit_bytes=VMEM_LIMIT
    )


def gather_kernel(dims, count, maps, *refs):
    shards, inputs = refs[:count], refs[count : count + maps]
    at = count + maps
    outs, fulls = refs[at : at + count], refs[at + count : at + count + maps]
    send_sems, recv_sems, local_sems, pair_sems = refs[at + count + maps :]
    pos = place(dims)
    model = lax.axis_index("mp")
    local = []
    for i in range(count):
        local.append(
            pltpu.make_async_copy(
                shards[i], outs[i].at[pos[0], pos[1], pos[2]], local_sems.at[i]
            )
        )
    for i in range(maps):
        width = inputs[i].shape[1]
        lanes = pl.ds(pl.multiple_of(model * width, width), width)
        local.append(
            pltpu.make_async_copy(inputs[i], fulls[i].at[:, lanes], local_sems.at[count + i])
        )
    for copy in local:
        copy.start()
    greet_lines(dims, True)
    pairs = []
    for i in range(maps):
        width = inputs[i].shape[1]
        lanes = pl.ds(pl.multiple_of(model * width, width), width)
        pairs.append(
            pltpu.make_async_remote_copy(
                src_ref=inputs[i],
                dst_ref=fulls[i].at[:, lanes],
                send_sem=pair_sems.at[0, i],
                recv_sem=pair_sems.at[1, i],
                device_id=partner(),
                device_id_type=MESH,
            )
        )
    for copy in pairs:
        copy.start()
    for copy in local:
        copy.wait()
    per_flow = 2 * round_count(dims)
    flows, base = [], 0
    for i in range(count):
        for order, start, size in row_cuts(shards[i].shape[0]):
            flows.append(
                gather_flow(
                    dims,
                    outs[i],
                    send_sems,
                    recv_sems,
                    base,
                    pl.ds(start, size),
                    GATHER_ORDERS[order],
                )
            )
            base += per_flow
    run_flows(flows, round_count(dims))
    for copy in pairs:
        copy.wait()


def gather_all(dims, shards, maps):
    count = len(shards)
    slots = 2 * round_count(dims) * sum(len(row_cuts(s.shape[0])) for s in shards)
    slots = max(slots, 1)
    shapes = [jax.ShapeDtypeStruct(dims + s.shape, s.dtype) for s in shards]
    shapes += [jax.ShapeDtypeStruct((m.shape[0], 2 * m.shape[1]), m.dtype) for m in maps]
    result = pl.pallas_call(
        partial(gather_kernel, dims, count, len(maps)),
        name="gather_weights",
        out_shape=shapes,
        in_specs=[pl.BlockSpec(memory_space=VMEM)] * (count + len(maps)),
        out_specs=[pl.BlockSpec(memory_space=VMEM)] * (count + len(maps)),
        scratch_shapes=[
            pltpu.SemaphoreType.DMA((slots,)),
            pltpu.SemaphoreType.DMA((slots,)),
            pltpu.SemaphoreType.DMA((count + len(maps),)),
            pltpu.SemaphoreType.DMA((2, len(maps))),
        ],
        compiler_params=params(0),
    )(*shards, *maps)
    return result[:count], result[count:]


def reduce_kernel(dims, count, *refs):
    parts, outs = refs[:count], refs[count : 2 * count]
    send_sems, recv_sems, local_sems = refs[2 * count : 2 * count + 3]
    rest = list(refs[2 * count + 3 :])
    totals, staged, rest = rest[:count], rest[count : 2 * count], rest[2 * count :]
    pos = place(dims)
    local = [
        pltpu.make_async_copy(parts[i], totals[i], local_sems.at[i]) for i in range(count)
    ]
    for copy in local:
        copy.start()
    greet_lines(dims, False)
    per_flow = 2 * round_count(dims)
    flows, base = [], 0
    for i in range(count):
        for order, start, size in row_cuts(parts[i].shape[3]):
            lands, rest = rest[:3], rest[3:]
            flows.append(
                reduce_flow(
                    dims,
                    totals[i],
                    staged[i],
                    lands,
                    send_sems,
                    recv_sems,
                    base,
                    pl.ds(start, size),
                    REDUCE_ORDERS[order],
                )
            )
            base += per_flow
    for i in range(count):
        local[i].wait()

        def cast(j, carry, i=i):
            index = (j // (dims[1] * dims[2]), lax.rem(j // dims[2], dims[1]), lax.rem(j, dims[2]))
            staged[i][index] = totals[i][index].astype(BF16)
            return carry

        lax.fori_loop(0, dims[0] * dims[1] * dims[2], cast, 0)
    run_flows(flows, round_count(dims))
    for i in range(count):
        outs[i][...] = totals[i][pos[0], pos[1], pos[2]]


def reduce_all(dims, parts):
    count = len(parts)
    cuts = [row_cuts(p.shape[3]) for p in parts]
    slots = max(1, 2 * round_count(dims) * sum(len(c) for c in cuts))
    scratch = [
        pltpu.SemaphoreType.DMA((slots,)),
        pltpu.SemaphoreType.DMA((slots,)),
        pltpu.SemaphoreType.DMA((count,)),
    ]
    scratch += [VMEM(p.shape, F32) for p in parts] + [VMEM(p.shape, BF16) for p in parts]
    for part, cut in zip(parts, cuts):
        for order, _, size in cut:
            for shape in landing_shapes(dims, size, part.shape[4], REDUCE_ORDERS[order]):
                scratch.append(VMEM(shape, BF16))
    return pl.pallas_call(
        partial(reduce_kernel, dims, count),
        name="reduce_gradients",
        out_shape=[jax.ShapeDtypeStruct(p.shape[3:], F32) for p in parts],
        in_specs=[pl.BlockSpec(memory_space=ANY)] * count,
        out_specs=[pl.BlockSpec(memory_space=VMEM)] * count,
        scratch_shapes=scratch,
        compiler_params=params(1),
    )(*parts)


def share_kernel(dims, own, out, send_sems, recv_sems, local_sem):
    pos = place(dims)
    model = lax.axis_index("mp")
    local = pltpu.make_async_copy(own, out.at[pos[0], pos[1], pos[2], model], local_sem)
    local.start()
    greet_all_lines(dims)
    local.wait()
    done, slot, sent = set(), 0, []
    for axis in (2, 1, 0):
        view = out.at[
            tuple(pl.ds(0, dims[k]) if k in done else pos[k] for k in range(3)) + (model,)
        ]
        now = []
        for offset in range(1, dims[axis]):
            now.append(
                pltpu.make_async_remote_copy(
                    src_ref=view,
                    dst_ref=view,
                    send_sem=send_sems.at[slot],
                    recv_sem=recv_sems.at[slot],
                    device_id=ring_step(dims, pos, axis, offset),
                    device_id_type=MESH,
                )
            )
            slot += 1
        for copy in now:
            copy.start()
        for copy in now:
            copy.wait_recv()
        sent += now
        done.add(axis)
    view = out.at[:, :, :, model]
    last = pltpu.make_async_remote_copy(
        src_ref=view,
        dst_ref=view,
        send_sem=send_sems.at[slot],
        recv_sem=recv_sems.at[slot],
        device_id=partner(),
        device_id_type=MESH,
    )
    last.start()
    last.wait()
    for copy in sent:
        copy.wait_send()


def share(dims, own, collective_id):
    slots = round_count(dims) + 1
    return pl.pallas_call(
        partial(share_kernel, dims),
        name="share_blocks",
        out_shape=jax.ShapeDtypeStruct(dims + (2,) + own.shape, own.dtype),
        in_specs=[pl.BlockSpec(memory_space=VMEM)],
        out_specs=pl.BlockSpec(memory_space=VMEM),
        scratch_shapes=[
            pltpu.SemaphoreType.DMA((slots,)),
            pltpu.SemaphoreType.DMA((slots,)),
            pltpu.SemaphoreType.DMA,
        ],
        compiler_params=params(collective_id),
    )(own)


def swap_kernel(count, *refs):
    ins, outs = refs[:count], refs[count : 2 * count]
    send_sems, recv_sems = refs[2 * count :]
    greet_partner()
    copies = [
        pltpu.make_async_remote_copy(
            src_ref=ins[i],
            dst_ref=outs[i],
            send_sem=send_sems.at[i],
            recv_sem=recv_sems.at[i],
            device_id=partner(),
            device_id_type=MESH,
        )
        for i in range(count)
    ]
    for copy in copies:
        copy.start()
    for copy in copies:
        copy.wait()


def swap(arrays, collective_id):
    count = len(arrays)
    return pl.pallas_call(
        partial(swap_kernel, count),
        name="swap_cores",
        out_shape=[jax.ShapeDtypeStruct(a.shape, a.dtype) for a in arrays],
        in_specs=[pl.BlockSpec(memory_space=VMEM)] * count,
        out_specs=[pl.BlockSpec(memory_space=VMEM)] * count,
        scratch_shapes=[
            pltpu.SemaphoreType.DMA((count,)),
            pltpu.SemaphoreType.DMA((count,)),
        ],
        compiler_params=params(collective_id),
    )(*arrays)

def flat_rows(weight):
    return weight.reshape(-1, weight.shape[-1])


def columns_in_lanes(weight):
    _, depth, width = weight.shape
    return weight.reshape(3, 3, depth, width).transpose(0, 2, 1, 3).reshape(3, depth, 3 * width)


def columns_from_lanes(weight):
    _, depth, width = weight.shape
    return (
        weight.reshape(3, depth, 3, width // 3).transpose(0, 2, 1, 3).reshape(9, depth, width // 3)
    )


def whole_weight(blocks, taps):
    rows, width = blocks.shape[3:]
    return (
        blocks.reshape(-1, taps, rows // taps, width)
        .transpose(1, 0, 2, 3)
        .reshape(taps, -1, width)
    )


def owner_blocks(gradient, dims):
    taps, _, width = gradient.shape
    owners = dims[0] * dims[1] * dims[2]
    return (
        gradient.reshape(taps, owners, -1, width)
        .transpose(1, 0, 2, 3)
        .reshape(dims + (-1, width))
    )


def both_cores(arrays, model_index, collective_id):
    flat = [flat_rows(a) for a in arrays]
    others = swap(flat, collective_id)
    first = model_index == 0
    return [
        jnp.where(
            first, jnp.concatenate([own, other], axis=1), jnp.concatenate([other, own], axis=1)
        ).reshape(a.shape[:-1] + (-1,))
        for a, own, other in zip(arrays, flat, others)
    ]


def own_half_sums(arrays, model_index, collective_id):
    halves = []
    for array in arrays:
        flat = flat_rows(array)
        halves.append(flat.reshape(flat.shape[0], 2, -1))
    away = [
        lax.dynamic_index_in_dim(half, 1 - model_index, 1, keepdims=False) for half in halves
    ]
    here = [lax.dynamic_index_in_dim(half, model_index, 1, keepdims=False) for half in halves]
    received = swap(away, collective_id)
    return [
        (own.astype(jnp.float32) + other.astype(jnp.float32)).reshape(a.shape[:-1] + (-1,))
        for a, own, other in zip(arrays, here, received)
    ]


def shifted_view(padded, tap_index, height, columns, direction):
    row_start = 1 + direction * (tap_index // 3 - 1)
    col_start = 1 + direction * (tap_index % 3 - 1)
    return padded[row_start : row_start + height, col_start : col_start + columns]


def padding(values):
    return jnp.pad(values, ((1, 1), (1, 1), (0, 0)))


def convolve(values, weight):
    height, columns = (values.shape[0], values.shape[1])
    padded = padding(values)
    summed = jnp.zeros((height, columns, weight.shape[2]), jnp.float32)
    for tap_index in range(9):
        summed = summed + jnp.einsum(
            "hwc,cd->hwd",
            shifted_view(padded, tap_index, height, columns, 1),
            weight[tap_index],
            preferred_element_type=jnp.float32,
        )
    return summed


def conv_input_grad(gradient, weight):
    height, columns = (gradient.shape[0], gradient.shape[1])
    padded = padding(gradient)
    summed = jnp.zeros((height, columns, weight.shape[1]), jnp.float32)
    for tap_index in range(9):
        summed = summed + jnp.einsum(
            "hwd,cd->hwc",
            shifted_view(padded, tap_index, height, columns, -1),
            weight[tap_index],
            preferred_element_type=jnp.float32,
        )
    return summed


def conv_weight_grad(values, gradient):
    height, columns = (values.shape[0], values.shape[1])
    padded = padding(values)
    return jnp.stack(
        [
            jnp.einsum(
                "hwc,hwd->cd",
                shifted_view(padded, tap_index, height, columns, 1),
                gradient,
                preferred_element_type=jnp.float32,
            )
            for tap_index in range(9)
        ]
    )


def norm_act(values, gain_row, bias_row, group_width):
    height, columns, channels = values.shape
    grouped = values.reshape(height * columns, channels // group_width, group_width)
    group_mean = jnp.mean(grouped, axis=(0, 2), keepdims=True)
    group_var = jnp.mean(jnp.square(grouped - group_mean), axis=(0, 2), keepdims=True)
    normed = ((grouped - group_mean) * lax.rsqrt(group_var + GN_EPS)).reshape(
        height, columns, channels
    )
    return jax.nn.relu(normed * gain_row + bias_row)


def pixel_sums(logits, mask_cols):
    probability = jax.nn.sigmoid(logits)
    return (jnp.sum(probability * mask_cols, axis=0), jnp.sum(probability * probability, axis=0))


def dice_from(intersection, squares_sum, mask_sum, live_slots, live_count):
    denominator = squares_sum + mask_sum + 1.0
    return jnp.sum(live_slots * (1.0 - 2.0 * intersection / denominator)) / live_count.astype(
        jnp.float32
    )


def focal_part(class_logits, cell_ids, live_slots, live_count, labels, class_start):
    cell_hot = (cell_ids[:, None] == jnp.arange(G * G)[None, :]).astype(jnp.float32) * live_slots[
        :, None
    ]
    class_hot = (
        labels[:, None] == class_start + jnp.arange(class_logits.shape[1])[None, :]
    ).astype(jnp.float32)
    target = jnp.dot(cell_hot.T, class_hot, precision=HIGHEST)
    class_prob = jax.nn.sigmoid(class_logits)
    log_pos = -jax.nn.softplus(-class_logits)
    log_neg = -jax.nn.softplus(class_logits)
    focal_terms = (
        FOCAL_ALPHA * target * jnp.square(1.0 - class_prob) * log_pos
        + (1.0 - FOCAL_ALPHA) * (1.0 - target) * jnp.square(class_prob) * log_neg
    )
    return -jnp.sum(focal_terms) / (live_count.astype(jnp.float32) + 1.0)


def adam_update(weight, moment, square, gradient, rate):
    moment_new = BETA_ONE * moment + (1.0 - BETA_ONE) * gradient
    square_new = BETA_TWO * square + (1.0 - BETA_TWO) * gradient * gradient
    moment_hat = moment_new / (1.0 - BETA_ONE**STEP_TIME)
    square_hat = square_new / (1.0 - BETA_TWO**STEP_TIME)
    weight_new = weight - rate * (
        moment_hat / (jnp.sqrt(square_hat) + ADAM_EPS) + WEIGHT_DECAY * weight
    )
    return (weight_new, moment_new, square_new)


def body(
    mask_features,
    grid_features,
    instance_cells,
    instance_counts,
    instance_labels,
    instance_masks,
    mask_convs,
    mask_convs_moment,
    mask_convs_square,
    grid_first,
    grid_first_moment,
    grid_first_square,
    grid_second,
    grid_second_moment,
    grid_second_square,
    class_conv,
    class_conv_moment,
    class_conv_square,
    mask_norms,
    mask_norms_moment,
    mask_norms_square,
    grid_norms,
    grid_norms_moment,
    grid_norms_square,
    class_bias,
    class_bias_moment,
    class_bias_square,
):
    image_total = lax.axis_size("dp")
    model_total = lax.axis_size("mp")
    data_index = lax.axis_index("dp")
    model_index = lax.axis_index("mp")
    dims = line_lengths(image_total)
    pixels_high, pixels_wide, _ = mask_features.shape[1:]
    class_share = class_conv.shape[2]
    shards = [
        flat_rows(mask_convs[0]),
        flat_rows(grid_first),
        flat_rows(mask_convs[1]),
        flat_rows(grid_second),
        flat_rows(columns_in_lanes(class_conv)),
    ]
    gathered, maps = gather_all(
        dims,
        [shard.astype(jnp.bfloat16) for shard in shards],
        [
            mask_features.reshape(-1, mask_features.shape[3]),
            grid_features.reshape(-1, grid_features.shape[3]),
        ],
    )
    mask_low = [whole_weight(gathered[0], 9), whole_weight(gathered[2], 9)]
    first_low = whole_weight(gathered[1], 9)
    second_low = whole_weight(gathered[3], 9)
    class_low = columns_from_lanes(whole_weight(gathered[4], 3))
    mask_full = maps[0].reshape(pixels_high, pixels_wide, -1)
    grid_full = maps[1].reshape(G, G, -1)
    mask_width = mask_full.shape[2] // GROUPS
    grid_width = first_low.shape[2] * model_total // GROUPS
    mask_norm_act = partial(norm_act, group_width=mask_width)
    grid_norm_act = partial(norm_act, group_width=grid_width)
    first_mask = convolve(mask_full, mask_low[0])
    first_grid = convolve(grid_full, first_low)
    hidden_mask, back_mask_one = jax.vjp(mask_norm_act, first_mask, mask_norms[0], mask_norms[1])
    hidden_grid, back_grid_one = jax.vjp(grid_norm_act, first_grid, grid_norms[0], grid_norms[1])
    hidden_mask_full, hidden_grid_full = both_cores(
        [hidden_mask.astype(jnp.bfloat16), hidden_grid.astype(jnp.bfloat16)], model_index, 2
    )
    second_mask = convolve(hidden_mask_full, mask_low[1])
    kernels = convolve(hidden_grid_full, second_low)
    class_part = convolve(hidden_grid_full, class_low)
    feature_map, back_mask_two = jax.vjp(mask_norm_act, second_mask, mask_norms[2], mask_norms[3])
    local_width = feature_map.shape[2]
    feature_low = feature_map.astype(jnp.bfloat16).reshape(-1, local_width)
    kernel_flat = kernels.reshape(-1, local_width)
    cell_ids = instance_cells[0]
    kernel_rows = jnp.take(kernel_flat, cell_ids, axis=0).astype(jnp.bfloat16)
    joined = share(dims, kernel_rows, 3)
    kernel_all = (
        joined.reshape(image_total, model_total, NI, local_width)
        .transpose(0, 2, 1, 3)
        .reshape(image_total * NI, model_total * local_width)
    )
    row_start = data_index * NI
    kernel_full = lax.dynamic_slice_in_dim(kernel_all, row_start, NI, 0)
    unscaled_scores = jnp.dot(kernel_full, kernel_all.T, preferred_element_type=jnp.float32)
    norms_all = jnp.sum(jnp.square(kernel_all.astype(jnp.float32)), axis=1)
    live_count = lax.dynamic_index_in_dim(instance_counts, data_index, keepdims=False)
    live_slots = (jnp.arange(NI) < live_count).astype(jnp.float32)
    live_all = (jnp.arange(NI)[None, :] < instance_counts[:, None]).astype(jnp.float32).reshape(-1)
    mask_cols = instance_masks[0].T.astype(jnp.float32)
    mask_sum = jnp.sum(mask_cols, axis=0)
    logits_part = jnp.dot(
        feature_low, kernel_rows.T, preferred_element_type=jnp.float32
    ).astype(jnp.bfloat16)
    logits = logits_part.astype(jnp.float32) + swap([logits_part], 4)[0].astype(jnp.float32)
    (intersection, squares_sum), back_pixels = jax.vjp(
        partial(pixel_sums, mask_cols=mask_cols), logits
    )
    class_width = class_part.shape[2]
    class_logits = class_part.reshape(-1, class_width) + class_bias

    def loss_heads(class_in, intersection_in, squares_in):
        focal_loss = focal_part(
            class_in,
            cell_ids,
            live_slots,
            live_count,
            instance_labels[0],
            model_index * class_width,
        )
        dice_loss = dice_from(intersection_in, squares_in, mask_sum, live_slots, live_count)
        return (focal_loss, DICE_WEIGHT * dice_loss)

    (focal_loss, dice_loss), back_heads = jax.vjp(
        loss_heads, class_logits, intersection, squares_sum
    )
    image_share = jnp.float32(1.0 / image_total)
    grad_class, grad_intersection, grad_squares = back_heads((image_share, image_share))
    grad_logits = back_pixels((grad_intersection, grad_squares))[0]
    logit_low = grad_logits.astype(jnp.bfloat16)
    first_model = (model_index == 0).astype(jnp.float32)

    reciprocal = lax.rsqrt(norms_all + 1e-06)
    own_reciprocal = lax.dynamic_slice_in_dim(reciprocal, row_start, NI)
    scale = own_reciprocal[:, None] * reciprocal[None, :] / CONTRAST_TEMP
    similarity = unscaled_scores * scale
    other_row = (
        jnp.arange(image_total * NI)[None, :] != (row_start + jnp.arange(NI))[:, None]
    )
    allowed = (live_all[None, :] > 0.5) & other_row
    masked = jnp.where(allowed, similarity, -1000000000.0)
    top_score = jnp.max(masked, axis=1, keepdims=True)
    log_total = top_score[:, 0] + jnp.log(jnp.sum(jnp.exp(masked - top_score), axis=1))
    contrast = jnp.sum(live_slots * log_total) / live_count.astype(jnp.float32)
    rest_loss = dice_loss + contrast
    own_totals = jnp.zeros((8, 128), jnp.float32).at[0, :NI].set(log_total)
    log_all = share(dims, own_totals, 5).reshape(image_total, model_total, 8, 128)[
        :, 0, 0, :NI
    ].reshape(-1)
    weight_all = live_all * jnp.repeat(image_share / instance_counts.astype(jnp.float32), NI)
    own_weight = lax.dynamic_slice_in_dim(weight_all, row_start, NI)
    query_part = jnp.where(
        allowed, jnp.exp(similarity - log_total[:, None]) * own_weight[:, None], 0.0
    )
    keyed = (live_slots[:, None] > 0.5) & other_row & (live_all[None, :] > 0.5)
    key_part = jnp.where(
        keyed, jnp.exp(similarity - log_all[None, :]) * weight_all[None, :], 0.0
    )
    query_low = (query_part * scale).astype(jnp.bfloat16)
    key_low = (key_part * scale).astype(jnp.bfloat16)
    grad_reciprocal = jnp.sum(
        (query_part + key_part) * unscaled_scores * reciprocal[None, :] / CONTRAST_TEMP, axis=1
    )
    grad_norms_own = -0.5 * own_reciprocal * own_reciprocal * own_reciprocal * grad_reciprocal
    kernel_part = lax.dynamic_slice_in_dim(kernel_all, model_index * local_width, local_width, 1)
    grad_feature = jnp.dot(logit_low, kernel_rows, preferred_element_type=jnp.float32).reshape(
        feature_map.shape
    )
    logit_rows = jnp.dot(logit_low.T, feature_low, preferred_element_type=jnp.float32)
    grad_rows = (
        jnp.dot(
            jnp.concatenate([query_low, key_low], axis=1),
            jnp.concatenate([kernel_part, kernel_part], axis=0),
            preferred_element_type=jnp.float32,
        )
        + 2.0 * kernel_rows.astype(jnp.float32) * grad_norms_own[:, None]
        + logit_rows
    )
    grad_second_mask, grad_gain_three, grad_bias_three = back_mask_two(grad_feature)
    grad_kernels = jnp.zeros(kernel_flat.shape, jnp.float32).at[cell_ids].add(grad_rows)
    class_gradient_reduced = grad_class.astype(jnp.bfloat16)
    grad_class_bias = jnp.sum(class_gradient_reduced.astype(jnp.float32), axis=0)
    mask_grad_low = grad_second_mask.astype(jnp.bfloat16)
    kernel_grad_low = grad_kernels.astype(jnp.bfloat16).reshape(kernels.shape)
    class_grad_map = class_gradient_reduced.reshape(class_part.shape)
    grad_mask_second = conv_weight_grad(hidden_mask_full, mask_grad_low)
    grad_grid_second = conv_weight_grad(hidden_grid_full, kernel_grad_low)
    grad_class_conv = conv_weight_grad(hidden_grid_full, class_grad_map)
    grid_input_terms = conv_input_grad(kernel_grad_low, second_low) + conv_input_grad(
        class_grad_map, class_low
    )
    grad_hidden_mask, grad_hidden_grid = own_half_sums(
        [
            conv_input_grad(mask_grad_low, mask_low[1]).astype(jnp.bfloat16),
            grid_input_terms.astype(jnp.bfloat16),
        ],
        model_index,
        6,
    )
    grad_first_mask, grad_gain_one, grad_bias_one = back_mask_one(grad_hidden_mask)
    grad_first_grid, grad_gain_five, grad_bias_five = back_grid_one(grad_hidden_grid)
    grad_mask_first = conv_weight_grad(mask_full, grad_first_mask.astype(jnp.bfloat16))
    grad_grid_first = conv_weight_grad(grid_full, grad_first_grid.astype(jnp.bfloat16))
    reduced = reduce_all(
        dims,
        [
            owner_blocks(grad_mask_first, dims),
            owner_blocks(grad_grid_first, dims),
            owner_blocks(grad_mask_second, dims),
            owner_blocks(grad_grid_second, dims),
            owner_blocks(columns_in_lanes(grad_class_conv), dims),
        ],
    )
    mask_sum_w = jnp.stack(
        [reduced[0].reshape(mask_convs.shape[1:]), reduced[2].reshape(mask_convs.shape[1:])]
    )
    first_sum_w = reduced[1].reshape(grid_first.shape)
    second_sum_w = reduced[3].reshape(grid_second.shape)
    class_sum_w = columns_from_lanes(reduced[4].reshape(3, -1, 3 * class_share))
    small = jnp.concatenate(
        [
            jnp.stack([grad_gain_one, grad_bias_one, grad_gain_three, grad_bias_three]),
            grad_gain_five.reshape(-1, local_width),
            grad_bias_five.reshape(-1, local_width),
            jnp.pad(grad_class_bias, (0, local_width - class_share))[None, :],
        ]
    )
    small_all = share(dims, jnp.pad(small, ((0, 16 - small.shape[0]), (0, 0))), 7).reshape(
        image_total, model_total, 16, local_width
    )
    small_sum = jnp.sum(
        lax.dynamic_index_in_dim(small_all, model_index, 1, keepdims=False), axis=0
    )
    mask_norm_sum = small_sum[:4]
    grid_norm_sum = small_sum[4:8].reshape(2, -1)
    bias_sum = small_sum[8, :class_share]
    first_device = (data_index == 0).astype(jnp.float32)
    squares = (
        jnp.sum(jnp.square(mask_sum_w))
        + jnp.sum(jnp.square(first_sum_w))
        + jnp.sum(jnp.square(second_sum_w))
        + jnp.sum(jnp.square(class_sum_w))
        + first_device
        * (
            jnp.sum(jnp.square(mask_norm_sum))
            + jnp.sum(jnp.square(grid_norm_sum))
            + jnp.sum(jnp.square(bias_sum))
        )
    )
    loss_part = (focal_loss + first_model * rest_loss) * image_share
    pair = jnp.concatenate([jnp.full((1, 128), squares), jnp.full((1, 128), loss_part)])
    pair_sum = jnp.sum(
        share(dims, jnp.pad(pair, ((0, 6), (0, 0))), 8).reshape(-1, 8, 128), axis=0
    )
    total_squares, step_loss = pair_sum[0, 0], pair_sum[1, 0]
    gradient_norm = jnp.sqrt(total_squares)
    factor = jnp.minimum(1.0, CLIP_LIMIT / gradient_norm)
    mask_new = adam_update(
        mask_convs, mask_convs_moment, mask_convs_square, mask_sum_w * factor, LEARN_RATE
    )
    first_new = adam_update(
        grid_first, grid_first_moment, grid_first_square, first_sum_w * factor, LEARN_RATE
    )
    second_new = adam_update(
        grid_second, grid_second_moment, grid_second_square, second_sum_w * factor, LEARN_RATE
    )
    class_new = adam_update(
        class_conv, class_conv_moment, class_conv_square, class_sum_w * factor, LEARN_RATE
    )
    mask_norm_new = adam_update(
        mask_norms, mask_norms_moment, mask_norms_square, mask_norm_sum * factor, SMALL_RATE
    )
    grid_norm_new = adam_update(
        grid_norms, grid_norms_moment, grid_norms_square, grid_norm_sum * factor, SMALL_RATE
    )
    bias_new = adam_update(
        class_bias, class_bias_moment, class_bias_square, bias_sum * factor, SMALL_RATE
    )
    return (
        step_loss,
        gradient_norm,
        mask_new[0],
        mask_new[1],
        mask_new[2],
        first_new[0],
        first_new[1],
        first_new[2],
        second_new[0],
        second_new[1],
        second_new[2],
        class_new[0],
        class_new[1],
        class_new[2],
        mask_norm_new[0],
        mask_norm_new[1],
        mask_norm_new[2],
        grid_norm_new[0],
        grid_norm_new[1],
        grid_norm_new[2],
        bias_new[0],
        bias_new[1],
        bias_new[2],
    )


def solution(mesh):
    in_specs = (
        P("dp", None, None, "mp"),
        P("dp", None, None, "mp"),
        P("dp", None),
        P(),
        P("dp", None),
        P("dp", None, None),
        P(None, None, "dp", "mp"),
        P(None, None, "dp", "mp"),
        P(None, None, "dp", "mp"),
        P(None, "dp", "mp"),
        P(None, "dp", "mp"),
        P(None, "dp", "mp"),
        P(None, "dp", "mp"),
        P(None, "dp", "mp"),
        P(None, "dp", "mp"),
        P(None, "dp", "mp"),
        P(None, "dp", "mp"),
        P(None, "dp", "mp"),
        P(None, "mp"),
        P(None, "mp"),
        P(None, "mp"),
        P(None, "mp"),
        P(None, "mp"),
        P(None, "mp"),
        P("mp"),
        P("mp"),
        P("mp"),
    )
    out_specs = (
        P(),
        P(),
        P(None, None, "dp", "mp"),
        P(None, None, "dp", "mp"),
        P(None, None, "dp", "mp"),
        P(None, "dp", "mp"),
        P(None, "dp", "mp"),
        P(None, "dp", "mp"),
        P(None, "dp", "mp"),
        P(None, "dp", "mp"),
        P(None, "dp", "mp"),
        P(None, "dp", "mp"),
        P(None, "dp", "mp"),
        P(None, "dp", "mp"),
        P(None, "mp"),
        P(None, "mp"),
        P(None, "mp"),
        P(None, "mp"),
        P(None, "mp"),
        P(None, "mp"),
        P("mp"),
        P("mp"),
        P("mp"),
    )
    return jax.shard_map(body, mesh=mesh, in_specs=in_specs, out_specs=out_specs, check_vma=False)
```

```python
from functools import partial

import jax
import jax.numpy as jnp
from jax import lax
from jax.experimental import pallas as pl
from jax.experimental.pallas import tpu as pltpu
from jax.sharding import PartitionSpec as P

GROUPS = 32
GN_EPS = 1e-05
CLIP_LIMIT = 0.02
LEARN_RATE = 0.02
SMALL_RATE = 0.5
BETA_ONE = 0.9
BETA_TWO = 0.95
ADAM_EPS = 1e-08
WEIGHT_DECAY = 0.05
CONTRAST_TEMP = 0.05
FOCAL_ALPHA = 0.25
DICE_WEIGHT = 3.0
STEP_TIME = 10.0
HIGHEST = lax.Precision.HIGHEST

MESH = pl.DeviceIdType.MESH
VMEM = pltpu.VMEM
ANY = pl.ANY
VMEM_LIMIT = 67043328
F32 = jnp.float32
BF16 = jnp.bfloat16
I32 = jnp.int32
SLOTS = 128
DMA = pltpu.SemaphoreType.DMA


def line_lengths(total):
    if total & (total - 1):
        return (total, 1, 1)
    bits = total.bit_length() - 1
    last = bits // 3
    middle = (bits - last) // 2
    return (1 << (bits - last - middle), 1 << middle, 1 << last)


def place(dims):
    index = lax.axis_index("dp")
    return (index // (dims[1] * dims[2]), (index // dims[2]) % dims[1], index % dims[2])


def split_index(dims, index):
    return (
        index // (dims[1] * dims[2]),
        lax.rem(index // dims[2], dims[1]),
        lax.rem(index, dims[2]),
    )


def along(dims, axis, step):
    stride = (dims[1] * dims[2], dims[2], 1)[axis]
    return {"dp": lax.axis_index("dp") + step * stride}


def partner():
    return {"mp": 1 - lax.axis_index("mp")}


def ring_step(dims, pos, axis, offset):
    other = lax.rem(pos[axis] + offset, dims[axis])
    return along(dims, axis, other - pos[axis])


def greet(dims):
    sem = pltpu.get_barrier_semaphore()
    pos = place(dims)
    count = 1
    for axis in range(3):
        for offset in range(1, dims[axis]):
            pl.semaphore_signal(
                sem, inc=1, device_id=ring_step(dims, pos, axis, offset), device_id_type=MESH
            )
            count += 1
    pl.semaphore_signal(sem, inc=1, device_id=partner(), device_id_type=MESH)
    pl.semaphore_wait(sem, count)


GATHER_ORDERS = ((2, 1, 0), (0, 2, 1), (0, 1, 2))
REDUCE_ORDERS = tuple(tuple(reversed(order)) for order in GATHER_ORDERS)


def rounds_of(dims, order):
    return [
        (stage, axis, step) for stage, axis in enumerate(order) for step in range(dims[axis] - 1)
    ]


def round_count(dims):
    return sum(n - 1 for n in dims)


def lane_cuts(width):
    tiles = width // 128
    if width % 128 or tiles < 3:
        return ((0, 0, width),)
    first = max(1, round(tiles * 0.2))
    second = (tiles - first) // 2
    sizes = (first, second, tiles - first - second)
    cuts, start = [], 0
    for order, size in enumerate(sizes):
        cuts.append((order, start * 128, size * 128))
        start += size
    return tuple(cuts)


class Flow:
    def __init__(self, rounds):
        self.rounds = rounds

    def start(self, r):
        for copy, sends, *_ in self.rounds[r]:

            @pl.when(sends)
            def _(copy=copy):
                copy.start()

    def finish(self, r):
        for copy, _, receives, land in self.rounds[r]:

            @pl.when(receives)
            def _(copy=copy, land=land):
                copy.wait_recv()
                if land is not None:
                    land()

    def drain(self):
        for copies in self.rounds:
            for copy, sends, *_ in copies:

                @pl.when(sends)
                def _(copy=copy):
                    copy.wait_send()


def gather_flow(dims, out, send_sems, recv_sems, base, lanes, order):
    pos = place(dims)
    result = []
    for r, (stage, axis, step) in enumerate(rounds_of(dims, order)):
        n, done = dims[axis], set(order[:stage])
        copies = []
        for side, delta in ((0, 1), (1, -1)):
            block = pos[axis] - delta * step
            sends = (
                (pos[axis] + delta >= 0)
                & (pos[axis] + delta < n)
                & (block >= 0)
                & (block < n)
            )
            block = jnp.clip(block, 0, n - 1)
            source = pos[axis] - delta * (1 + step)
            receives = (source >= 0) & (source < n)
            view = out.at[
                tuple(
                    pl.ds(0, dims[k]) if k in done else (block if k == axis else pos[k])
                    for k in range(3)
                )
                + (slice(None), lanes)
            ]
            copy = pltpu.make_async_remote_copy(
                src_ref=view,
                dst_ref=view,
                send_sem=send_sems.at[base + 2 * r + side],
                recv_sem=recv_sems.at[base + 2 * r + side],
                device_id=along(dims, axis, delta),
                device_id_type=MESH,
            )
            copies.append((copy, sends, receives, None))
        result.append(copies)
    return Flow(result)


def landing_shapes(dims, rows, width, order):
    shapes, left = [], {0, 1, 2}
    for axis in order:
        left = left - {axis}
        n = dims[axis]
        slots = max(1, n - 1) * (1 if n <= 2 else 2)
        shapes.append((slots,) + tuple(dims[k] for k in sorted(left)) + (rows, width))
    return shapes


def reduce_flow(dims, total, staged, lands, send_sems, recv_sems, base, lanes, order):
    pos = place(dims)
    result = []
    for r, (stage, axis, step) in enumerate(rounds_of(dims, order)):
        n, reduced = dims[axis], set(order[:stage])
        free = [k for k in range(3) if k not in reduced and k != axis]

        def view(block, lead=None, axis=axis, reduced=reduced):
            lead = iter(lead) if lead is not None else None
            index = []
            for k in range(3):
                if k == axis:
                    index.append(block)
                elif k in reduced:
                    index.append(pos[k])
                else:
                    index.append(pl.ds(0, dims[k]) if lead is None else next(lead))
            return tuple(index) + (slice(None), lanes)

        copies = []
        for side, delta in ((0, 1), (1, -1)):
            rank = pos[axis] if delta == 1 else n - 1 - pos[axis]
            sends = rank <= step
            if n == 1:
                sends = sends & False
            block = n - 1 - step + rank
            block = jnp.clip(block if delta == 1 else n - 1 - block, 0, n - 1)
            receives = (rank >= 1) & (rank - 1 <= step)
            taken = n - 1 - step + rank - 1
            taken = jnp.clip(taken if delta == 1 else n - 1 - taken, 0, n - 1)
            land_ref = lands[stage].at[step if n <= 2 else side * (n - 1) + step]
            copy = pltpu.make_async_remote_copy(
                src_ref=staged.at[view(block)],
                dst_ref=land_ref,
                send_sem=send_sems.at[base + 2 * r + side],
                recv_sem=recv_sems.at[base + 2 * r + side],
                device_id=along(dims, axis, delta),
                device_id_type=MESH,
            )

            def land(taken=taken, land_ref=land_ref, free=free, view=view):
                sizes = [dims[k] for k in free]
                blocks = 1
                for size in sizes:
                    blocks *= size

                def add(i, carry):
                    lead, rest = [], i
                    for size in reversed(sizes):
                        lead.append(lax.rem(rest, size))
                        rest = rest // size
                    lead = lead[::-1]
                    index = view(taken, lead)
                    value = total[index] + land_ref[tuple(lead)].astype(F32)
                    total[index] = value
                    staged[index] = value.astype(BF16)
                    return carry

                if blocks == 1:
                    add(jnp.int32(0), 0)
                else:
                    lax.fori_loop(0, blocks, add, 0)

            copies.append((copy, sends, receives, land))
        result.append(copies)
    return Flow(result)


class Share:
    def __init__(self, dims, out, send_sems, recv_sems, core):
        pos = place(dims)
        model = lax.axis_index("mp")
        tail = (model,) if core else ()
        self.stages, done, slot = [], set(), 0
        for axis in (2, 1, 0):
            view = out.at[
                tuple(pl.ds(0, dims[k]) if k in done else pos[k] for k in range(3)) + tail
            ]
            copies = []
            for offset in range(1, dims[axis]):
                copies.append(
                    pltpu.make_async_remote_copy(
                        src_ref=view,
                        dst_ref=view,
                        send_sem=send_sems.at[slot],
                        recv_sem=recv_sems.at[slot],
                        device_id=ring_step(dims, pos, axis, offset),
                        device_id_type=MESH,
                    )
                )
                slot += 1
            if copies:
                self.stages.append(copies)
            done.add(axis)
        if core:
            view = out.at[:, :, :, model]
            self.stages.append(
                [
                    pltpu.make_async_remote_copy(
                        src_ref=view,
                        dst_ref=view,
                        send_sem=send_sems.at[slot],
                        recv_sem=recv_sems.at[slot],
                        device_id=partner(),
                        device_id_type=MESH,
                    )
                ]
            )
        self.next = 0

    def advance(self):
        if self.next > len(self.stages):
            return
        if self.next > 0:
            for copy in self.stages[self.next - 1]:
                copy.wait_recv()
        if self.next < len(self.stages):
            for copy in self.stages[self.next]:
                copy.start()
        self.next += 1

    def complete(self):
        while self.next <= len(self.stages):
            self.advance()

    def drain(self):
        for stage in self.stages:
            for copy in stage:
                copy.wait_send()


def share_sems(dims):
    return [DMA((round_count(dims) + 1,)), DMA((round_count(dims) + 1,))]


def pair_copy(source, target, sems):
    return pltpu.make_async_remote_copy(
        src_ref=source,
        dst_ref=target,
        send_sem=sems.at[0],
        recv_sem=sems.at[1],
        device_id=partner(),
        device_id_type=MESH,
    )


def params(collective_id):
    return pltpu.CompilerParams(
        collective_id=collective_id, has_side_effects=True, vmem_limit_bytes=VMEM_LIMIT
    )


def gather_flows(dims, outs, send_sems, recv_sems):
    groups, base = [], 0
    for out in outs:
        group = []
        for order, start, size in lane_cuts(out.shape[4]):
            group.append(
                gather_flow(
                    dims, out, send_sems, recv_sems, base, pl.ds(start, size), GATHER_ORDERS[order]
                )
            )
            base += 2 * round_count(dims)
        groups.append(group)
    return groups


def reduce_flows(dims, totals, staged, lands, send_sems, recv_sems):
    groups, base, lands = [], 0, list(lands)
    for total, stage in zip(totals, staged):
        group = []
        for order, start, size in lane_cuts(total.shape[4]):
            group.append(
                reduce_flow(
                    dims,
                    total,
                    stage,
                    lands[:3],
                    send_sems,
                    recv_sems,
                    base,
                    pl.ds(start, size),
                    REDUCE_ORDERS[order],
                )
            )
            lands = lands[3:]
            base += 2 * round_count(dims)
        groups.append(group)
    return groups


def flow_slots(dims, shapes):
    return max(1, 2 * round_count(dims) * sum(len(lane_cuts(s[-1])) for s in shapes))


def landing_scratch(dims, shapes):
    scratch = []
    for shape in shapes:
        for order, _, size in lane_cuts(shape[-1]):
            for land in landing_shapes(dims, shape[-2], size, REDUCE_ORDERS[order]):
                scratch.append(VMEM(land, BF16))
    return scratch


def cast_blocks(dims, total, staged):
    def cast(j, carry):
        index = split_index(dims, j)
        staged[index] = total[index].astype(BF16)
        return carry

    lax.fori_loop(0, dims[0] * dims[1] * dims[2], cast, 0)


def run_rounds(dims, groups):
    flows = [flow for group in groups for flow in group]
    for r in range(round_count(dims) + 1):
        for flow in flows:
            if r > 0:
                flow.finish(r - 1)
            if r < round_count(dims):
                flow.start(r)
    for flow in flows:
        flow.drain()


def gather_kernel(dims, count, *refs):
    shards, outs = refs[:count], refs[count : 2 * count]
    send_sems, recv_sems, local_sems = refs[2 * count :]
    pos = place(dims)
    local = [
        pltpu.make_async_copy(shards[i], outs[i].at[pos[0], pos[1], pos[2]], local_sems.at[i])
        for i in range(count)
    ]
    for copy in local:
        copy.start()
    greet(dims)
    for copy in local:
        copy.wait()
    run_rounds(dims, gather_flows(dims, outs, send_sems, recv_sems))


def gather_all(dims, shards):
    count = len(shards)
    shapes = [dims + s.shape for s in shards]
    slots = flow_slots(dims, shapes)
    return pl.pallas_call(
        partial(gather_kernel, dims, count),
        name="gather_weights",
        out_shape=[jax.ShapeDtypeStruct(s, BF16) for s in shapes],
        in_specs=[pl.BlockSpec(memory_space=VMEM)] * count,
        out_specs=[pl.BlockSpec(memory_space=VMEM)] * count,
        scratch_shapes=[DMA((slots,)), DMA((slots,)), DMA((count,))],
        compiler_params=params(1),
    )(*shards)


def reduce_kernel(dims, count, *refs):
    parts, outs = refs[:count], refs[count : 2 * count]
    send_sems, recv_sems, local_sems = refs[2 * count : 2 * count + 3]
    rest = list(refs[2 * count + 3 :])
    totals, staged, lands = rest[:count], rest[count : 2 * count], rest[2 * count :]
    pos = place(dims)
    local = [pltpu.make_async_copy(parts[i], totals[i], local_sems.at[i]) for i in range(count)]
    for copy in local:
        copy.start()
    greet(dims)
    for i in range(count):
        local[i].wait()
        cast_blocks(dims, totals[i], staged[i])
    run_rounds(dims, reduce_flows(dims, totals, staged, lands, send_sems, recv_sems))
    for i in range(count):
        outs[i][...] = totals[i][pos[0], pos[1], pos[2]]


def reduce_all(dims, parts):
    count = len(parts)
    shapes = [p.shape for p in parts]
    slots = flow_slots(dims, shapes)
    scratch = [DMA((slots,)), DMA((slots,)), DMA((count,))]
    scratch += [VMEM(s, F32) for s in shapes] + [VMEM(s, BF16) for s in shapes]
    scratch += landing_scratch(dims, shapes)
    return pl.pallas_call(
        partial(reduce_kernel, dims, count),
        name="reduce_gradients",
        out_shape=[jax.ShapeDtypeStruct(s[3:], F32) for s in shapes],
        in_specs=[pl.BlockSpec(memory_space=ANY)] * count,
        out_specs=[pl.BlockSpec(memory_space=VMEM)] * count,
        scratch_shapes=scratch,
        compiler_params=params(2),
    )(*parts)


def group_sums(row, spread):
    width = row.shape[1]
    return lax.dot_general(
        jnp.broadcast_to(row, (8, width)),
        spread,
        (((1,), (0,)), ((), ())),
        precision=HIGHEST,
        preferred_element_type=F32,
    )[0:1]


def group_spread(width, group):
    rows = lax.broadcasted_iota(I32, (width, width), 0) // group
    cols = lax.broadcasted_iota(I32, (width, width), 1) // group
    return (rows == cols).astype(F32)


def column_of(tile, width, lanes):
    return lax.broadcasted_iota(I32, (tile // width, width, lanes), 1).reshape(tile, lanes)


def dot(a, b, contract):
    return lax.dot_general(a, b, ((contract[0], contract[1]), ((), ())), preferred_element_type=F32)


NN = ((1,), (0,))
NT = ((1,), (1,))
TN = ((0,), (0,))


def conv_forward(source, weight, raw, rows, width, tile, n, live):
    def body(i, total):
        start = pl.multiple_of(i * tile, tile)
        wide = None
        for du in range(3):
            rows_in = pl.ds(pl.multiple_of(start + du * width, 16), tile)
            part = dot(source[rows_in, :], weight(du), NN)
            wide = part if wide is None else wide + part
        left = pltpu.roll(wide[:, :n], 1, 0)
        right = pltpu.roll(wide[:, 2 * n :], tile - 1, 0)
        column = column_of(tile, width, n)
        if live == width:
            left = jnp.where(column == 0, 0.0, left)
            right = jnp.where(column == width - 1, 0.0, right)
        value = left + wide[:, n : 2 * n] + right
        if live < width:
            value = jnp.where(column < live, value, 0.0)
        raw[pl.ds(start, tile), :] = value
        return total + jnp.sum(value, axis=0, keepdims=True)

    return lax.fori_loop(0, rows // tile, body, jnp.zeros((1, n), F32))


def norm_forward(raw, total, rows, width, tile, n, live, count, spread, gain, bias, store):
    mean = group_sums(total, spread) / count

    def spread_of(i, acc):
        start = pl.multiple_of(i * tile, tile)
        away = raw[pl.ds(start, tile), :] - mean
        if live < width:
            away = jnp.where(column_of(tile, width, n) < live, away, 0.0)
        return acc + jnp.sum(away * away, axis=0, keepdims=True)

    squares = lax.fori_loop(0, rows // tile, spread_of, jnp.zeros((1, n), F32))
    scale = lax.rsqrt(group_sums(squares, spread) / count + GN_EPS)

    def normalize(i, carry):
        start = pl.multiple_of(i * tile, tile)
        normed = (raw[pl.ds(start, tile), :] - mean) * scale
        raw[pl.ds(start, tile), :] = normed
        value = jnp.maximum(normed * gain + bias, 0.0)
        if live < width:
            value = jnp.where(column_of(tile, width, n) < live, value, 0.0)
        store(start, value.astype(BF16))
        return carry

    lax.fori_loop(0, rows // tile, normalize, 0)
    return scale


def norm_backward(
    normed, upstream, spare, shifted, rows, width, tile, n, live, count, spread, gain, bias, scale
):
    def first(i, sums):
        start = pl.multiple_of(i * tile, tile)
        here = normed[pl.ds(start, tile), :]
        value = jnp.where(here * gain + bias > 0.0, upstream(start), 0.0)
        if live < width:
            value = jnp.where(column_of(tile, width, n) < live, value, 0.0)
        spare[pl.ds(start, tile), :] = value
        return (
            sums[0] + jnp.sum(value * here, axis=0, keepdims=True),
            sums[1] + jnp.sum(value, axis=0, keepdims=True),
        )

    zero = jnp.zeros((1, n), F32)
    gain_sum, bias_sum = lax.fori_loop(0, rows // tile, first, (zero, zero))
    level = group_sums(bias_sum * gain, spread) / count
    slope = group_sums(gain_sum * gain, spread) / count

    def second(i, carry):
        start = pl.multiple_of(i * tile, tile)
        value = scale * (
            spare[pl.ds(start, tile), :] * gain - level - normed[pl.ds(start, tile), :] * slope
        )
        column = column_of(tile, width, n)
        if live < width:
            value = jnp.where(column < live, value, 0.0)
        left = pltpu.roll(value, tile - 1, 0)
        right = pltpu.roll(value, 1, 0)
        if live == width:
            left = jnp.where(column == width - 1, 0.0, left)
            right = jnp.where(column == 0, 0.0, right)
        into = pl.ds(pl.multiple_of(start + width, 16), tile)
        shifted[into, 0:n] = left.astype(BF16)
        shifted[into, n : 2 * n] = value.astype(BF16)
        shifted[into, 2 * n : 3 * n] = right.astype(BF16)
        return carry

    lax.fori_loop(0, rows // tile, second, 0)
    return gain_sum, bias_sum


def weight_gradient(source, shifted, total, rows, width, tile, lanes):
    span = lanes.stop - lanes.start

    def body(i, carry):
        start = pl.multiple_of(i * tile, tile)
        right = shifted[pl.ds(pl.multiple_of(start + width, 16), tile), lanes]
        for du in range(3):
            left = source[pl.ds(pl.multiple_of(start + du * width, 16), tile), :]
            value = dot(left, right, TN)
            into = total.at[..., du * span : (du + 1) * span]
            value = value.reshape(into.shape)

            @pl.when(i == 0)
            def _(into=into, value=value):
                into[...] = value

            @pl.when(i > 0)
            def _(into=into, value=value):
                into[...] += value

        return carry

    lax.fori_loop(0, rows // tile, body, 0)


def zero_rows(ref, rows):
    ref[0:rows, :] = jnp.zeros((rows, ref.shape[1]), ref.dtype)
    last = ref.shape[0]
    ref[last - rows : last, :] = jnp.zeros((rows, ref.shape[1]), ref.dtype)


def as_row(column):
    n = column.shape[0]
    rows = lax.broadcasted_iota(I32, (n, n), 0)
    cols = lax.broadcasted_iota(I32, (n, n), 1)
    return jnp.sum(jnp.where(rows == cols, column, 0.0), axis=0, keepdims=True)


def step_kernel(cfg, names, *refs):
    r = dict(zip(names, refs))
    dims, images = cfg["dims"], cfg["images"]
    wide, rows = cfg["wide"], cfg["rows"]
    pad, grid_rows, grid = cfg["pad"], cfg["grid_rows"], cfg["grid"]
    nm, ng, kc = cfg["nm"], cfg["ng"], cfg["kc"]
    fused = cfg["fused"]
    tile, small_tile = cfg["tile"], cfg["small_tile"]
    gtile = cfg["gtile"]
    pos = place(dims)
    model = lax.axis_index("mp")
    own_m = pl.ds(pl.multiple_of(model * nm, nm), nm)
    away_m = pl.ds(pl.multiple_of((1 - model) * nm, nm), nm)
    own_g = pl.ds(pl.multiple_of(model * ng, ng), ng)
    away_g = pl.ds(pl.multiple_of((1 - model) * ng, ng), ng)
    gin = r["xg_own"].shape[1]
    own_x = pl.ds(pl.multiple_of(model * gin, gin), gin)
    map_rows = pl.ds(wide, rows)
    grid_span = pl.ds(pad, grid_rows)
    mask_count = float(rows * (2 * nm // GROUPS))
    grid_count = float(grid * grid * (2 * ng // GROUPS))
    spread_m = group_spread(nm, 2 * nm // GROUPS)
    spread_g = group_spread(ng, 2 * ng // GROUPS)

    xm, xg = r["xm"], r["xg"]
    local = [
        pltpu.make_async_copy(r["xm_own"], xm.at[map_rows, own_x], r["local"].at[0]),
        pltpu.make_async_copy(r["xg_own"], xg.at[grid_span, own_x], r["local"].at[1]),
    ]
    if fused:
        for i in range(5):
            local.append(
                pltpu.make_async_copy(
                    r["w%d_own" % i],
                    r["w%d" % i].at[pos[0], pos[1], pos[2]],
                    r["local"].at[2 + i],
                )
            )
    for copy in local:
        copy.start()
    for name, count in (("xm", wide), ("hm", wide), ("dm", wide)):
        zero_rows(r[name], count)
    for name in ("xg", "hg", "dg2", "dg1"):
        zero_rows(r[name], pad)
    greet(dims)
    feature_copies = [
        pair_copy(r["xm_own"], xm.at[map_rows, own_x], r["pair"].at[0]),
        pair_copy(r["xg_own"], xg.at[grid_span, own_x], r["pair"].at[1]),
    ]
    for copy in feature_copies:
        copy.start()
    for copy in local:
        copy.wait()
    if fused:
        weights = [r["w%d" % i] for i in range(5)]
        run_rounds(dims, gather_flows(dims, weights, r["gs"], r["gr"]))

    def weight(i, span):
        def part(du):
            value = r["w%d" % i][..., du * span : (du + 1) * span]
            return value.reshape(-1, span) if fused else value

        return part

    mask_one, grid_one, mask_two = weight(0, 3 * nm), weight(1, 3 * ng), weight(2, 3 * nm)
    grid_two, class_two = weight(3, 3 * nm), weight(4, 128)

    norms, gnorms = r["mask_norms"], r["grid_norms"]
    row = lambda ref, k: ref[k : k + 1, :]
    feature_copies[0].wait()
    xh1, hm = r["xh1"], r["hm"]
    total = conv_forward(xm, mask_one, xh1, rows, wide, tile, nm, wide)

    def keep_mask(start, value):
        hm[pl.ds(pl.multiple_of(start + wide, 16), value.shape[0]), own_m] = value

    scale_one = norm_forward(
        xh1, total, rows, wide, small_tile, nm, wide, mask_count, spread_m,
        row(norms, 0), row(norms, 1), keep_mask,
    )
    hm_copy = pair_copy(hm.at[map_rows, own_m], hm.at[map_rows, own_m], r["pair"].at[2])
    hm_copy.start()
    feature_copies[1].wait()
    xhg, hg = r["xhg"], r["hg"]
    total = conv_forward(xg, grid_one, xhg, grid_rows, pad, gtile, ng, grid)

    def keep_grid(start, value):
        hg[pl.ds(pl.multiple_of(start + pad, 16), value.shape[0]), own_g] = value

    scale_grid = norm_forward(
        xhg, total, grid_rows, pad, gtile, ng, grid, grid_count, spread_g,
        row(gnorms, 0), row(gnorms, 1), keep_grid,
    )
    hg_copy = pair_copy(hg.at[grid_span, own_g], hg.at[grid_span, own_g], r["pair"].at[3])
    hg_copy.start()

    hm_copy.wait()
    xh2, feature = r["xh2"], r["feature"]
    total = conv_forward(hm, mask_two, xh2, rows, wide, tile, nm, wide)

    def keep_feature(start, value):
        feature[pl.ds(start, value.shape[0]), :] = value

    scale_two = norm_forward(
        xh2, total, rows, wide, small_tile, nm, wide, mask_count, spread_m,
        row(norms, 2), row(norms, 3), keep_feature,
    )

    hg_copy.wait()
    cells_col, cells_row = r["cells_col"][...], r["cells_row"][...]
    patches = r["patches"]
    lane = lax.broadcasted_iota(I32, (SLOTS, grid_rows), 1)
    depth = hg.shape[1]
    picked = None
    for t in range(9):
        chosen = (lane == cells_col + ((t // 3 - 1) * pad + t % 3 - 1)).astype(F32).astype(BF16)
        part = dot(chosen, hg[grid_span, :], NN).astype(BF16)
        patches[:, t * depth : (t + 1) * depth] = part
        w = grid_two(t // 3)[:, (t % 3) * nm : (t % 3 + 1) * nm]
        part = dot(part, w, NN)
        picked = part if picked is None else picked + part
    kernels = r["kernels"]
    kernels[pos[0], pos[1], pos[2], model] = picked.astype(BF16)
    kernel_share = Share(dims, kernels, r["ks"], r["kr"], True)
    kernel_share.advance()

    kernel_rows = kernels[pos[0], pos[1], pos[2], model]
    logits, logits_in = r["logits"], r["logits_in"]
    high_slots = logits.shape[0]
    for i in range(rows // tile):
        span = slice(i * tile, (i + 1) * tile)
        logits[:, span] = dot(kernel_rows[:high_slots], feature[span, :], NT).astype(BF16)
    logits_copy = pair_copy(logits, logits_in, r["pair"].at[4])
    logits_copy.start()
    kernel_share.advance()

    cdx = r["dg2"]
    focal_rows = r["focal_rows"][...]
    class_hot = (
        (lax.broadcasted_iota(I32, (SLOTS, 128), 1) == r["labels_col"][...])
        .astype(F32)
        .astype(BF16)
    )
    live_row = focal_rows[1:2]
    focal_scale = focal_rows[2:3]
    class_bias = focal_rows[0:1]

    def class_tile(i, sums):
        start = pl.multiple_of(i * gtile, gtile)
        value = None
        for du in range(3):
            part = dot(
                hg[pl.ds(pl.multiple_of(start + du * pad, 16), gtile), :], class_two(du), NN
            )
            value = part if value is None else value + part
        x = (
            pltpu.roll(value, 1, 0)
            + pltpu.roll(value, 128 - kc, 1)
            + pltpu.roll(pltpu.roll(value, 128 - 2 * kc, 1), gtile - 1, 0)
            + class_bias
        )
        at = lax.broadcasted_iota(I32, (gtile, SLOTS), 0) + start
        cell_hot = jnp.where(at == cells_row, live_row, 0.0).astype(BF16)
        t = dot(cell_hot, class_hot, NN)
        lanes = lax.broadcasted_iota(I32, (gtile, 128), 1)
        real = (column_of(gtile, pad, 128) < grid) & (lanes < kc)
        small = jnp.exp(-jnp.abs(x))
        extra = jnp.log1p(small)
        inverse = 1.0 / (1.0 + small)
        q = jnp.where(x >= 0.0, 1.0, small) * inverse
        p = jnp.where(x >= 0.0, small, 1.0) * inverse
        log_q = -(jnp.maximum(-x, 0.0) + extra)
        log_p = -(jnp.maximum(x, 0.0) + extra)
        terms = FOCAL_ALPHA * t * p * p * log_q + (1.0 - FOCAL_ALPHA) * (1.0 - t) * q * q * log_p
        slope = FOCAL_ALPHA * t * p * p * (p - 2.0 * q * log_q) + (1.0 - FOCAL_ALPHA) * (
            1.0 - t
        ) * q * q * (2.0 * p * log_p - q)
        slope = jnp.where(real, -focal_scale * slope, 0.0).astype(BF16).astype(F32)
        shifted = (
            pltpu.roll(slope, gtile - 1, 0)
            + pltpu.roll(slope, kc, 1)
            + pltpu.roll(pltpu.roll(slope, 2 * kc, 1), 1, 0)
        )
        cdx[pl.ds(pl.multiple_of(start + pad, 16), gtile), 3 * nm :] = shifted.astype(BF16)
        return (
            sums[0] + jnp.sum(jnp.where(real, -focal_scale * terms, 0.0), axis=0, keepdims=True),
            sums[1] + jnp.sum(slope, axis=0, keepdims=True),
        )

    zero = jnp.zeros((1, 128), F32)
    focal_sum, class_bias_sum = lax.fori_loop(
        0, grid_rows // gtile, class_tile, (zero, zero)
    )
    kernel_share.advance()

    logits_copy.wait()
    cols = r["cols"][...]
    dice_col = cols[:, 0:1]
    masks = r["masks"]
    slots = masks.shape[0]
    dice_sum = jnp.zeros((1, 1), F32)
    for start in range(0, slots, 16):
        span = slice(start, start + 16)
        x = logits[span, :].astype(F32) + logits_in[span, :].astype(F32)
        s = jax.nn.sigmoid(x)
        m = masks[start : min(start + 16, slots), :].astype(F32)
        if m.shape[0] < 16:
            m = jnp.concatenate([m, jnp.zeros((16 - m.shape[0], rows), F32)], axis=0)
        inter = jnp.sum(s * m, axis=1, keepdims=True)
        whole = jnp.sum(s * s, axis=1, keepdims=True) + jnp.sum(m, axis=1, keepdims=True) + 1.0
        share_here = dice_col[span]
        dice_sum += jnp.sum(share_here * (1.0 - 2.0 * inter / whole), keepdims=True)
        a = -2.0 * share_here / whole
        b = 2.0 * share_here * inter / (whole * whole)
        logits[span, :] = ((a * m + 2.0 * b * s) * s * (1.0 - s)).astype(BF16)
    kernel_share.complete()

    own_full = [kernels[pos[0], pos[1], pos[2], k] for k in range(2)]

    def key_block(d):
        index = split_index(dims, d)
        return [kernels[index[0], index[1], index[2], k] for k in range(2)]

    def squares_of(block):
        return sum(
            jnp.sum(jnp.square(part.astype(F32)), axis=1, keepdims=True) for part in block
        )

    own_scale = lax.rsqrt(squares_of(own_full) + 1e-06)
    own_image = lax.axis_index("dp")
    diagonal = lax.broadcasted_iota(I32, (SLOTS, SLOTS), 0) == lax.broadcasted_iota(
        I32, (SLOTS, SLOTS), 1
    )

    def scores(d):
        block = key_block(d)
        raw = dot(own_full[0], block[0], NT) + dot(own_full[1], block[1], NT)
        key_scale = lax.rsqrt(as_row(squares_of(block)) + 1e-06)
        scale = own_scale * key_scale / CONTRAST_TEMP
        keys = r["keys"][d]
        allowed = (keys[0:1] > 0.5) & jnp.logical_not(diagonal & (d == own_image))
        return block, raw, key_scale, scale, keys, allowed

    def sum_keys(d, acc):
        _, raw, _, scale, _, allowed = scores(d)
        value = jnp.where(allowed, jnp.exp(raw * scale), 0.0)
        return acc + jnp.sum(value, axis=1, keepdims=True)

    totals_col = lax.fori_loop(0, images, sum_keys, jnp.zeros((SLOTS, 1), F32))
    log_col = jnp.log(totals_col)
    weight_col = cols[:, 1:2]
    live_col = cols[:, 2:3]
    contrast_sum = jnp.sum(
        jnp.where(weight_col > 0.0, weight_col * log_col, 0.0), keepdims=True
    )
    logs = r["logs"]
    logs[pos[0], pos[1], pos[2]] = jnp.broadcast_to(as_row(log_col), (8, SLOTS))
    log_share = Share(dims, logs, r["ls"], r["lr"], False)
    log_share.advance()

    logit_rows = dot(logits[...], feature[...], NN)
    log_share.advance()
    dlogits = logits

    def from_logits(start):
        return dot(dlogits[:, pl.ds(start, small_tile)], kernel_rows[:high_slots], TN)

    dm = r["dm"]
    gain_two, bias_two = norm_backward(
        xh2, from_logits, r["spare"], dm, rows, wide, small_tile, nm, wide, mask_count, spread_m,
        row(norms, 2), row(norms, 3), scale_two,
    )
    log_share.advance()
    weight_gradient(hm, dm, r["g2"], rows, wide, tile, slice(0, 3 * nm))
    hidden = hm

    def input_tile(i, carry):
        start = pl.multiple_of(i * tile, tile)
        value = None
        for du in range(3):
            part = dot(
                dm[pl.ds(pl.multiple_of(start + (2 - du) * wide, 16), tile), :], mask_two(du), NT
            )
            value = part if value is None else value + part
        hidden[pl.ds(pl.multiple_of(start + wide, 16), tile), :] = value.astype(BF16)
        return carry

    lax.fori_loop(0, rows // tile, input_tile, 0)
    hidden_copy = pair_copy(hidden.at[map_rows, away_m], r["dhm_in"], r["pair"].at[5])
    hidden_copy.start()
    log_share.complete()

    def row_terms(d, acc):
        block, raw, key_scale, scale, keys, allowed = scores(d)
        index = split_index(dims, d)
        log_row = logs[index[0], index[1], index[2]][0:1]
        value = raw * scale
        query = jnp.where(allowed, jnp.exp(value - log_col) * weight_col, 0.0)
        keyed = allowed & (live_col > 0.5)
        key = jnp.where(keyed, jnp.exp(value - log_row) * keys[1:2], 0.0)
        query_low = (query * scale).astype(BF16)
        key_low = (key * scale).astype(BF16)
        mine = jnp.where(model == 0, block[0].astype(F32), block[1].astype(F32)).astype(BF16)
        return (
            acc[0] + dot(query_low, mine, NN) + dot(key_low, mine, NN),
            acc[1]
            + jnp.sum((query + key) * raw * key_scale / CONTRAST_TEMP, axis=1, keepdims=True),
        )

    row_sum, scale_sum = lax.fori_loop(
        0, images, row_terms, (jnp.zeros((SLOTS, nm), F32), jnp.zeros((SLOTS, 1), F32))
    )
    norm_grad = -0.5 * own_scale * own_scale * own_scale * scale_sum
    row_grad = row_sum + 2.0 * kernel_rows.astype(F32) * norm_grad
    row_grad = row_grad + jnp.concatenate(
        [logit_rows, jnp.zeros((SLOTS - high_slots, nm), F32)], axis=0
    )
    row_low = row_grad.astype(BF16)

    dg2 = r["dg2"]
    for i in range(grid_rows // gtile):
        at = lax.broadcasted_iota(I32, (gtile, SLOTS), 0) + i * gtile
        for dv in range(3):
            chosen = (at == cells_row + (dv - 1)).astype(F32).astype(BF16)
            dg2[pad + i * gtile : pad + (i + 1) * gtile, dv * nm : (dv + 1) * nm] = dot(
                chosen, row_low, NN
            ).astype(BF16)
    for t in range(9):
        value = dot(patches[:, t * depth : (t + 1) * depth], row_low, TN)
        into = r["g3"].at[..., t * nm : (t + 1) * nm]
        into[...] = value.reshape(into.shape)
    weight_gradient(hg, dg2, r["g4"], grid_rows, pad, gtile, slice(3 * nm, 3 * nm + 128))
    hidden_grid = hg

    def grid_input_tile(i, carry):
        start = pl.multiple_of(i * gtile, gtile)
        value = None
        for du in range(3):
            here = pl.ds(pl.multiple_of(start + (2 - du) * pad, 16), gtile)
            part = dot(dg2[here, : 3 * nm], grid_two(du), NT) + dot(
                dg2[here, 3 * nm :], class_two(du), NT
            )
            value = part if value is None else value + part
        hidden_grid[pl.ds(pl.multiple_of(start + pad, 16), gtile), :] = value.astype(BF16)
        return carry

    lax.fori_loop(0, grid_rows // gtile, grid_input_tile, 0)
    hidden_grid_copy = pair_copy(hidden_grid.at[grid_span, away_g], r["dhg_in"], r["pair"].at[6])
    hidden_grid_copy.start()

    hidden_copy.wait()
    hidden_in = r["dhm_in"]

    def both_halves(start):
        here = pl.ds(pl.multiple_of(start + wide, 16), small_tile)
        received = hidden_in[pl.ds(start, small_tile), :]
        return hidden[here, own_m].astype(F32) + received.astype(F32)

    gain_one, bias_one = norm_backward(
        xh1, both_halves, r["spare"], dm, rows, wide, small_tile, nm, wide, mask_count, spread_m,
        row(norms, 0), row(norms, 1), scale_one,
    )
    weight_gradient(xm, dm, r["g0"], rows, wide, tile, slice(0, 3 * nm))
    hidden_grid_copy.wait()
    hidden_grid_in = r["dhg_in"]

    def both_grid_halves(start):
        here = pl.ds(pl.multiple_of(start + pad, 16), gtile)
        received = hidden_grid_in[pl.ds(start, gtile), :]
        return hidden_grid[here, own_g].astype(F32) + received.astype(F32)

    dg1 = r["dg1"]
    gain_grid, bias_grid = norm_backward(
        xhg, both_grid_halves, r["spare_g"], dg1, grid_rows, pad, gtile, ng, grid, grid_count,
        spread_g, row(gnorms, 0), row(gnorms, 1), scale_grid,
    )
    weight_gradient(xg, dg1, r["g1"], grid_rows, pad, gtile, slice(0, 3 * ng))

    smalls = r["smalls"]
    blank = jnp.zeros((1, 128), F32)
    pieces = [gain_one, bias_one, gain_two, bias_two]
    pieces += [gain_grid[:, i : i + nm] for i in range(0, ng, nm)]
    pieces += [bias_grid[:, i : i + nm] for i in range(0, ng, nm)]
    pieces += [class_bias_sum]
    pieces += [blank] * (16 - len(pieces))
    smalls[pos[0], pos[1], pos[2]] = jnp.concatenate(pieces, axis=0)
    small_share = Share(dims, smalls, r["ss"], r["sr"], False)
    small_share.advance()

    if fused:
        totals = [r["g%d" % i] for i in range(5)]
        staged = weights
        lands = [r["land%d" % i] for i in range(cfg["lands"])]
        for a, b in zip(totals, staged):
            cast_blocks(dims, a, b)
        run_rounds(dims, reduce_flows(dims, totals, staged, lands, r["rs"], r["rr"]))
        squares = jnp.zeros((1, 1), F32)
        for i in range(5):
            value = totals[i][pos[0], pos[1], pos[2]]
            r["out%d" % i][...] = value
            squares += jnp.sum(value * value, keepdims=True)
    small_share.complete()

    def add_small(d, acc):
        index = split_index(dims, d)
        return acc + smalls[index[0], index[1], index[2]]

    small_sum = lax.fori_loop(0, images, add_small, jnp.zeros((16, 128), F32))
    r["small_out"][...] = small_sum
    first_model = (model == 0).astype(F32)
    loss = jnp.sum(focal_sum, keepdims=True) + first_model * (dice_sum + contrast_sum)
    if fused:
        first_device = (own_image == 0).astype(F32)
        squares += first_device * jnp.sum(small_sum * small_sum, keepdims=True)
        sums = r["sums"]
        at = lax.broadcasted_iota(I32, (8, 128), 0)
        sums[pos[0], pos[1], pos[2], model] = jnp.where(at == 0, squares, loss)
        sum_share = Share(dims, sums, r["us"], r["ur"], True)
        sum_share.complete()

        def add_sums(d, acc):
            index = split_index(dims, d)
            return acc + sums[index[0], index[1], index[2], 0] + sums[
                index[0], index[1], index[2], 1
            ]

        r["sum_out"][...] = lax.fori_loop(0, images, add_sums, jnp.zeros((8, 128), F32))
        sum_share.drain()
    else:
        r["sum_out"][...] = jnp.broadcast_to(loss, (8, 128))
    for shared in (kernel_share, log_share, small_share):
        shared.drain()


def run_step(cfg, inputs, weights):
    dims, fused = cfg["dims"], cfg["fused"]
    rows, wide, pad, grid_rows = cfg["rows"], cfg["wide"], cfg["pad"], cfg["grid_rows"]
    nm, ng = cfg["nm"], cfg["ng"]
    any_space = {"xm_own", "xg_own"}
    names, args, specs = [], [], []
    for name, value in inputs.items():
        names.append(name)
        args.append(value)
        specs.append(pl.BlockSpec(memory_space=ANY if name in any_space else VMEM))
    for i, value in enumerate(weights):
        names.append("w%d_own" % i if fused else "w%d" % i)
        args.append(value)
        specs.append(pl.BlockSpec(memory_space=VMEM))
    outs = {"small_out": ((16, 128), F32), "sum_out": ((8, 128), F32)}
    scratch = {}
    if fused:
        blocks = [dims + w.shape for w in weights]
        for i, shape in enumerate(blocks):
            outs["out%d" % i] = (shape[3:], F32)
            scratch["w%d" % i] = VMEM(shape, BF16)
            scratch["g%d" % i] = VMEM(shape, F32)
        lands = landing_scratch(dims, blocks)
        cfg = dict(cfg, lands=len(lands))
        for i, land in enumerate(lands):
            scratch["land%d" % i] = land
        slots = flow_slots(dims, blocks)
        for name in ("gs", "gr", "rs", "rr"):
            scratch[name] = DMA((slots,))
        scratch["sums"] = VMEM(dims + (2, 8, 128), F32)
        scratch["us"], scratch["ur"] = share_sems(dims)
    else:
        for i, w in enumerate(weights):
            outs["g%d" % i] = (w.shape, F32)
    c_in = 2 * inputs["xm_own"].shape[1]
    depth = 2 * ng
    slot_rows = -(-inputs["masks"].shape[0] // 16) * 16
    scratch.update(
        xm=VMEM((rows + 2 * wide, c_in), BF16),
        xg=VMEM((grid_rows + 2 * pad, c_in), BF16),
        xh1=VMEM((rows, nm), F32),
        hm=VMEM((rows + 2 * wide, 2 * nm), BF16),
        xhg=VMEM((grid_rows, ng), F32),
        hg=VMEM((grid_rows + 2 * pad, depth), BF16),
        xh2=VMEM((rows, nm), F32),
        feature=VMEM((rows, nm), BF16),
        patches=VMEM((SLOTS, 9 * depth), BF16),
        kernels=VMEM(dims + (2, SLOTS, nm), BF16),
        logits=VMEM((slot_rows, rows), BF16),
        logits_in=VMEM((slot_rows, rows), BF16),
        logs=VMEM(dims + (8, SLOTS), F32),
        dm=VMEM((rows + 2 * wide, 3 * nm), BF16),
        spare=VMEM((rows, nm), F32),
        dhm_in=VMEM((rows, nm), BF16),
        dg2=VMEM((grid_rows + 2 * pad, 3 * nm + 128), BF16),
        dhg_in=VMEM((grid_rows, ng), BF16),
        dg1=VMEM((grid_rows + 2 * pad, 3 * ng), BF16),
        spare_g=VMEM((grid_rows, ng), F32),
        smalls=VMEM(dims + (16, 128), F32),
        local=DMA((7,)),
        pair=DMA((7, 2)),
    )
    for a, b in (("ks", "kr"), ("ls", "lr"), ("ss", "sr")):
        scratch[a], scratch[b] = share_sems(dims)
    names += list(outs) + list(scratch)
    result = pl.pallas_call(
        partial(step_kernel, cfg, tuple(names)),
        name="step",
        out_shape=[jax.ShapeDtypeStruct(s, d) for s, d in outs.values()],
        in_specs=specs,
        out_specs=[pl.BlockSpec(memory_space=VMEM)] * len(outs),
        scratch_shapes=list(scratch.values()),
        compiler_params=params(0),
    )(*args)
    return dict(zip(outs, result))


def lanes_of_taps(weight):
    taps, depth, width = weight.shape
    return weight.transpose(1, 0, 2).reshape(depth, taps * width)


def taps_of_lanes(weight, width):
    depth = weight.shape[0]
    return weight.reshape(depth, -1, width).transpose(1, 0, 2)


def class_lanes(weight):
    _, depth, width = weight.shape
    rows = weight.transpose(1, 0, 2).reshape(depth, 3, 3 * width)
    return jnp.pad(rows, ((0, 0), (0, 0), (0, 128 - 3 * width))).reshape(depth, 384)


def class_taps(weight, width):
    depth = weight.shape[0]
    rows = weight.reshape(depth, 3, 128)[:, :, : 3 * width]
    return rows.reshape(depth, 9, width).transpose(1, 0, 2)


def adam_update(weight, moment, square, gradient, rate):
    moment_new = BETA_ONE * moment + (1.0 - BETA_ONE) * gradient
    square_new = BETA_TWO * square + (1.0 - BETA_TWO) * gradient * gradient
    moment_hat = moment_new / (1.0 - BETA_ONE**STEP_TIME)
    square_hat = square_new / (1.0 - BETA_TWO**STEP_TIME)
    weight_new = weight - rate * (
        moment_hat / (jnp.sqrt(square_hat) + ADAM_EPS) + WEIGHT_DECAY * weight
    )
    return (weight_new, moment_new, square_new)


def body(
    mask_features,
    grid_features,
    instance_cells,
    instance_counts,
    instance_labels,
    instance_masks,
    mask_convs,
    mask_convs_moment,
    mask_convs_square,
    grid_first,
    grid_first_moment,
    grid_first_square,
    grid_second,
    grid_second_moment,
    grid_second_square,
    class_conv,
    class_conv_moment,
    class_conv_square,
    mask_norms,
    mask_norms_moment,
    mask_norms_square,
    grid_norms,
    grid_norms_moment,
    grid_norms_square,
    class_bias,
    class_bias_moment,
    class_bias_square,
):
    images = lax.axis_size("dp")
    data_index = lax.axis_index("dp")
    model_index = lax.axis_index("mp")
    dims = line_lengths(images)
    _, high, wide, half = mask_features.shape
    grid = grid_features.shape[1]
    pad = -(-(grid + 1) // 16) * 16
    nm, ng, kc = mask_convs.shape[3], grid_first.shape[2], class_conv.shape[2]
    count = instance_cells.shape[1]
    owner_rows = grid_first.shape[1]
    fused = owner_rows % 16 == 0
    cfg = dict(
        dims=dims,
        images=images,
        wide=wide,
        rows=high * wide,
        pad=pad,
        grid=grid,
        grid_rows=grid * pad,
        nm=nm,
        ng=ng,
        kc=kc,
        fused=fused,
        tile=8 * wide,
        small_tile=4 * wide,
        gtile=grid // 2 * pad,
    )

    share = jnp.float32(1.0 / images)
    counts = instance_counts.astype(F32)
    slot = jnp.arange(SLOTS)
    live = (slot[None, :] < instance_counts[:, None]).astype(F32)
    weights_all = live * (share / counts)[:, None]
    keys = jnp.stack([live, weights_all], axis=1)
    keys = jnp.pad(keys, ((0, 0), (0, 6), (0, 0)))
    own_live = lax.dynamic_index_in_dim(live, data_index, keepdims=False)
    own_weight = lax.dynamic_index_in_dim(weights_all, data_index, keepdims=False)
    own_count = lax.dynamic_index_in_dim(counts, data_index, keepdims=False)
    cols = jnp.stack([DICE_WEIGHT * own_weight, own_weight, own_live], axis=1)
    cols = jnp.pad(cols, ((0, 0), (0, 5)))
    cells = instance_cells[0]
    cells = (cells // grid) * pad + cells % grid
    cells = jnp.pad(cells, (0, SLOTS - count), constant_values=-(1 << 20))
    labels = instance_labels[0] - model_index * kc
    labels = jnp.pad(labels, (0, SLOTS - count), constant_values=-1)
    labels = jnp.where((labels >= 0) & (labels < kc), labels, -1)
    focal_rows = jnp.stack(
        [
            jnp.pad(class_bias, (0, 128 - kc)),
            own_live,
            jnp.full((128,), share / (own_count + 1.0)),
        ]
    )
    inputs = dict(
        xm_own=mask_features.reshape(-1, half),
        xg_own=jnp.pad(grid_features[0], ((0, 0), (0, pad - grid), (0, 0))).reshape(-1, half),
        masks=instance_masks[0],
        mask_norms=mask_norms,
        grid_norms=grid_norms,
        focal_rows=jnp.pad(focal_rows, ((0, 5), (0, 0))),
        cols=cols,
        cells_col=cells[:, None],
        cells_row=cells[None, :],
        labels_col=labels[:, None],
        keys=keys,
    )
    shards = [
        lanes_of_taps(mask_convs[0].astype(BF16)),
        lanes_of_taps(grid_first.astype(BF16)),
        lanes_of_taps(mask_convs[1].astype(BF16)),
        lanes_of_taps(grid_second.astype(BF16)),
        class_lanes(class_conv.astype(BF16)),
    ]
    if fused:
        out = run_step(cfg, inputs, shards)
        reduced = [out["out%d" % i] for i in range(5)]
        sums = out["sum_out"]
        total_squares, step_loss = sums[0, 0], sums[1, 0]
    else:
        blocks = gather_all(dims, shards)
        out = run_step(cfg, inputs, [b.reshape(-1, b.shape[-1]) for b in blocks])
        reduced = reduce_all(
            dims, [out["g%d" % i].reshape(b.shape) for i, b in enumerate(blocks)]
        )
        squares = sum(jnp.sum(jnp.square(value)) for value in reduced)
        squares += (data_index == 0).astype(F32) * jnp.sum(jnp.square(out["small_out"]))
        total_squares, step_loss = lax.psum((squares, out["sum_out"][0, 0]), ("dp", "mp"))
    small = out["small_out"]
    mask_sum_w = jnp.stack([taps_of_lanes(reduced[0], nm), taps_of_lanes(reduced[2], nm)])
    first_sum_w = taps_of_lanes(reduced[1], ng)
    second_sum_w = taps_of_lanes(reduced[3], nm)
    class_sum_w = class_taps(reduced[4], kc)
    per = ng // nm
    mask_norm_sum = small[:4]
    grid_norm_sum = small[4 : 4 + 2 * per].reshape(2, ng)
    bias_sum = small[4 + 2 * per, :kc]
    gradient_norm = jnp.sqrt(total_squares)
    factor = jnp.minimum(1.0, CLIP_LIMIT / gradient_norm)
    mask_new = adam_update(
        mask_convs, mask_convs_moment, mask_convs_square, mask_sum_w * factor, LEARN_RATE
    )
    first_new = adam_update(
        grid_first, grid_first_moment, grid_first_square, first_sum_w * factor, LEARN_RATE
    )
    second_new = adam_update(
        grid_second, grid_second_moment, grid_second_square, second_sum_w * factor, LEARN_RATE
    )
    class_new = adam_update(
        class_conv, class_conv_moment, class_conv_square, class_sum_w * factor, LEARN_RATE
    )
    mask_norm_new = adam_update(
        mask_norms, mask_norms_moment, mask_norms_square, mask_norm_sum * factor, SMALL_RATE
    )
    grid_norm_new = adam_update(
        grid_norms, grid_norms_moment, grid_norms_square, grid_norm_sum * factor, SMALL_RATE
    )
    bias_new = adam_update(
        class_bias, class_bias_moment, class_bias_square, bias_sum * factor, SMALL_RATE
    )
    return (
        step_loss,
        gradient_norm,
        mask_new[0],
        mask_new[1],
        mask_new[2],
        first_new[0],
        first_new[1],
        first_new[2],
        second_new[0],
        second_new[1],
        second_new[2],
        class_new[0],
        class_new[1],
        class_new[2],
        mask_norm_new[0],
        mask_norm_new[1],
        mask_norm_new[2],
        grid_norm_new[0],
        grid_norm_new[1],
        grid_norm_new[2],
        bias_new[0],
        bias_new[1],
        bias_new[2],
    )


def solution(mesh):
    in_specs = (
        P("dp", None, None, "mp"),
        P("dp", None, None, "mp"),
        P("dp", None),
        P(),
        P("dp", None),
        P("dp", None, None),
        P(None, None, "dp", "mp"),
        P(None, None, "dp", "mp"),
        P(None, None, "dp", "mp"),
        P(None, "dp", "mp"),
        P(None, "dp", "mp"),
        P(None, "dp", "mp"),
        P(None, "dp", "mp"),
        P(None, "dp", "mp"),
        P(None, "dp", "mp"),
        P(None, "dp", "mp"),
        P(None, "dp", "mp"),
        P(None, "dp", "mp"),
        P(None, "mp"),
        P(None, "mp"),
        P(None, "mp"),
        P(None, "mp"),
        P(None, "mp"),
        P(None, "mp"),
        P("mp"),
        P("mp"),
        P("mp"),
    )
    out_specs = (
        P(),
        P(),
        P(None, None, "dp", "mp"),
        P(None, None, "dp", "mp"),
        P(None, None, "dp", "mp"),
        P(None, "dp", "mp"),
        P(None, "dp", "mp"),
        P(None, "dp", "mp"),
        P(None, "dp", "mp"),
        P(None, "dp", "mp"),
        P(None, "dp", "mp"),
        P(None, "dp", "mp"),
        P(None, "dp", "mp"),
        P(None, "dp", "mp"),
        P(None, "mp"),
        P(None, "mp"),
        P(None, "mp"),
        P(None, "mp"),
        P(None, "mp"),
        P(None, "mp"),
        P("mp"),
        P("mp"),
        P("mp"),
    )
    return jax.shard_map(body, mesh=mesh, in_specs=in_specs, out_specs=out_specs, check_vma=False)
```

```python
from functools import partial

import jax
import jax.numpy as jnp
from jax import lax
from jax.experimental import pallas as pl
from jax.experimental.pallas import tpu as pltpu
from jax.sharding import PartitionSpec as P

GROUPS = 32
GN_EPS = 1e-05
CLIP_LIMIT = 0.02
LEARN_RATE = 0.02
SMALL_RATE = 0.5
BETA_ONE = 0.9
BETA_TWO = 0.95
ADAM_EPS = 1e-08
WEIGHT_DECAY = 0.05
CONTRAST_TEMP = 0.05
FOCAL_ALPHA = 0.25
DICE_WEIGHT = 3.0
STEP_TIME = 10.0
HIGHEST = lax.Precision.HIGHEST

MESH = pl.DeviceIdType.MESH
VMEM = pltpu.VMEM
ANY = pl.ANY
VMEM_LIMIT = 67043328
F32 = jnp.float32
BF16 = jnp.bfloat16
I32 = jnp.int32
SLOTS = 128
DMA = pltpu.SemaphoreType.DMA


def line_lengths(total):
    if total & (total - 1):
        return (total, 1, 1)
    bits = total.bit_length() - 1
    last = bits // 3
    middle = (bits - last) // 2
    return (1 << (bits - last - middle), 1 << middle, 1 << last)


def place(dims):
    index = lax.axis_index("dp")
    return (index // (dims[1] * dims[2]), (index // dims[2]) % dims[1], index % dims[2])


def split_index(dims, index):
    return (
        index // (dims[1] * dims[2]),
        lax.rem(index // dims[2], dims[1]),
        lax.rem(index, dims[2]),
    )


def along(dims, axis, step):
    stride = (dims[1] * dims[2], dims[2], 1)[axis]
    return {"dp": lax.axis_index("dp") + step * stride}


def partner():
    return {"mp": 1 - lax.axis_index("mp")}


def ring_step(dims, pos, axis, offset):
    other = lax.rem(pos[axis] + offset, dims[axis])
    return along(dims, axis, other - pos[axis])


def greet(dims):
    sem = pltpu.get_barrier_semaphore()
    pos = place(dims)
    count = 1
    for axis in range(3):
        for offset in range(1, dims[axis]):
            pl.semaphore_signal(
                sem, inc=1, device_id=ring_step(dims, pos, axis, offset), device_id_type=MESH
            )
            count += 1
    pl.semaphore_signal(sem, inc=1, device_id=partner(), device_id_type=MESH)
    pl.semaphore_wait(sem, count)


GATHER_ORDERS = ((2, 1, 0), (0, 2, 1), (0, 1, 2))
REDUCE_ORDERS = tuple(tuple(reversed(order)) for order in GATHER_ORDERS)


def line_copies(dims):
    return sum(n - 1 for n in dims)


def lane_cuts(width):
    tiles = width // 128
    if width % 128 or tiles < 3:
        return ((0, 0, width),)
    first = max(1, round(tiles * 0.1))
    second = (tiles - first) // 2
    sizes = (first, second, tiles - first - second)
    cuts, start = [], 0
    for order, size in enumerate(sizes):
        cuts.append((order, start * 128, size * 128))
        start += size
    return tuple(cuts)


class Exchange:
    def __init__(self):
        self.stages, self.lands, self.next = [], [], 0

    def finish(self):
        if 0 < self.next <= len(self.stages):
            for copy in self.stages[self.next - 1]:
                copy.wait_recv()
            self.lands[self.next - 1]()

    def start(self):
        if self.next < len(self.stages):
            for copy in self.stages[self.next]:
                copy.start()
        self.next += 1

    def drain(self):
        for stage in self.stages:
            for copy in stage:
                copy.wait_send()


def advance(*exchanges):
    for exchange in exchanges:
        exchange.finish()
    for exchange in exchanges:
        exchange.start()


def complete(*exchanges):
    while any(e.next <= len(e.stages) for e in exchanges):
        advance(*exchanges)


def nothing():
    return None


def gather_exchange(dims, out, send_sems, recv_sems, base, lanes, order, tail=None):
    pos = place(dims)
    result, done = Exchange(), set()
    tail = (slice(None), lanes) if tail is None else tail
    for axis in order:
        view = out.at[tuple(pl.ds(0, dims[k]) if k in done else pos[k] for k in range(3)) + tail]
        copies = []
        for offset in range(1, dims[axis]):
            copies.append(
                pltpu.make_async_remote_copy(
                    src_ref=view,
                    dst_ref=view,
                    send_sem=send_sems.at[base],
                    recv_sem=recv_sems.at[base],
                    device_id=ring_step(dims, pos, axis, offset),
                    device_id_type=MESH,
                )
            )
            base += 1
        if copies:
            result.stages.append(copies)
            result.lands.append(nothing)
        done.add(axis)
    return result


def share_exchange(dims, out, send_sems, recv_sems, core):
    model = lax.axis_index("mp")
    result = gather_exchange(
        dims, out, send_sems, recv_sems, 0, None, (2, 1, 0), (model,) if core else ()
    )
    if core:
        view = out.at[:, :, :, model]
        result.stages.append(
            [
                pltpu.make_async_remote_copy(
                    src_ref=view,
                    dst_ref=view,
                    send_sem=send_sems.at[line_copies(dims)],
                    recv_sem=recv_sems.at[line_copies(dims)],
                    device_id=partner(),
                    device_id_type=MESH,
                )
            ]
        )
        result.lands.append(nothing)
    return result


def landing_shapes(dims, rows, width, order):
    shapes, left = [], {0, 1, 2}
    for axis in order:
        left = left - {axis}
        shapes.append(
            (max(1, dims[axis] - 1),) + tuple(dims[k] for k in sorted(left)) + (rows, width)
        )
    return shapes


def reduce_exchange(dims, total, staged, lands, send_sems, recv_sems, base, lanes, order):
    pos = place(dims)
    result, reduced = Exchange(), set()
    for stage, axis in enumerate(order):
        n = dims[axis]
        free = [k for k in range(3) if k not in reduced and k != axis]

        def view(block, lead=None, axis=axis, reduced=frozenset(reduced)):
            lead = iter(lead) if lead is not None else None
            index = []
            for k in range(3):
                if k == axis:
                    index.append(block)
                elif k in reduced:
                    index.append(pos[k])
                else:
                    index.append(pl.ds(0, dims[k]) if lead is None else next(lead))
            return tuple(index) + (slice(None), lanes)

        copies = []
        for offset in range(1, n):
            copies.append(
                pltpu.make_async_remote_copy(
                    src_ref=staged.at[view(lax.rem(pos[axis] + offset, n))],
                    dst_ref=lands[stage].at[offset - 1],
                    send_sem=send_sems.at[base],
                    recv_sem=recv_sems.at[base],
                    device_id=ring_step(dims, pos, axis, offset),
                    device_id_type=MESH,
                )
            )
            base += 1

        def land(stage=stage, axis=axis, n=n, free=free, view=view):
            sizes = [dims[k] for k in free]
            blocks = 1
            for size in sizes:
                blocks *= size

            def add(i, carry):
                lead, rest = [], i
                for size in reversed(sizes):
                    lead.append(lax.rem(rest, size))
                    rest = rest // size
                lead = lead[::-1]
                index = view(pos[axis], lead)
                value = total[index]
                for k in range(n - 1):
                    value = value + lands[stage][(k,) + tuple(lead)].astype(F32)
                total[index] = value
                if sizes:
                    staged[index] = value.astype(BF16)
                return carry

            if blocks == 1:
                add(jnp.int32(0), 0)
            else:
                lax.fori_loop(0, blocks, add, 0)

        if copies:
            result.stages.append(copies)
            result.lands.append(land)
        reduced.add(axis)
    return result


def share_sems(dims):
    return [DMA((line_copies(dims) + 1,)), DMA((line_copies(dims) + 1,))]


def pair_copy(source, target, sems):
    return pltpu.make_async_remote_copy(
        src_ref=source,
        dst_ref=target,
        send_sem=sems.at[0],
        recv_sem=sems.at[1],
        device_id=partner(),
        device_id_type=MESH,
    )


def params(collective_id):
    return pltpu.CompilerParams(
        collective_id=collective_id, has_side_effects=True, vmem_limit_bytes=VMEM_LIMIT
    )


def gather_groups(dims, outs, send_sems, recv_sems):
    groups, base = [], 0
    for out in outs:
        group = []
        for order, start, size in lane_cuts(out.shape[4]):
            group.append(
                gather_exchange(
                    dims, out, send_sems, recv_sems, base, pl.ds(start, size), GATHER_ORDERS[order]
                )
            )
            base += line_copies(dims)
        groups.append(group)
    return groups


def reduce_groups(dims, totals, staged, lands, send_sems, recv_sems):
    groups, base, lands = [], 0, list(lands)
    for total, stage in zip(totals, staged):
        group = []
        for order, start, size in lane_cuts(total.shape[4]):
            group.append(
                reduce_exchange(
                    dims,
                    total,
                    stage,
                    lands[:3],
                    send_sems,
                    recv_sems,
                    base,
                    pl.ds(start, size),
                    REDUCE_ORDERS[order],
                )
            )
            lands = lands[3:]
            base += line_copies(dims)
        groups.append(group)
    return groups


def flow_slots(dims, shapes):
    return max(1, line_copies(dims) * sum(len(lane_cuts(s[-1])) for s in shapes))


def landing_scratch(dims, shapes):
    scratch = []
    for shape in shapes:
        for order, _, size in lane_cuts(shape[-1]):
            for land in landing_shapes(dims, shape[-2], size, REDUCE_ORDERS[order]):
                scratch.append(VMEM(land, BF16))
    return scratch


def cast_blocks(dims, total, staged):
    def cast(j, carry):
        index = split_index(dims, j)
        staged[index] = total[index].astype(BF16)
        return carry

    lax.fori_loop(0, dims[0] * dims[1] * dims[2], cast, 0)


def run_all(groups):
    exchanges = [exchange for group in groups for exchange in group]
    complete(*exchanges)
    for exchange in exchanges:
        exchange.drain()


def gather_kernel(dims, count, *refs):
    shards, outs = refs[:count], refs[count : 2 * count]
    send_sems, recv_sems, local_sems = refs[2 * count :]
    pos = place(dims)
    local = [
        pltpu.make_async_copy(shards[i], outs[i].at[pos[0], pos[1], pos[2]], local_sems.at[i])
        for i in range(count)
    ]
    for copy in local:
        copy.start()
    greet(dims)
    for copy in local:
        copy.wait()
    run_all(gather_groups(dims, outs, send_sems, recv_sems))


def gather_all(dims, shards):
    count = len(shards)
    shapes = [dims + s.shape for s in shards]
    slots = flow_slots(dims, shapes)
    return pl.pallas_call(
        partial(gather_kernel, dims, count),
        name="gather_weights",
        out_shape=[jax.ShapeDtypeStruct(s, BF16) for s in shapes],
        in_specs=[pl.BlockSpec(memory_space=VMEM)] * count,
        out_specs=[pl.BlockSpec(memory_space=VMEM)] * count,
        scratch_shapes=[DMA((slots,)), DMA((slots,)), DMA((count,))],
        compiler_params=params(1),
    )(*shards)


def reduce_kernel(dims, count, *refs):
    parts, outs = refs[:count], refs[count : 2 * count]
    send_sems, recv_sems, local_sems = refs[2 * count : 2 * count + 3]
    rest = list(refs[2 * count + 3 :])
    totals, staged, lands = rest[:count], rest[count : 2 * count], rest[2 * count :]
    pos = place(dims)
    local = [pltpu.make_async_copy(parts[i], totals[i], local_sems.at[i]) for i in range(count)]
    for copy in local:
        copy.start()
    greet(dims)
    for i in range(count):
        local[i].wait()
        cast_blocks(dims, totals[i], staged[i])
    run_all(reduce_groups(dims, totals, staged, lands, send_sems, recv_sems))
    for i in range(count):
        outs[i][...] = totals[i][pos[0], pos[1], pos[2]]


def reduce_all(dims, parts):
    count = len(parts)
    shapes = [p.shape for p in parts]
    slots = flow_slots(dims, shapes)
    scratch = [DMA((slots,)), DMA((slots,)), DMA((count,))]
    scratch += [VMEM(s, F32) for s in shapes] + [VMEM(s, BF16) for s in shapes]
    scratch += landing_scratch(dims, shapes)
    return pl.pallas_call(
        partial(reduce_kernel, dims, count),
        name="reduce_gradients",
        out_shape=[jax.ShapeDtypeStruct(s[3:], F32) for s in shapes],
        in_specs=[pl.BlockSpec(memory_space=ANY)] * count,
        out_specs=[pl.BlockSpec(memory_space=VMEM)] * count,
        scratch_shapes=scratch,
        compiler_params=params(2),
    )(*parts)


def group_sums(row, spread):
    width = row.shape[1]
    return lax.dot_general(
        jnp.broadcast_to(row, (8, width)),
        spread,
        (((1,), (0,)), ((), ())),
        precision=HIGHEST,
        preferred_element_type=F32,
    )[0:1]


def group_spread(width, group):
    rows = lax.broadcasted_iota(I32, (width, width), 0) // group
    cols = lax.broadcasted_iota(I32, (width, width), 1) // group
    return (rows == cols).astype(F32)


def dot(a, b, contract):
    return lax.dot_general(a, b, ((contract[0], contract[1]), ((), ())), preferred_element_type=F32)


NN = ((1,), (0,))
NT = ((1,), (1,))
TN = ((0,), (0,))


class Map:
    def __init__(self, high, width, live, span, part, channels, group):
        self.high, self.width, self.live = high, width, live
        self.span, self.part, self.channels = span, part, channels
        self.pixels = float(high * live * group)

    def column(self, span):
        shape = (span, self.width, self.channels)
        return lax.broadcasted_iota(I32, shape, 1).reshape(span * self.width, self.channels)

    def masked(self, value, span):
        if self.live == self.width:
            return value
        return jnp.where(self.column(span) < self.live, value, 0.0)

    def at(self, i, span):
        return pl.ds(pl.multiple_of(i * span * self.width, 16), span * self.width)


def take(source, first, count, lanes=slice(None)):
    value = source[pl.ds(first, count), :, lanes]
    return value.reshape(-1, value.shape[2])


def conv_forward(m, source, weight, raw, first=0, last=None, total=None):
    n, tile = m.channels, m.span * m.width

    def body(i, total):
        wide = None
        for du in range(3):
            part = dot(take(source, i * m.span + du, m.span), weight(du), NN)
            wide = part if wide is None else wide + part
        left = pltpu.roll(wide[:, :n], 1, 0)
        right = pltpu.roll(wide[:, 2 * n :], tile - 1, 0)
        if m.live == m.width:
            column = m.column(m.span)
            left = jnp.where(column == 0, 0.0, left)
            right = jnp.where(column == m.width - 1, 0.0, right)
        value = m.masked(left + wide[:, n : 2 * n] + right, m.span)
        raw[m.at(i, m.span), :] = value
        return total + jnp.sum(value, axis=0, keepdims=True)

    last = m.high // m.span if last is None else last
    total = jnp.zeros((1, n), F32) if total is None else total
    return lax.fori_loop(first, last, body, total)


def norm_forward(m, raw, total, spread, gain, bias, store):
    n, part = m.channels, m.part
    mean = group_sums(total, spread) / m.pixels

    def spread_of(i, acc):
        away = m.masked(raw[m.at(i, part), :] - mean, part)
        return acc + jnp.sum(away * away, axis=0, keepdims=True)

    squares = lax.fori_loop(0, m.high // part, spread_of, jnp.zeros((1, n), F32))
    scale = lax.rsqrt(group_sums(squares, spread) / m.pixels + GN_EPS)

    def normalize(i, carry):
        normed = (raw[m.at(i, part), :] - mean) * scale
        raw[m.at(i, part), :] = normed
        value = m.masked(jnp.maximum(normed * gain + bias, 0.0), part)
        store(i, value.astype(BF16))
        return carry

    lax.fori_loop(0, m.high // part, normalize, 0)
    return scale


def norm_backward(m, normed, upstream, spare, shifted, spread, gain, bias, scale):
    n, part = m.channels, m.part
    tile = part * m.width

    def first(i, sums):
        here = normed[m.at(i, part), :]
        value = m.masked(jnp.where(here * gain + bias > 0.0, upstream(i), 0.0), part)
        spare[m.at(i, part), :] = value
        return (
            sums[0] + jnp.sum(value * here, axis=0, keepdims=True),
            sums[1] + jnp.sum(value, axis=0, keepdims=True),
        )

    zero = jnp.zeros((1, n), F32)
    gain_sum, bias_sum = lax.fori_loop(0, m.high // part, first, (zero, zero))
    level = group_sums(bias_sum * gain, spread) / m.pixels
    slope = group_sums(gain_sum * gain, spread) / m.pixels

    def second(i, carry):
        value = scale * (spare[m.at(i, part), :] * gain - level - normed[m.at(i, part), :] * slope)
        value = m.masked(value, part)
        left = pltpu.roll(value, tile - 1, 0)
        right = pltpu.roll(value, 1, 0)
        if m.live == m.width:
            column = m.column(part)
            left = jnp.where(column == m.width - 1, 0.0, left)
            right = jnp.where(column == 0, 0.0, right)
        into = pl.ds(i * part + 1, part)
        for k, piece in enumerate((left, value, right)):
            shifted[into, :, k * n : (k + 1) * n] = piece.astype(BF16).reshape(part, m.width, n)
        return carry

    lax.fori_loop(0, m.high // part, second, 0)
    return gain_sum, bias_sum


def weight_gradient(m, source, shifted, total, lanes):
    width = lanes.stop - lanes.start

    def body(i, carry):
        right = take(shifted, i * m.span + 1, m.span, lanes)
        for du in range(3):
            value = dot(take(source, i * m.span + du, m.span), right, TN)
            into = total.at[..., du * width : (du + 1) * width]
            value = value.reshape(into.shape)

            @pl.when(i == 0)
            def _(into=into, value=value):
                into[...] = value

            @pl.when(i > 0)
            def _(into=into, value=value):
                into[...] += value

        return carry

    lax.fori_loop(0, m.high // m.span, body, 0)


def zero_edges(ref):
    blank = jnp.zeros((1,) + ref.shape[1:], ref.dtype)
    ref[0:1] = blank
    ref[ref.shape[0] - 1 : ref.shape[0]] = blank


def diagonal(n):
    return lax.broadcasted_iota(I32, (n, n), 0) == lax.broadcasted_iota(I32, (n, n), 1)


def as_row(column):
    return jnp.sum(jnp.where(diagonal(column.shape[0]), column, 0.0), axis=0, keepdims=True)


def as_column(row):
    return jnp.sum(jnp.where(diagonal(row.shape[1]), row, 0.0), axis=1, keepdims=True)


def step_kernel(cfg, names, *refs):
    r = dict(zip(names, refs))
    dims, images, fused = cfg["dims"], cfg["images"], cfg["fused"]
    big, small = cfg["mask_map"], cfg["grid_map"]
    nm, ng, kc = big.channels, small.channels, cfg["kc"]
    grid, pad = small.live, small.width
    rows, grid_rows = big.high * big.width, small.high * small.width
    gtile = small.span * small.width
    pos = place(dims)
    model = lax.axis_index("mp")
    own_image = lax.axis_index("dp")

    def lanes_of(width, side):
        return pl.ds(pl.multiple_of(side * width, width), width)

    own_m, away_m = lanes_of(nm, model), lanes_of(nm, 1 - model)
    own_g, away_g = lanes_of(ng, model), lanes_of(ng, 1 - model)
    own_x = lanes_of(r["xm_own"].shape[3], model)
    map_rows, grid_span = pl.ds(1, big.high), pl.ds(1, small.high)
    spread_m = group_spread(nm, 2 * nm // GROUPS)
    spread_g = group_spread(ng, 2 * ng // GROUPS)

    xm, xg, hm, hg, dm = r["xm"], r["xg"], r["hm"], r["hg"], r["dm"]
    dg1, dg2 = r["dg1"], r["dg2"]
    mask_in, grid_in = r["xm_own"].at[0], r["xg_own"].at[0]
    mask_into = xm.at[map_rows, :, own_x]
    grid_into = xg.at[grid_span, pl.ds(0, grid), own_x]
    local = [
        pltpu.make_async_copy(mask_in, mask_into, r["local"].at[0]),
        pltpu.make_async_copy(grid_in, grid_into, r["local"].at[1]),
    ]
    for copy in local:
        copy.start()
    weights = [r["w%d" % i] for i in range(5)]
    groups = []
    if fused:
        for t in range(9):
            for i, value in (
                (0, r["mask_convs"][0, t]),
                (1, r["grid_first"][t]),
                (2, r["mask_convs"][1, t]),
                (3, r["grid_second"][t]),
            ):
                width = value.shape[1]
                weights[i][pos[0], pos[1], pos[2], :, t * width : (t + 1) * width] = value.astype(
                    BF16
                )
        class_in = r["class_conv"]
        for du in range(3):
            pieces = [class_in[3 * du + dv] for dv in range(3)]
            pieces.append(jnp.zeros((class_in.shape[1], 128 - 3 * kc), F32))
            weights[4][pos[0], pos[1], pos[2], :, du * 128 : (du + 1) * 128] = jnp.concatenate(
                pieces, axis=1
            ).astype(BF16)
        groups = gather_groups(dims, weights, r["gs"], r["gr"])

    def bring(*which):
        if fused:
            advance(*[exchange for i in which for exchange in groups[i]])

    greet(dims)
    feature_copies = [
        pair_copy(mask_in, mask_into, r["pair"].at[0]),
        pair_copy(grid_in, grid_into, r["pair"].at[1]),
    ]
    for copy in feature_copies:
        copy.start()
    bring(0)
    bring(1)

    for ref in (xm, xg, hm, hg, dm, dg1, dg2):
        zero_edges(ref)
    xg[:, grid:, :] = jnp.zeros((xg.shape[0], pad - grid, xg.shape[2]), BF16)
    share = jnp.float32(1.0 / images)
    table, bias_table = r["table"], r["bias_table"]
    slots = r["cells"].shape[1]
    table[...] = jnp.full(table.shape, -(1 << 20), I32)
    table[0:1, 0:slots] = r["cells"][...]
    table[1:2, 0:slots] = r["labels"][...]
    bias_table[...] = jnp.zeros(bias_table.shape, F32)
    bias_table[0:1, 0:kc] = r["class_bias"][...]
    cells = table[0:1, :].astype(F32)
    cells = cells + jnp.floor((cells + 0.5) / grid) * (pad - grid)
    cells_row = cells.astype(I32)
    cells_col = as_column(cells).astype(I32)
    labels_col = as_column(table[1:2, :].astype(F32)).astype(I32) - model * kc
    class_bias = bias_table[0:1, :]
    own_count = r["counts"][own_image]
    slot_lanes = lax.broadcasted_iota(I32, (1, SLOTS), 1)
    slot_rows = lax.broadcasted_iota(I32, (SLOTS, 1), 0)
    own_float = jnp.full((1, 1), own_count, I32).astype(F32)
    live_row = (slot_lanes < own_count).astype(F32)
    live_col = (slot_rows < own_count).astype(F32)
    weight_col = live_col * (share / own_float)
    dice_col = DICE_WEIGHT * weight_col
    focal_scale = share / (own_float + 1.0)
    bring(0)
    bring(0)
    bring(1)

    def weight(i, span):
        def part(du):
            value = weights[i][..., du * span : (du + 1) * span]
            return value.reshape(-1, span) if fused else value

        return part

    mask_one, grid_one, mask_two = weight(0, 3 * nm), weight(1, 3 * ng), weight(2, 3 * nm)
    grid_two, class_two = weight(3, 3 * nm), weight(4, 128)

    norms, gnorms = r["mask_norms"], r["grid_norms"]
    row = lambda ref, k: ref[k : k + 1, :]
    bring(2)
    for copy in local:
        copy.wait()
    feature_copies[0].wait()
    bring(0)
    xh1 = r["xh1"]
    half = big.high // big.span // 2
    total = conv_forward(big, xm, mask_one, xh1, 0, half)
    bring(1)
    total = conv_forward(big, xm, mask_one, xh1, half, None, total)
    bring(2)
    bring(3)

    def keep_mask(i, value):
        hm[pl.ds(i * big.part + 1, big.part), :, own_m] = value.reshape(big.part, big.width, nm)

    scale_one = norm_forward(big, xh1, total, spread_m, row(norms, 0), row(norms, 1), keep_mask)
    hm_copy = pair_copy(
        hm.at[map_rows, :, own_m], hm.at[map_rows, :, own_m], r["pair"].at[2]
    )
    hm_copy.start()
    bring(2)
    feature_copies[1].wait()
    bring(1)
    bring(3)
    bring(4)
    xhg = r["xhg"]
    total = conv_forward(small, xg, grid_one, xhg)
    bring(2)
    bring(3)
    bring(4)

    def keep_grid(i, value):
        hg[pl.ds(i * small.part + 1, small.part), :, own_g] = value.reshape(
            small.part, small.width, ng
        )

    scale_grid = norm_forward(
        small, xhg, total, spread_g, row(gnorms, 0), row(gnorms, 1), keep_grid
    )
    hg_copy = pair_copy(
        hg.at[grid_span, :, own_g], hg.at[grid_span, :, own_g], r["pair"].at[3]
    )
    hg_copy.start()

    hm_copy.wait()
    xh2, feature = r["xh2"], r["feature"]
    total = conv_forward(big, hm, mask_two, xh2)
    bring(3)
    bring(4)

    def keep_feature(i, value):
        feature[big.at(i, big.part), :] = value

    scale_two = norm_forward(
        big, xh2, total, spread_m, row(norms, 2), row(norms, 3), keep_feature
    )
    for group in groups:
        complete(*group)
        for exchange in group:
            exchange.drain()

    hg_copy.wait()
    patches = r["patches"]
    lane = lax.broadcasted_iota(I32, (SLOTS, grid_rows), 1)
    depth = hg.shape[2]
    picked = None
    for t in range(9):
        chosen = (lane == cells_col + ((t // 3 - 1) * pad + t % 3 - 1)).astype(F32).astype(BF16)
        part = dot(chosen, take(hg, 1, small.high), NN).astype(BF16)
        patches[:, t * depth : (t + 1) * depth] = part
        w = grid_two(t // 3)[:, (t % 3) * nm : (t % 3 + 1) * nm]
        part = dot(part, w, NN)
        picked = part if picked is None else picked + part
    kernels = r["kernels"]
    kernels[pos[0], pos[1], pos[2], model] = picked.astype(BF16)
    kernel_share = share_exchange(dims, kernels, r["ks"], r["kr"], True)
    advance(kernel_share)

    kernel_rows = kernels[pos[0], pos[1], pos[2], model]
    logits, logits_in = r["logits"], r["logits_in"]
    high_slots = logits.shape[0]
    tile = big.span * big.width
    for i in range(rows // tile):
        span = slice(i * tile, (i + 1) * tile)
        logits[:, span] = dot(kernel_rows[:high_slots], feature[span, :], NT).astype(BF16)
    logits_copy = pair_copy(logits, logits_in, r["pair"].at[4])
    logits_copy.start()
    advance(kernel_share)

    class_hot = (
        (lax.broadcasted_iota(I32, (SLOTS, 128), 1) == labels_col).astype(F32).astype(BF16)
    )

    def class_tile(i, sums):
        value = None
        for du in range(3):
            part = dot(take(hg, i * small.span + du, small.span), class_two(du), NN)
            value = part if value is None else value + part
        x = (
            pltpu.roll(value, 1, 0)
            + pltpu.roll(value, 128 - kc, 1)
            + pltpu.roll(pltpu.roll(value, 128 - 2 * kc, 1), gtile - 1, 0)
            + class_bias
        )
        at = lax.broadcasted_iota(I32, (gtile, SLOTS), 0) + i * gtile
        cell_hot = jnp.where(at == cells_row, live_row, 0.0).astype(BF16)
        t = dot(cell_hot, class_hot, NN)
        lanes = lax.broadcasted_iota(I32, (gtile, 128), 1)
        column = lax.broadcasted_iota(I32, (small.span, pad, 128), 1).reshape(gtile, 128)
        real = (column < grid) & (lanes < kc)
        tiny = jnp.exp(-jnp.abs(x))
        extra = jnp.log1p(tiny)
        inverse = 1.0 / (1.0 + tiny)
        q = jnp.where(x >= 0.0, 1.0, tiny) * inverse
        p = jnp.where(x >= 0.0, tiny, 1.0) * inverse
        log_q = -(jnp.maximum(-x, 0.0) + extra)
        log_p = -(jnp.maximum(x, 0.0) + extra)
        terms = FOCAL_ALPHA * t * p * p * log_q + (1.0 - FOCAL_ALPHA) * (1.0 - t) * q * q * log_p
        slope = FOCAL_ALPHA * t * p * p * (p - 2.0 * q * log_q) + (1.0 - FOCAL_ALPHA) * (
            1.0 - t
        ) * q * q * (2.0 * p * log_p - q)
        slope = jnp.where(real, -focal_scale * slope, 0.0).astype(BF16).astype(F32)
        shifted = (
            pltpu.roll(slope, gtile - 1, 0)
            + pltpu.roll(slope, kc, 1)
            + pltpu.roll(pltpu.roll(slope, 2 * kc, 1), 1, 0)
        )
        dg2[pl.ds(i * small.span + 1, small.span), :, 3 * nm :] = shifted.astype(BF16).reshape(
            small.span, pad, 128
        )
        return (
            sums[0] + jnp.sum(jnp.where(real, -focal_scale * terms, 0.0), axis=0, keepdims=True),
            sums[1] + jnp.sum(slope, axis=0, keepdims=True),
        )

    zero = jnp.zeros((1, 128), F32)
    focal_sum, class_bias_sum = lax.fori_loop(
        0, small.high // small.span, class_tile, (zero, zero)
    )
    advance(kernel_share)

    logits_copy.wait()
    masks = r["masks"].at[0]
    dice_sum = jnp.zeros((1, 1), F32)
    for start in range(0, slots, 16):
        span = slice(start, start + 16)
        x = logits[span, :].astype(F32) + logits_in[span, :].astype(F32)
        s = jax.nn.sigmoid(x)
        mask = masks[start : min(start + 16, slots), :].astype(F32)
        if mask.shape[0] < 16:
            mask = jnp.concatenate([mask, jnp.zeros((16 - mask.shape[0], rows), F32)], axis=0)
        inter = jnp.sum(s * mask, axis=1, keepdims=True)
        whole = jnp.sum(s * s, axis=1, keepdims=True) + jnp.sum(mask, axis=1, keepdims=True) + 1.0
        share_here = dice_col[span]
        dice_sum += jnp.sum(share_here * (1.0 - 2.0 * inter / whole), keepdims=True)
        a = -2.0 * share_here / whole
        b = 2.0 * share_here * inter / (whole * whole)
        logits[span, :] = ((a * mask + 2.0 * b * s) * s * (1.0 - s)).astype(BF16)
    complete(kernel_share)

    own_full = [kernels[pos[0], pos[1], pos[2], k] for k in range(2)]

    def key_block(d):
        index = split_index(dims, d)
        return [kernels[index[0], index[1], index[2], k] for k in range(2)]

    def squares_of(block):
        return sum(
            jnp.sum(jnp.square(part.astype(F32)), axis=1, keepdims=True) for part in block
        )

    own_scale = lax.rsqrt(squares_of(own_full) + 1e-06)
    same_slot = diagonal(SLOTS)

    def scores(d):
        block = key_block(d)
        raw = dot(own_full[0], block[0], NT) + dot(own_full[1], block[1], NT)
        key_scale = lax.rsqrt(as_row(squares_of(block)) + 1e-06)
        scale = own_scale * key_scale / CONTRAST_TEMP
        live = slot_lanes < r["counts"][d]
        allowed = live & jnp.logical_not(same_slot & (d == own_image))
        return block, raw, key_scale, scale, allowed

    def sum_keys(d, acc):
        _, raw, _, scale, allowed = scores(d)
        value = jnp.where(allowed, jnp.exp(raw * scale), 0.0)
        return acc + jnp.sum(value, axis=1, keepdims=True)

    totals_col = lax.fori_loop(0, images, sum_keys, jnp.zeros((SLOTS, 1), F32))
    log_col = jnp.log(totals_col)
    contrast_sum = jnp.sum(
        jnp.where(weight_col > 0.0, weight_col * log_col, 0.0), keepdims=True
    )
    logs = r["logs"]
    logs[pos[0], pos[1], pos[2]] = jnp.broadcast_to(as_row(log_col), (8, SLOTS))
    log_share = share_exchange(dims, logs, r["ls"], r["lr"], False)
    advance(log_share)

    totals = [r["g%d" % i] for i in range(5)]
    out_groups = []
    if fused:
        staged = [weights[2], weights[1], weights[0], weights[3], weights[4]]
        lands = [r["land%d" % i] for i in range(cfg["lands"])]
        out_groups = reduce_groups(dims, totals, staged, lands, r["rs"], r["rr"])

    def send(*which):
        if fused:
            advance(*[exchange for i in which for exchange in out_groups[i]])

    def send_first(i):
        if fused:
            cast_blocks(dims, totals[i], staged[i])
            send(i)

    logit_rows = dot(logits[...], feature[...], NN)
    advance(log_share)
    dlogits, part_rows = logits, big.part * big.width

    def from_logits(i):
        pixels = pl.ds(pl.multiple_of(i * part_rows, part_rows), part_rows)
        return dot(dlogits[:, pixels], kernel_rows[:high_slots], TN)

    gain_two, bias_two = norm_backward(
        big, xh2, from_logits, r["spare"], dm, spread_m, row(norms, 2), row(norms, 3), scale_two
    )
    advance(log_share)
    weight_gradient(big, hm, dm, totals[2], slice(0, 3 * nm))
    send_first(2)
    complete(log_share)
    hidden = hm

    def input_tile(i, carry):
        value = None
        for du in range(3):
            part = dot(take(dm, i * big.span + 2 - du, big.span), mask_two(du), NT)
            value = part if value is None else value + part
        hidden[pl.ds(i * big.span + 1, big.span)] = value.astype(BF16).reshape(
            big.span, big.width, 2 * nm
        )
        return carry

    lax.fori_loop(0, big.high // big.span, input_tile, 0)
    hidden_copy = pair_copy(hidden.at[map_rows, :, away_m], r["dhm_in"], r["pair"].at[5])
    hidden_copy.start()
    send(2)

    def row_terms(d, acc):
        block, raw, key_scale, scale, allowed = scores(d)
        index = split_index(dims, d)
        log_row = logs[index[0], index[1], index[2]][0:1]
        value = raw * scale
        query = jnp.where(allowed, jnp.exp(value - log_col) * weight_col, 0.0)
        key_count = jnp.full((1, 1), r["counts"][d], I32).astype(F32)
        keyed = allowed & (live_col > 0.5)
        key = jnp.where(keyed, jnp.exp(value - log_row) * (share / key_count), 0.0)
        query_low = (query * scale).astype(BF16)
        key_low = (key * scale).astype(BF16)
        mine = jnp.where(model == 0, block[0].astype(F32), block[1].astype(F32)).astype(BF16)
        return (
            acc[0] + dot(query_low, mine, NN) + dot(key_low, mine, NN),
            acc[1]
            + jnp.sum((query + key) * raw * key_scale / CONTRAST_TEMP, axis=1, keepdims=True),
        )

    row_sum, scale_sum = lax.fori_loop(
        0, images, row_terms, (jnp.zeros((SLOTS, nm), F32), jnp.zeros((SLOTS, 1), F32))
    )
    norm_grad = -0.5 * own_scale * own_scale * own_scale * scale_sum
    row_grad = row_sum + 2.0 * kernel_rows.astype(F32) * norm_grad
    row_grad = row_grad + jnp.concatenate(
        [logit_rows, jnp.zeros((SLOTS - high_slots, nm), F32)], axis=0
    )
    row_low = row_grad.astype(BF16)

    weight_gradient(small, hg, dg2, totals[4], slice(3 * nm, 3 * nm + 128))
    send(2)
    for i in range(small.high // small.span):
        at = lax.broadcasted_iota(I32, (gtile, SLOTS), 0) + i * gtile
        for dv in range(3):
            chosen = (at == cells_row + (dv - 1)).astype(F32).astype(BF16)
            dg2[1 + i * small.span : 1 + (i + 1) * small.span, :, dv * nm : (dv + 1) * nm] = (
                dot(chosen, row_low, NN).astype(BF16).reshape(small.span, pad, nm)
            )
    hidden_grid = hg

    def grid_input_tile(i, carry):
        value = None
        for du in range(3):
            first = i * small.span + 2 - du
            part = dot(take(dg2, first, small.span, slice(0, 3 * nm)), grid_two(du), NT) + dot(
                take(dg2, first, small.span, slice(3 * nm, 3 * nm + 128)), class_two(du), NT
            )
            value = part if value is None else value + part
        hidden_grid[pl.ds(i * small.span + 1, small.span)] = value.astype(BF16).reshape(
            small.span, pad, 2 * ng
        )
        return carry

    lax.fori_loop(0, small.high // small.span, grid_input_tile, 0)
    hidden_grid_copy = pair_copy(
        hidden_grid.at[grid_span, :, away_g], r["dhg_in"], r["pair"].at[6]
    )
    hidden_grid_copy.start()
    for t in range(9):
        value = dot(patches[:, t * depth : (t + 1) * depth], row_low, TN)
        into = totals[3].at[..., t * nm : (t + 1) * nm]
        into[...] = value.reshape(into.shape)
    send_first(3)
    send_first(4)
    send(2)

    hidden_grid_copy.wait()
    hidden_grid_in = r["dhg_in"]

    def both_grid_halves(i):
        mine = take(hidden_grid, i * small.part + 1, small.part, own_g)
        return mine.astype(F32) + take(hidden_grid_in, i * small.part, small.part).astype(F32)

    gain_grid, bias_grid = norm_backward(
        small, xhg, both_grid_halves, r["spare_g"], dg1, spread_g, row(gnorms, 0),
        row(gnorms, 1), scale_grid,
    )
    send(3, 4)
    weight_gradient(small, xg, dg1, totals[1], slice(0, 3 * ng))
    send_first(1)
    hidden_copy.wait()
    hidden_in = r["dhm_in"]

    def both_halves(i):
        mine = take(hidden, i * big.part + 1, big.part, own_m)
        return mine.astype(F32) + take(hidden_in, i * big.part, big.part).astype(F32)

    gain_one, bias_one = norm_backward(
        big, xh1, both_halves, r["spare"], dm, spread_m, row(norms, 0), row(norms, 1), scale_one
    )
    send(3, 4)
    send(1)
    weight_gradient(big, xm, dm, totals[0], slice(0, 3 * nm))
    send_first(0)

    smalls = r["smalls"]
    blank = jnp.zeros((1, 128), F32)
    pieces = [gain_one, bias_one, gain_two, bias_two]
    pieces += [gain_grid[:, i : i + nm] for i in range(0, ng, nm)]
    pieces += [bias_grid[:, i : i + nm] for i in range(0, ng, nm)]
    pieces += [class_bias_sum]
    pieces += [blank] * (16 - len(pieces))
    smalls[pos[0], pos[1], pos[2]] = jnp.concatenate(pieces, axis=0)
    small_share = share_exchange(dims, smalls, r["ss"], r["sr"], False)
    advance(small_share)
    send(3, 4)
    send(1)
    send(0)
    advance(small_share)

    squares = jnp.zeros((1, 1), F32)

    def hand_out(i):
        complete(*out_groups[i])
        value = totals[i][pos[0], pos[1], pos[2]]
        r["out%d" % i][...] = value
        return jnp.sum(value * value, keepdims=True)

    if fused:
        for i in (2, 3, 4):
            squares += hand_out(i)
        send(1)
        send(0)
        squares += hand_out(1)
    complete(small_share)

    def add_small(d, acc):
        index = split_index(dims, d)
        return acc + smalls[index[0], index[1], index[2]]

    small_sum = lax.fori_loop(0, images, add_small, jnp.zeros((16, 128), F32))
    r["small_out"][...] = small_sum
    first_model = (model == 0).astype(F32)
    loss = jnp.sum(focal_sum, keepdims=True) + first_model * (dice_sum + contrast_sum)
    if fused:
        squares += hand_out(0)
        first_device = (own_image == 0).astype(F32)
        squares += first_device * jnp.sum(small_sum * small_sum, keepdims=True)
        sums = r["sums"]
        at = lax.broadcasted_iota(I32, (8, 128), 0)
        sums[pos[0], pos[1], pos[2], model] = jnp.where(at == 0, squares, loss)
        sum_share = share_exchange(dims, sums, r["us"], r["ur"], True)
        complete(sum_share)

        def add_sums(d, acc):
            index = split_index(dims, d)
            return acc + sums[index[0], index[1], index[2], 0] + sums[
                index[0], index[1], index[2], 1
            ]

        r["sum_out"][...] = lax.fori_loop(0, images, add_sums, jnp.zeros((8, 128), F32))
        sum_share.drain()
    else:
        r["sum_out"][...] = jnp.broadcast_to(loss, (8, 128))
    for shared in (kernel_share, log_share, small_share):
        shared.drain()
    for group in out_groups:
        for exchange in group:
            exchange.drain()


def run_step(cfg, inputs, weights, blocks):
    dims, fused = cfg["dims"], cfg["fused"]
    big, small = cfg["mask_map"], cfg["grid_map"]
    nm, ng = big.channels, small.channels
    rows, grid_rows = big.high * big.width, small.high * small.width
    inputs = dict(inputs, **weights)
    spaces = dict(xm_own=ANY, xg_own=ANY, counts=pltpu.SMEM)
    names = list(inputs)
    specs = [pl.BlockSpec(memory_space=spaces.get(name, VMEM)) for name in names]
    outs = {"small_out": ((16, 128), F32), "sum_out": ((8, 128), F32)}
    scratch = {}
    if fused:
        for i, shape in enumerate(blocks):
            outs["out%d" % i] = (shape[3:], F32)
            scratch["w%d" % i] = VMEM(shape, BF16)
            scratch["g%d" % i] = VMEM(shape, F32)
        lands = landing_scratch(dims, blocks)
        cfg = dict(cfg, lands=len(lands))
        for i, land in enumerate(lands):
            scratch["land%d" % i] = land
        slots = flow_slots(dims, blocks)
        for name in ("gs", "gr", "rs", "rr"):
            scratch[name] = DMA((slots,))
        scratch["sums"] = VMEM(dims + (2, 8, 128), F32)
        scratch["us"], scratch["ur"] = share_sems(dims)
    else:
        for i in range(5):
            outs["g%d" % i] = (inputs["w%d" % i].shape, F32)
    c_in = 2 * inputs["xm_own"].shape[3]
    depth = 2 * ng
    slot_rows = -(-inputs["masks"].shape[1] // 16) * 16

    def padded(m, channels):
        return VMEM((m.high + 2, m.width, channels), BF16)

    scratch.update(
        xm=padded(big, c_in),
        xg=padded(small, c_in),
        xh1=VMEM((rows, nm), F32),
        hm=padded(big, 2 * nm),
        xhg=VMEM((grid_rows, ng), F32),
        hg=padded(small, depth),
        xh2=VMEM((rows, nm), F32),
        feature=VMEM((rows, nm), BF16),
        patches=VMEM((SLOTS, 9 * depth), BF16),
        kernels=VMEM(dims + (2, SLOTS, nm), BF16),
        logits=VMEM((slot_rows, rows), BF16),
        logits_in=VMEM((slot_rows, rows), BF16),
        logs=VMEM(dims + (8, SLOTS), F32),
        dm=padded(big, 3 * nm),
        spare=VMEM((rows, nm), F32),
        dhm_in=VMEM((big.high, big.width, nm), BF16),
        dg2=padded(small, 3 * nm + 128),
        dhg_in=VMEM((small.high, small.width, ng), BF16),
        dg1=padded(small, 3 * ng),
        spare_g=VMEM((grid_rows, ng), F32),
        smalls=VMEM(dims + (16, 128), F32),
        table=VMEM((8, SLOTS), I32),
        bias_table=VMEM((8, 128), F32),
        local=DMA((2,)),
        pair=DMA((7, 2)),
    )
    for a, b in (("ks", "kr"), ("ls", "lr"), ("ss", "sr")):
        scratch[a], scratch[b] = share_sems(dims)
    names += list(outs) + list(scratch)
    result = pl.pallas_call(
        partial(step_kernel, cfg, tuple(names)),
        name="step",
        out_shape=[jax.ShapeDtypeStruct(s, d) for s, d in outs.values()],
        in_specs=specs,
        out_specs=[pl.BlockSpec(memory_space=VMEM)] * len(outs),
        scratch_shapes=list(scratch.values()),
        compiler_params=params(0),
    )(*inputs.values())
    return dict(zip(outs, result))


def update_kernel(nm, ng, kc, *refs):
    reduced, small, sums = refs[:5], refs[5], refs[6]
    states, outs = refs[7:28], refs[28:]
    total = sums[0:1, 0:1]
    norm = jnp.sqrt(total)
    outs[0][...] = sums[1:2, 0:1]
    outs[1][...] = norm
    factor = jnp.minimum(1.0, CLIP_LIMIT / norm)

    def update(which, index, gradient, rate):
        old = [states[3 * which + k][index] for k in range(3)]
        new = adam_update(*old, gradient * factor, rate)
        for k in range(3):
            outs[2 + 3 * which + k][index] = new[k]

    for t in range(9):
        update(0, (0, t), reduced[0][:, t * nm : (t + 1) * nm], LEARN_RATE)
        update(0, (1, t), reduced[2][:, t * nm : (t + 1) * nm], LEARN_RATE)
        update(1, (t,), reduced[1][:, t * ng : (t + 1) * ng], LEARN_RATE)
        update(2, (t,), reduced[3][:, t * nm : (t + 1) * nm], LEARN_RATE)
        at = t // 3 * 128 + t % 3 * kc
        update(3, (t,), reduced[4][:, at : at + kc], LEARN_RATE)
    update(4, (slice(None),), small[0:4, :], SMALL_RATE)
    per = ng // nm
    for k in range(2):
        pieces = [small[4 + k * per + i : 5 + k * per + i, :] for i in range(per)]
        update(5, (slice(k, k + 1),), jnp.concatenate(pieces, axis=1), SMALL_RATE)
    at = 4 + 2 * per
    update(6, (slice(None),), small[at : at + 1, :kc], SMALL_RATE)


def run_update(nm, ng, kc, reduced, small, sums, states):
    args = list(reduced) + [small, sums] + list(states)
    shapes = [jax.ShapeDtypeStruct((1, 1), F32)] * 2
    shapes += [jax.ShapeDtypeStruct(s.shape, F32) for s in states]
    return pl.pallas_call(
        partial(update_kernel, nm, ng, kc),
        name="update",
        out_shape=shapes,
        in_specs=[pl.BlockSpec(memory_space=VMEM)] * len(args),
        out_specs=[pl.BlockSpec(memory_space=VMEM)] * len(shapes),
        compiler_params=pltpu.CompilerParams(vmem_limit_bytes=VMEM_LIMIT),
    )(*args)


def lanes_of_taps(weight):
    taps, depth, width = weight.shape
    return weight.transpose(1, 0, 2).reshape(depth, taps * width)


def class_lanes(weight):
    _, depth, width = weight.shape
    rows = weight.transpose(1, 0, 2).reshape(depth, 3, 3 * width)
    return jnp.pad(rows, ((0, 0), (0, 0), (0, 128 - 3 * width))).reshape(depth, 384)


def adam_update(weight, moment, square, gradient, rate):
    moment_new = BETA_ONE * moment + (1.0 - BETA_ONE) * gradient
    square_new = BETA_TWO * square + (1.0 - BETA_TWO) * gradient * gradient
    moment_hat = moment_new / (1.0 - BETA_ONE**STEP_TIME)
    square_hat = square_new / (1.0 - BETA_TWO**STEP_TIME)
    weight_new = weight - rate * (
        moment_hat / (jnp.sqrt(square_hat) + ADAM_EPS) + WEIGHT_DECAY * weight
    )
    return (weight_new, moment_new, square_new)


def body(
    mask_features,
    grid_features,
    instance_cells,
    instance_counts,
    instance_labels,
    instance_masks,
    *states,
):
    images = lax.axis_size("dp")
    data_index = lax.axis_index("dp")
    dims = line_lengths(images)
    mask_convs, grid_first, grid_second, class_conv = states[0:12:3]
    mask_norms, grid_norms, class_bias = states[12::3]
    _, high, wide, half = mask_features.shape
    grid = grid_features.shape[1]
    pad = -(-(grid + 1) // 16) * 16
    nm, ng, kc = mask_convs.shape[3], grid_first.shape[2], class_conv.shape[2]
    fused = grid_first.shape[1] % 16 == 0
    cfg = dict(
        dims=dims,
        images=images,
        mask_map=Map(high, wide, wide, 8, 4, nm, 2 * nm // GROUPS),
        grid_map=Map(grid, pad, grid, grid // 2, grid // 2, ng, 2 * ng // GROUPS),
        kc=kc,
        fused=fused,
    )
    inputs = dict(
        xm_own=mask_features,
        xg_own=grid_features,
        masks=instance_masks,
        counts=instance_counts,
        cells=instance_cells,
        labels=instance_labels,
        mask_norms=mask_norms,
        grid_norms=grid_norms,
        class_bias=class_bias[None, :],
    )
    if fused:
        weights = dict(
            mask_convs=mask_convs,
            grid_first=grid_first,
            grid_second=grid_second,
            class_conv=class_conv,
        )
        blocks = [
            dims + (mask_convs.shape[2], 9 * nm),
            dims + (grid_first.shape[1], 9 * ng),
            dims + (mask_convs.shape[2], 9 * nm),
            dims + (grid_second.shape[1], 9 * nm),
            dims + (class_conv.shape[1], 384),
        ]
        out = run_step(cfg, inputs, weights, blocks)
        reduced = [out["out%d" % i] for i in range(5)]
        sums = out["sum_out"]
    else:
        shards = [
            lanes_of_taps(mask_convs[0].astype(BF16)),
            lanes_of_taps(grid_first.astype(BF16)),
            lanes_of_taps(mask_convs[1].astype(BF16)),
            lanes_of_taps(grid_second.astype(BF16)),
            class_lanes(class_conv.astype(BF16)),
        ]
        gathered = gather_all(dims, shards)
        weights = {"w%d" % i: b.reshape(-1, b.shape[-1]) for i, b in enumerate(gathered)}
        out = run_step(cfg, inputs, weights, None)
        reduced = reduce_all(
            dims, [out["g%d" % i].reshape(b.shape) for i, b in enumerate(gathered)]
        )
        squares = sum(jnp.sum(jnp.square(value)) for value in reduced)
        squares += (data_index == 0).astype(F32) * jnp.sum(jnp.square(out["small_out"]))
        pair = lax.psum((squares, out["sum_out"][0, 0]), ("dp", "mp"))
        sums = jnp.broadcast_to(jnp.pad(jnp.stack(pair), (0, 6))[:, None], (8, 128))
    states = states[:18] + tuple(state[None, :] for state in states[18:])
    result = run_update(nm, ng, kc, reduced, out["small_out"], sums, states)
    result = [value.reshape(()) for value in result[:2]] + list(result[2:])
    return tuple(result[:20]) + tuple(value[0] for value in result[20:])


def solution(mesh):
    in_specs = (
        P("dp", None, None, "mp"),
        P("dp", None, None, "mp"),
        P("dp", None),
        P(),
        P("dp", None),
        P("dp", None, None),
        P(None, None, "dp", "mp"),
        P(None, None, "dp", "mp"),
        P(None, None, "dp", "mp"),
        P(None, "dp", "mp"),
        P(None, "dp", "mp"),
        P(None, "dp", "mp"),
        P(None, "dp", "mp"),
        P(None, "dp", "mp"),
        P(None, "dp", "mp"),
        P(None, "dp", "mp"),
        P(None, "dp", "mp"),
        P(None, "dp", "mp"),
        P(None, "mp"),
        P(None, "mp"),
        P(None, "mp"),
        P(None, "mp"),
        P(None, "mp"),
        P(None, "mp"),
        P("mp"),
        P("mp"),
        P("mp"),
    )
    out_specs = (
        P(),
        P(),
        P(None, None, "dp", "mp"),
        P(None, None, "dp", "mp"),
        P(None, None, "dp", "mp"),
        P(None, "dp", "mp"),
        P(None, "dp", "mp"),
        P(None, "dp", "mp"),
        P(None, "dp", "mp"),
        P(None, "dp", "mp"),
        P(None, "dp", "mp"),
        P(None, "dp", "mp"),
        P(None, "dp", "mp"),
        P(None, "dp", "mp"),
        P(None, "mp"),
        P(None, "mp"),
        P(None, "mp"),
        P(None, "mp"),
        P(None, "mp"),
        P(None, "mp"),
        P("mp"),
        P("mp"),
        P("mp"),
    )
    return jax.shard_map(body, mesh=mesh, in_specs=in_specs, out_specs=out_specs, check_vma=False)
```

```python
from functools import partial

import jax
import jax.numpy as jnp
from jax import lax
from jax.experimental import pallas as pl
from jax.experimental.pallas import tpu as pltpu
from jax.sharding import PartitionSpec as P

GROUPS = 32
GN_EPS = 1e-05
CLIP_LIMIT = 0.02
LEARN_RATE = 0.02
SMALL_RATE = 0.5
BETA_ONE = 0.9
BETA_TWO = 0.95
ADAM_EPS = 1e-08
WEIGHT_DECAY = 0.05
CONTRAST_TEMP = 0.05
FOCAL_ALPHA = 0.25
DICE_WEIGHT = 3.0
STEP_TIME = 10.0
HIGHEST = lax.Precision.HIGHEST

MESH = pl.DeviceIdType.MESH
VMEM = pltpu.VMEM
ANY = pl.ANY
VMEM_LIMIT = 67043328
F32 = jnp.float32
BF16 = jnp.bfloat16
I32 = jnp.int32
SLOTS = 128
DMA = pltpu.SemaphoreType.DMA


def line_lengths(total):
    if total & (total - 1):
        return (total, 1, 1)
    bits = total.bit_length() - 1
    last = bits // 3
    middle = (bits - last) // 2
    return (1 << (bits - last - middle), 1 << middle, 1 << last)


def place(dims):
    index = lax.axis_index("dp")
    return (index // (dims[1] * dims[2]), (index // dims[2]) % dims[1], index % dims[2])


def split_index(dims, index):
    return (
        index // (dims[1] * dims[2]),
        lax.rem(index // dims[2], dims[1]),
        lax.rem(index, dims[2]),
    )


def along(dims, axis, step):
    stride = (dims[1] * dims[2], dims[2], 1)[axis]
    return {"dp": lax.axis_index("dp") + step * stride}


def partner():
    return {"mp": 1 - lax.axis_index("mp")}


def ring_step(dims, pos, axis, offset):
    other = lax.rem(pos[axis] + offset, dims[axis])
    return along(dims, axis, other - pos[axis])


def plane_peers(dims, cores):
    pos = place(dims)
    model = lax.axis_index("mp")
    peers = []
    for y in range(dims[1]):
        for x in range(dims[2]):
            for core in range(2 if cores else 1):
                if y == x == core == 0:
                    continue
                at = (pos[0] * dims[1] + lax.rem(pos[1] + y, dims[1])) * dims[2]
                peer = {"dp": at + lax.rem(pos[2] + x, dims[2])}
                if core:
                    peer["mp"] = 1 - model
                peers.append(peer)
    return peers


def greet(dims):
    sem = pltpu.get_barrier_semaphore()
    pos = place(dims)
    peers = plane_peers(dims, True)
    peers += [ring_step(dims, pos, 0, offset) for offset in range(1, dims[0])]
    for peer in peers:
        pl.semaphore_signal(sem, inc=1, device_id=peer, device_id_type=MESH)
    pl.semaphore_wait(sem, len(peers))


GATHER_ORDERS = ((2, 1, 0), (0, 2, 1), (0, 1, 2))
REDUCE_ORDERS = tuple(tuple(reversed(order)) for order in GATHER_ORDERS)


def line_copies(dims):
    return sum(n - 1 for n in dims)


def lane_cuts(width):
    tiles = width // 128
    if width % 128 or tiles < 3:
        return ((0, 0, width),)
    first = max(1, round(tiles * 0.1))
    second = (tiles - first) // 2
    sizes = (first, second, tiles - first - second)
    cuts, start = [], 0
    for order, size in enumerate(sizes):
        cuts.append((order, start * 128, size * 128))
        start += size
    return tuple(cuts)


def tap_row_cuts(width):
    third = width // 3
    if third % 384:
        return lane_cuts(width)
    near = third // 384 * 128
    return ((2, 0, third), (1, third, third), (1, 2 * third, near), (2, 2 * third + near, 2 * near))


class Exchange:
    def __init__(self):
        self.stages, self.lands, self.next = [], [], 0

    def finish(self):
        if 0 < self.next <= len(self.stages):
            for copy in self.stages[self.next - 1]:
                copy.wait_recv()
            self.lands[self.next - 1]()

    def start(self):
        if self.next < len(self.stages):
            for copy in self.stages[self.next]:
                copy.start()
        self.next += 1

    def drain(self):
        for stage in self.stages:
            for copy in stage:
                copy.wait_send()


def advance(*exchanges):
    for exchange in exchanges:
        exchange.finish()
    for exchange in exchanges:
        exchange.start()


def complete(*exchanges):
    while any(e.next <= len(e.stages) for e in exchanges):
        advance(*exchanges)


def nothing():
    return None


def gather_exchange(dims, out, send_sems, recv_sems, base, lanes, order, tail=None):
    pos = place(dims)
    result, done = Exchange(), set()
    tail = (slice(None), lanes) if tail is None else tail
    for axis in order:
        view = out.at[tuple(pl.ds(0, dims[k]) if k in done else pos[k] for k in range(3)) + tail]
        copies = []
        for offset in range(1, dims[axis]):
            copies.append(
                pltpu.make_async_remote_copy(
                    src_ref=view,
                    dst_ref=view,
                    send_sem=send_sems.at[base],
                    recv_sem=recv_sems.at[base],
                    device_id=ring_step(dims, pos, axis, offset),
                    device_id_type=MESH,
                )
            )
            base += 1
        if copies:
            result.stages.append(copies)
            result.lands.append(nothing)
        done.add(axis)
    return result


def remote(view, send_sem, recv_sem, device):
    return pltpu.make_async_remote_copy(
        src_ref=view,
        dst_ref=view,
        send_sem=send_sem,
        recv_sem=recv_sem,
        device_id=device,
        device_id_type=MESH,
    )


def core_exchange(out, sems):
    result = Exchange()
    view = out.at[:, :, :, lax.axis_index("mp")]
    result.stages.append([remote(view, sems.at[0], sems.at[1], partner())])
    result.lands.append(nothing)
    return result


def plane_slots(dims):
    return 2 * dims[1] * dims[2] + dims[0]


def plane_sems(dims):
    return [DMA((plane_slots(dims),)), DMA((plane_slots(dims),))]


def plane_exchange(dims, view, line_view, cores, land, send_sems, recv_sems):
    result, pos = Exchange(), place(dims)
    first = [
        remote(view, send_sems.at[i], recv_sems.at[i], peer)
        for i, peer in enumerate(plane_peers(dims, cores))
    ]
    base = len(first)
    second = [
        remote(
            line_view,
            send_sems.at[base + offset - 1],
            recv_sems.at[base + offset - 1],
            ring_step(dims, pos, 0, offset),
        )
        for offset in range(1, dims[0])
    ]
    result.stages, result.lands = [first, second], [land, nothing]
    return result


def landing_shapes(dims, rows, width, order):
    shapes, left = [], {0, 1, 2}
    for axis in order:
        left = left - {axis}
        shapes.append(
            (max(1, dims[axis] - 1),) + tuple(dims[k] for k in sorted(left)) + (rows, width)
        )
    return shapes


def reduce_exchange(dims, total, staged, lands, send_sems, recv_sems, base, lanes, order):
    pos = place(dims)
    result, reduced = Exchange(), set()
    for stage, axis in enumerate(order):
        n = dims[axis]
        free = [k for k in range(3) if k not in reduced and k != axis]

        def view(block, lead=None, axis=axis, reduced=frozenset(reduced)):
            lead = iter(lead) if lead is not None else None
            index = []
            for k in range(3):
                if k == axis:
                    index.append(block)
                elif k in reduced:
                    index.append(pos[k])
                else:
                    index.append(pl.ds(0, dims[k]) if lead is None else next(lead))
            return tuple(index) + (slice(None), lanes)

        copies = []
        for offset in range(1, n):
            copies.append(
                pltpu.make_async_remote_copy(
                    src_ref=staged.at[view(lax.rem(pos[axis] + offset, n))],
                    dst_ref=lands[stage].at[offset - 1],
                    send_sem=send_sems.at[base],
                    recv_sem=recv_sems.at[base],
                    device_id=ring_step(dims, pos, axis, offset),
                    device_id_type=MESH,
                )
            )
            base += 1

        def land(stage=stage, axis=axis, n=n, free=free, view=view):
            sizes = [dims[k] for k in free]
            blocks = 1
            for size in sizes:
                blocks *= size

            def add(i, carry):
                lead, rest = [], i
                for size in reversed(sizes):
                    lead.append(lax.rem(rest, size))
                    rest = rest // size
                lead = lead[::-1]
                index = view(pos[axis], lead)
                value = total[index]
                for k in range(n - 1):
                    value = value + lands[stage][(k,) + tuple(lead)].astype(F32)
                total[index] = value
                if sizes:
                    staged[index] = value.astype(BF16)
                return carry

            if blocks == 1:
                add(jnp.int32(0), 0)
            else:
                lax.fori_loop(0, blocks, add, 0)

        if copies:
            result.stages.append(copies)
            result.lands.append(land)
        reduced.add(axis)
    return result


def share_sems(dims, pieces):
    return [DMA((pieces * line_copies(dims),)), DMA((pieces * line_copies(dims),))]


def pair_copy(source, target, sems):
    return pltpu.make_async_remote_copy(
        src_ref=source,
        dst_ref=target,
        send_sem=sems.at[0],
        recv_sem=sems.at[1],
        device_id=partner(),
        device_id_type=MESH,
    )


def params(collective_id):
    return pltpu.CompilerParams(
        collective_id=collective_id, has_side_effects=True, vmem_limit_bytes=VMEM_LIMIT
    )


def gather_groups(dims, outs, send_sems, recv_sems):
    groups, base = [], 0
    for out in outs:
        group = []
        for order, start, size in lane_cuts(out.shape[4]):
            group.append(
                gather_exchange(
                    dims, out, send_sems, recv_sems, base, pl.ds(start, size), GATHER_ORDERS[order]
                )
            )
            base += line_copies(dims)
        groups.append(group)
    return groups


def reduce_groups(dims, totals, staged, lands, send_sems, recv_sems, cuts):
    groups, base, lands = [], 0, list(lands)
    for total, stage, cut in zip(totals, staged, cuts):
        group = []
        for order, start, size in cut:
            group.append(
                reduce_exchange(
                    dims,
                    total,
                    stage,
                    lands[:3],
                    send_sems,
                    recv_sems,
                    base,
                    pl.ds(start, size),
                    REDUCE_ORDERS[order],
                )
            )
            lands = lands[3:]
            base += line_copies(dims)
        groups.append(group)
    return groups


def flow_slots(dims, cuts):
    return max(1, line_copies(dims) * sum(len(cut) for cut in cuts))


def landing_scratch(dims, shapes, cuts):
    scratch = []
    for shape, cut in zip(shapes, cuts):
        for order, _, size in cut:
            for land in landing_shapes(dims, shape[-2], size, REDUCE_ORDERS[order]):
                scratch.append(VMEM(land, BF16))
    return scratch


def cast_blocks(dims, total, staged, lanes=slice(None)):
    def cast(j, carry):
        index = split_index(dims, j) + (slice(None), lanes)
        staged[index] = total[index].astype(BF16)
        return carry

    lax.fori_loop(0, dims[0] * dims[1] * dims[2], cast, 0)


def run_all(groups):
    exchanges = [exchange for group in groups for exchange in group]
    complete(*exchanges)
    for exchange in exchanges:
        exchange.drain()


def gather_kernel(dims, count, *refs):
    shards, outs = refs[:count], refs[count : 2 * count]
    send_sems, recv_sems, local_sems = refs[2 * count :]
    pos = place(dims)
    local = [
        pltpu.make_async_copy(shards[i], outs[i].at[pos[0], pos[1], pos[2]], local_sems.at[i])
        for i in range(count)
    ]
    for copy in local:
        copy.start()
    greet(dims)
    for copy in local:
        copy.wait()
    run_all(gather_groups(dims, outs, send_sems, recv_sems))


def gather_all(dims, shards):
    count = len(shards)
    shapes = [dims + s.shape for s in shards]
    slots = flow_slots(dims, [lane_cuts(s[-1]) for s in shapes])
    return pl.pallas_call(
        partial(gather_kernel, dims, count),
        name="gather_weights",
        out_shape=[jax.ShapeDtypeStruct(s, BF16) for s in shapes],
        in_specs=[pl.BlockSpec(memory_space=VMEM)] * count,
        out_specs=[pl.BlockSpec(memory_space=VMEM)] * count,
        scratch_shapes=[DMA((slots,)), DMA((slots,)), DMA((count,))],
        compiler_params=params(1),
    )(*shards)


def reduce_kernel(dims, count, *refs):
    parts, outs = refs[:count], refs[count : 2 * count]
    send_sems, recv_sems, local_sems = refs[2 * count : 2 * count + 3]
    rest = list(refs[2 * count + 3 :])
    totals, staged, lands = rest[:count], rest[count : 2 * count], rest[2 * count :]
    pos = place(dims)
    local = [pltpu.make_async_copy(parts[i], totals[i], local_sems.at[i]) for i in range(count)]
    for copy in local:
        copy.start()
    greet(dims)
    for i in range(count):
        local[i].wait()
        cast_blocks(dims, totals[i], staged[i])
    cuts = [lane_cuts(total.shape[4]) for total in totals]
    run_all(reduce_groups(dims, totals, staged, lands, send_sems, recv_sems, cuts))
    for i in range(count):
        outs[i][...] = totals[i][pos[0], pos[1], pos[2]]


def reduce_all(dims, parts):
    count = len(parts)
    shapes = [p.shape for p in parts]
    cuts = [lane_cuts(s[-1]) for s in shapes]
    slots = flow_slots(dims, cuts)
    scratch = [DMA((slots,)), DMA((slots,)), DMA((count,))]
    scratch += [VMEM(s, F32) for s in shapes] + [VMEM(s, BF16) for s in shapes]
    scratch += landing_scratch(dims, shapes, cuts)
    return pl.pallas_call(
        partial(reduce_kernel, dims, count),
        name="reduce_gradients",
        out_shape=[jax.ShapeDtypeStruct(s[3:], F32) for s in shapes],
        in_specs=[pl.BlockSpec(memory_space=ANY)] * count,
        out_specs=[pl.BlockSpec(memory_space=VMEM)] * count,
        scratch_shapes=scratch,
        compiler_params=params(2),
    )(*parts)


def group_sums(row, spread):
    width = row.shape[1]
    return lax.dot_general(
        jnp.broadcast_to(row, (8, width)),
        spread,
        (((1,), (0,)), ((), ())),
        precision=HIGHEST,
        preferred_element_type=F32,
    )[0:1]


def group_spread(width, group):
    rows = lax.broadcasted_iota(I32, (width, width), 0) // group
    cols = lax.broadcasted_iota(I32, (width, width), 1) // group
    return (rows == cols).astype(F32)


def dot(a, b, contract):
    return lax.dot_general(a, b, ((contract[0], contract[1]), ((), ())), preferred_element_type=F32)


NN = ((1,), (0,))
NT = ((1,), (1,))
TN = ((0,), (0,))


class Map:
    def __init__(self, high, width, live, span, part, channels, group):
        self.high, self.width, self.live = high, width, live
        self.span, self.part, self.channels = span, part, channels
        self.pixels = float(high * live * group)

    def column(self, span):
        shape = (span, self.width, self.channels)
        return lax.broadcasted_iota(I32, shape, 1).reshape(span * self.width, self.channels)

    def masked(self, value, span):
        if self.live == self.width:
            return value
        return jnp.where(self.column(span) < self.live, value, 0.0)

    def at(self, i, span):
        return pl.ds(pl.multiple_of(i * span * self.width, 16), span * self.width)


def take(source, first, count, lanes=slice(None)):
    value = source[pl.ds(first, count), :, lanes]
    return value.reshape(-1, value.shape[2])


def conv_forward(m, source, weight, raw, first=0, last=None, total=None):
    n, tile = m.channels, m.span * m.width

    def body(i, total):
        wide = None
        for du in range(3):
            part = dot(take(source, i * m.span + du, m.span), weight(du), NN)
            wide = part if wide is None else wide + part
        left = pltpu.roll(wide[:, :n], 1, 0)
        right = pltpu.roll(wide[:, 2 * n :], tile - 1, 0)
        if m.live == m.width:
            column = m.column(m.span)
            left = jnp.where(column == 0, 0.0, left)
            right = jnp.where(column == m.width - 1, 0.0, right)
        value = m.masked(left + wide[:, n : 2 * n] + right, m.span)
        raw[m.at(i, m.span), :] = value
        return total + jnp.sum(value, axis=0, keepdims=True)

    last = m.high // m.span if last is None else last
    total = jnp.zeros((1, n), F32) if total is None else total
    return lax.fori_loop(first, last, body, total)


def norm_forward(m, raw, total, spread, gain, bias, store):
    n, part = m.channels, m.part
    mean = group_sums(total, spread) / m.pixels

    def spread_of(i, acc):
        away = m.masked(raw[m.at(i, part), :] - mean, part)
        return acc + jnp.sum(away * away, axis=0, keepdims=True)

    squares = lax.fori_loop(0, m.high // part, spread_of, jnp.zeros((1, n), F32))
    scale = lax.rsqrt(group_sums(squares, spread) / m.pixels + GN_EPS)

    def normalize(i, carry):
        normed = (raw[m.at(i, part), :] - mean) * scale
        raw[m.at(i, part), :] = normed
        value = m.masked(jnp.maximum(normed * gain + bias, 0.0), part)
        store(i, value.astype(BF16))
        return carry

    lax.fori_loop(0, m.high // part, normalize, 0)
    return scale


def norm_backward(m, normed, upstream, spare, shifted, spread, gain, bias, scale):
    n, part = m.channels, m.part
    tile = part * m.width

    def first(i, sums):
        here = normed[m.at(i, part), :]
        value = m.masked(jnp.where(here * gain + bias > 0.0, upstream(i), 0.0), part)
        spare[m.at(i, part), :] = value
        return (
            sums[0] + jnp.sum(value * here, axis=0, keepdims=True),
            sums[1] + jnp.sum(value, axis=0, keepdims=True),
        )

    zero = jnp.zeros((1, n), F32)
    gain_sum, bias_sum = lax.fori_loop(0, m.high // part, first, (zero, zero))
    level = group_sums(bias_sum * gain, spread) / m.pixels
    slope = group_sums(gain_sum * gain, spread) / m.pixels

    def second(i, carry):
        value = scale * (spare[m.at(i, part), :] * gain - level - normed[m.at(i, part), :] * slope)
        value = m.masked(value, part)
        left = pltpu.roll(value, tile - 1, 0)
        right = pltpu.roll(value, 1, 0)
        if m.live == m.width:
            column = m.column(part)
            left = jnp.where(column == m.width - 1, 0.0, left)
            right = jnp.where(column == 0, 0.0, right)
        into = pl.ds(i * part + 1, part)
        for k, piece in enumerate((left, value, right)):
            shifted[into, :, k * n : (k + 1) * n] = piece.astype(BF16).reshape(part, m.width, n)
        return carry

    lax.fori_loop(0, m.high // part, second, 0)
    return gain_sum, bias_sum


def weight_gradient(m, source, shifted, total, lanes, each=None):
    width = lanes.stop - lanes.start
    for du in range(3):
        value = dot(take(source, du, m.high), take(shifted, 1, m.high, lanes), TN)
        into = total.at[..., du * width : (du + 1) * width]
        into[...] = value.reshape(into.shape)
        if each is not None:
            each(du)


def zero_edges(ref):
    blank = jnp.zeros((1,) + ref.shape[1:], ref.dtype)
    ref[0:1] = blank
    ref[ref.shape[0] - 1 : ref.shape[0]] = blank


def diagonal(n):
    return lax.broadcasted_iota(I32, (n, n), 0) == lax.broadcasted_iota(I32, (n, n), 1)


def as_row(column):
    return jnp.sum(jnp.where(diagonal(column.shape[0]), column, 0.0), axis=0, keepdims=True)


def as_column(row):
    return jnp.sum(jnp.where(diagonal(row.shape[1]), row, 0.0), axis=1, keepdims=True)


def step_kernel(cfg, names, *refs):
    r = dict(zip(names, refs))
    dims, images, fused = cfg["dims"], cfg["images"], cfg["fused"]
    big, small = cfg["mask_map"], cfg["grid_map"]
    nm, ng, kc = big.channels, small.channels, cfg["kc"]
    grid, pad = small.live, small.width
    rows, grid_rows = big.high * big.width, small.high * small.width
    gtile = small.span * small.width
    pos = place(dims)
    model = lax.axis_index("mp")
    own_image = lax.axis_index("dp")

    def lanes_of(width, side):
        return pl.ds(pl.multiple_of(side * width, width), width)

    own_m, away_m = lanes_of(nm, model), lanes_of(nm, 1 - model)
    own_g, away_g = lanes_of(ng, model), lanes_of(ng, 1 - model)
    own_x = lanes_of(r["xm_own"].shape[3], model)
    map_rows, grid_span = pl.ds(1, big.high), pl.ds(1, small.high)
    spread_m = group_spread(nm, 2 * nm // GROUPS)
    spread_g = group_spread(ng, 2 * ng // GROUPS)

    xm, xg, hm, hg, dm = r["xm"], r["xg"], r["hm"], r["hg"], r["dm"]
    dg1, dg2 = r["dg1"], r["dg2"]
    mask_in, grid_in = r["xm_own"].at[0], r["xg_own"].at[0]
    mask_into = xm.at[map_rows, :, own_x]
    grid_into = xg.at[grid_span, pl.ds(0, grid), own_x]
    local = [
        pltpu.make_async_copy(mask_in, mask_into, r["local"].at[0]),
        pltpu.make_async_copy(grid_in, grid_into, r["local"].at[1]),
    ]
    masks = r["mask_bits"]
    mask_copy = pltpu.make_async_copy(r["masks"].at[:, 0, :], masks, r["local"].at[2])
    for copy in local:
        copy.start()
    mask_copy.start()
    weights = [r["w%d" % i] for i in range(5)]
    groups = []
    if fused:
        for t in range(9):
            for i, value in (
                (0, r["mask_convs"][0, t]),
                (1, r["grid_first"][t]),
                (2, r["mask_convs"][1, t]),
                (3, r["grid_second"][t]),
            ):
                width = value.shape[1]
                weights[i][pos[0], pos[1], pos[2], :, t * width : (t + 1) * width] = value.astype(
                    BF16
                )
        class_in = r["class_conv"]
        for du in range(3):
            pieces = [class_in[3 * du + dv] for dv in range(3)]
            pieces.append(jnp.zeros((class_in.shape[1], 128 - 3 * kc), F32))
            weights[4][pos[0], pos[1], pos[2], :, du * 128 : (du + 1) * 128] = jnp.concatenate(
                pieces, axis=1
            ).astype(BF16)
        groups = gather_groups(dims, weights, r["gs"], r["gr"])

    def bring(*which):
        if fused:
            advance(*[exchange for i in which for exchange in groups[i]])

    greet(dims)
    feature_copies = [
        pair_copy(mask_in, mask_into, r["pair"].at[0]),
        pair_copy(grid_in, grid_into, r["pair"].at[1]),
    ]
    for copy in feature_copies:
        copy.start()
    bring(0)
    bring(1)

    for ref in (xm, xg, hm, hg, dm, dg1, dg2):
        zero_edges(ref)
    xg[:, grid:, :] = jnp.zeros((xg.shape[0], pad - grid, xg.shape[2]), BF16)
    share = jnp.float32(1.0 / images)
    table, bias_table = r["table"], r["bias_table"]
    slots = r["cells"].shape[1]
    table[...] = jnp.full(table.shape, -(1 << 20), I32)
    table[0:1, 0:slots] = r["cells"][...]
    table[1:2, 0:slots] = r["labels"][...]
    bias_table[...] = jnp.zeros(bias_table.shape, F32)
    bias_table[0:1, 0:kc] = r["class_bias"][...]
    cells = table[0:1, :].astype(F32)
    cells = cells + jnp.floor((cells + 0.5) / grid) * (pad - grid)
    cells_row = cells.astype(I32)
    cells_col = as_column(cells).astype(I32)
    labels_col = as_column(table[1:2, :].astype(F32)).astype(I32) - model * kc
    class_bias = bias_table[0:1, :]
    own_count = r["counts"][own_image]
    slot_lanes = lax.broadcasted_iota(I32, (1, SLOTS), 1)
    slot_rows = lax.broadcasted_iota(I32, (SLOTS, 1), 0)
    own_float = jnp.full((1, 1), own_count, I32).astype(F32)
    live_row = (slot_lanes < own_count).astype(F32)
    live_col = (slot_rows < own_count).astype(F32)
    weight_col = live_col * (share / own_float)
    dice_col = DICE_WEIGHT * weight_col
    focal_scale = share / (own_float + 1.0)
    bring(0)
    bring(0)
    bring(1)

    def weight(i, span):
        def part(du):
            value = weights[i][..., du * span : (du + 1) * span]
            return value.reshape(-1, span) if fused else value

        return part

    mask_one, grid_one, mask_two = weight(0, 3 * nm), weight(1, 3 * ng), weight(2, 3 * nm)
    grid_two, class_two = weight(3, 3 * nm), weight(4, 128)

    norms, gnorms = r["mask_norms"], r["grid_norms"]
    row = lambda ref, k: ref[k : k + 1, :]
    bring(2)
    for copy in local:
        copy.wait()
    feature_copies[0].wait()
    bring(0)
    xh1 = r["xh1"]
    total = conv_forward(big, xm, mask_one, xh1)
    bring(1)
    bring(2)
    bring(4)
    bring(3)

    def keep_mask(i, value):
        hm[pl.ds(i * big.part + 1, big.part), :, own_m] = value.reshape(big.part, big.width, nm)

    scale_one = norm_forward(big, xh1, total, spread_m, row(norms, 0), row(norms, 1), keep_mask)
    hm_copy = pair_copy(
        hm.at[map_rows, :, own_m], hm.at[map_rows, :, own_m], r["pair"].at[2]
    )
    hm_copy.start()
    feature_copies[1].wait()
    bring(1)
    xhg = r["xhg"]
    total = conv_forward(small, xg, grid_one, xhg, 0, 1)
    bring(2)
    bring(4)
    bring(3)
    total = conv_forward(small, xg, grid_one, xhg, 1, None, total)

    def keep_grid(i, value):
        hg[pl.ds(i * small.part + 1, small.part), :, own_g] = value.reshape(
            small.part, small.width, ng
        )

    scale_grid = norm_forward(
        small, xhg, total, spread_g, row(gnorms, 0), row(gnorms, 1), keep_grid
    )
    hg_copy = pair_copy(
        hg.at[grid_span, :, own_g], hg.at[grid_span, :, own_g], r["pair"].at[3]
    )
    hg_copy.start()

    hm_copy.wait()
    bring(2)
    xh2, feature = r["xh2"], r["feature"]
    half = big.high // big.span // 2
    total = conv_forward(big, hm, mask_two, xh2, 0, half)
    bring(4)
    bring(3)
    total = conv_forward(big, hm, mask_two, xh2, half, None, total)

    def keep_feature(i, value):
        feature[big.at(i, big.part), :] = value

    scale_two = norm_forward(
        big, xh2, total, spread_m, row(norms, 2), row(norms, 3), keep_feature
    )

    hg_copy.wait()
    patches = r["patches"]
    lane = lax.broadcasted_iota(I32, (SLOTS, grid_rows), 1)
    depth = hg.shape[2]
    for t in range(9):
        chosen = (lane == cells_col + ((t // 3 - 1) * pad + t % 3 - 1)).astype(F32).astype(BF16)
        patches[:, t * depth : (t + 1) * depth] = dot(
            chosen, take(hg, 1, small.high), NN
        ).astype(BF16)
    if fused:
        complete(*groups[4])

    class_hot = (
        (lax.broadcasted_iota(I32, (SLOTS, 128), 1) == labels_col).astype(F32).astype(BF16)
    )

    def class_tile(i, sums):
        value = None
        for du in range(3):
            part = dot(take(hg, i * small.span + du, small.span), class_two(du), NN)
            value = part if value is None else value + part
        x = (
            pltpu.roll(value, 1, 0)
            + pltpu.roll(value, 128 - kc, 1)
            + pltpu.roll(pltpu.roll(value, 128 - 2 * kc, 1), gtile - 1, 0)
            + class_bias
        )
        at = lax.broadcasted_iota(I32, (gtile, SLOTS), 0) + i * gtile
        cell_hot = jnp.where(at == cells_row, live_row, 0.0).astype(BF16)
        t = dot(cell_hot, class_hot, NN)
        lanes = lax.broadcasted_iota(I32, (gtile, 128), 1)
        column = lax.broadcasted_iota(I32, (small.span, pad, 128), 1).reshape(gtile, 128)
        real = (column < grid) & (lanes < kc)
        tiny = jnp.exp(-jnp.abs(x))
        extra = jnp.log1p(tiny)
        inverse = 1.0 / (1.0 + tiny)
        q = jnp.where(x >= 0.0, 1.0, tiny) * inverse
        p = jnp.where(x >= 0.0, tiny, 1.0) * inverse
        log_q = -(jnp.maximum(-x, 0.0) + extra)
        log_p = -(jnp.maximum(x, 0.0) + extra)
        terms = FOCAL_ALPHA * t * p * p * log_q + (1.0 - FOCAL_ALPHA) * (1.0 - t) * q * q * log_p
        slope = FOCAL_ALPHA * t * p * p * (p - 2.0 * q * log_q) + (1.0 - FOCAL_ALPHA) * (
            1.0 - t
        ) * q * q * (2.0 * p * log_p - q)
        slope = jnp.where(real, -focal_scale * slope, 0.0).astype(BF16).astype(F32)
        shifted = (
            pltpu.roll(slope, gtile - 1, 0)
            + pltpu.roll(slope, kc, 1)
            + pltpu.roll(pltpu.roll(slope, 2 * kc, 1), 1, 0)
        )
        dg2[pl.ds(i * small.span + 1, small.span), :, 3 * nm :] = shifted.astype(BF16).reshape(
            small.span, pad, 128
        )
        return (
            sums[0] + jnp.sum(jnp.where(real, -focal_scale * terms, 0.0), axis=0, keepdims=True),
            sums[1] + jnp.sum(slope, axis=0, keepdims=True),
        )

    zero = jnp.zeros((1, 128), F32)
    focal_sum, class_bias_sum = lax.fori_loop(
        0, small.high // small.span, class_tile, (zero, zero)
    )

    for group in groups:
        complete(*group)
        for exchange in group:
            exchange.drain()
    picked = None
    for t in range(9):
        w = grid_two(t // 3)[:, (t % 3) * nm : (t % 3 + 1) * nm]
        part = dot(patches[:, t * depth : (t + 1) * depth], w, NN)
        picked = part if picked is None else picked + part
    kernels = r["kernels"]
    kept = (slots + 15) // 16 * 16
    if kept < SLOTS:
        kernels[..., kept:, :] = jnp.zeros(dims + (2, SLOTS - kept, nm), BF16)
    kernels[pos[0], pos[1], pos[2], model, 0:kept] = picked[0:kept].astype(BF16)
    upper = kept // 32 * 16
    kernel_share = [
        gather_exchange(
            dims, kernels, r["ks"], r["kr"], i * line_copies(dims), None, order,
            (model, pl.ds(start, size)),
        )
        for i, (order, start, size) in enumerate(
            ((GATHER_ORDERS[1], 0, upper), (GATHER_ORDERS[2], upper, kept - upper))
        )
    ]
    kernel_cores = core_exchange(kernels, r["pair"].at[7])
    advance(*kernel_share)

    kernel_rows = kernels[pos[0], pos[1], pos[2], model]
    logits, logits_in = r["logits"], r["logits_in"]
    high_slots = logits.shape[0]
    tile = big.span * big.width
    for i in range(rows // tile):
        span = slice(i * tile, (i + 1) * tile)
        logits[:, span] = dot(kernel_rows[:high_slots], feature[span, :], NT).astype(BF16)
    logits_copy = pair_copy(logits, logits_in, r["pair"].at[4])
    logits_copy.start()
    advance(*kernel_share)

    logits_copy.wait()
    mask_copy.wait()
    dice_sum = jnp.zeros((1, 1), F32)
    for start in range(0, slots, 16):
        span = slice(start, start + 16)
        x = logits[span, :].astype(F32) + logits_in[span, :].astype(F32)
        s = jax.nn.sigmoid(x)
        mask = masks[start : min(start + 16, slots), :].astype(F32)
        if mask.shape[0] < 16:
            mask = jnp.concatenate([mask, jnp.zeros((16 - mask.shape[0], rows), F32)], axis=0)
        inter = jnp.sum(s * mask, axis=1, keepdims=True)
        whole = jnp.sum(s * s, axis=1, keepdims=True) + jnp.sum(mask, axis=1, keepdims=True) + 1.0
        share_here = dice_col[span]
        dice_sum += jnp.sum(share_here * (1.0 - 2.0 * inter / whole), keepdims=True)
        a = -2.0 * share_here / whole
        b = 2.0 * share_here * inter / (whole * whole)
        logits[span, :] = ((a * mask + 2.0 * b * s) * s * (1.0 - s)).astype(BF16)
    advance(*kernel_share)

    several = 4 if images % 4 == 0 else 1

    def key_block(d):
        index = split_index(dims, d)
        return [kernels[index[0], index[1], index[2], k] for k in range(2)]

    def squares_of(block):
        return sum(
            jnp.sum(jnp.square(part.astype(F32)), axis=1, keepdims=True) for part in block
        )

    same_slot = diagonal(SLOTS)

    def scores(d, own_scale):
        block = key_block(d)
        raw = dot(own_full[0], block[0], NT) + dot(own_full[1], block[1], NT)
        key_scale = lax.rsqrt(as_row(squares_of(block)) + 1e-06)
        scale = own_scale * key_scale / CONTRAST_TEMP
        live = slot_lanes < r["counts"][d]
        allowed = live & jnp.logical_not(same_slot & (d == own_image))
        return block, raw, key_scale, scale, allowed

    def own_key_scale():
        return lax.rsqrt(squares_of(own_full) + 1e-06)

    totals = [r["g%d" % i] for i in range(5)]
    out_groups = []
    if fused:
        staged = [weights[2], weights[1], weights[0], weights[3], r["class_stage"]]
        lands = [r["land%d" % i] for i in range(cfg["lands"])]
        out_groups = reduce_groups(dims, totals, staged, lands, r["rs"], r["rr"], cfg["cuts"])

    def send(*which):
        if fused:
            advance(*[exchange for i in which for exchange in out_groups[i]])

    def send_first(i):
        if fused:
            cast_blocks(dims, totals[i], staged[i])
            send(i)

    def send_tap_row(du):
        if not fused:
            return
        third = 3 * nm
        cast_blocks(dims, totals[0], staged[0], slice(du * third, (du + 1) * third))
        for (_, start, _), exchange in zip(cfg["cuts"][0], out_groups[0]):
            if len(out_groups[0]) == 1 and du == 2 or start // third == du:
                advance(exchange)

    logit_rows = dot(logits[...], feature[...], NN)
    dlogits, part_rows = logits, big.part * big.width

    def from_logits(i):
        pixels = pl.ds(pl.multiple_of(i * part_rows, part_rows), part_rows)
        return dot(dlogits[:, pixels], kernel_rows[:high_slots], TN)

    gain_two, bias_two = norm_backward(
        big, xh2, from_logits, r["spare"], dm, spread_m, row(norms, 2), row(norms, 3), scale_two
    )
    complete(*kernel_share)
    advance(kernel_cores)
    weight_gradient(big, hm, dm, totals[2], slice(0, 3 * nm))
    send_first(2)
    complete(kernel_cores)
    own_full = [kernels[pos[0], pos[1], pos[2], k] for k in range(2)]
    own_scale = own_key_scale()

    def sum_keys(i, acc):
        for k in range(several):
            _, raw, _, scale, allowed = scores(i * several + k, own_scale)
            value = jnp.where(allowed, jnp.exp(raw * scale), 0.0)
            acc = acc + jnp.sum(value, axis=1, keepdims=True)
        return acc

    totals_col = lax.fori_loop(0, images // several, sum_keys, jnp.zeros((SLOTS, 1), F32))
    contrast_sum = jnp.sum(
        jnp.where(weight_col > 0.0, weight_col * jnp.log(totals_col), 0.0), keepdims=True
    )
    key_totals = r["key_totals"]
    key_totals[pos[0], pos[1], pos[2]] = jnp.broadcast_to(as_row(totals_col), (8, SLOTS))
    total_share = plane_exchange(
        dims,
        key_totals.at[pos[0], pos[1], pos[2]],
        key_totals.at[pos[0]],
        False,
        nothing,
        r["ls"],
        r["lr"],
    )
    advance(total_share)
    hidden = hm

    def input_tile(i, carry):
        value = None
        for du in range(3):
            part = dot(take(dm, i * big.span + 2 - du, big.span), mask_two(du), NT)
            value = part if value is None else value + part
        hidden[pl.ds(i * big.span + 1, big.span)] = value.astype(BF16).reshape(
            big.span, big.width, 2 * nm
        )
        return carry

    lax.fori_loop(0, big.high // big.span, input_tile, 0)
    hidden_copy = pair_copy(hidden.at[map_rows, :, away_m], r["dhm_in"], r["pair"].at[5])
    hidden_copy.start()
    advance(total_share)
    send(2)
    weight_gradient(small, hg, dg2, totals[4], slice(3 * nm, 3 * nm + 128))
    send_first(4)
    send(2)
    complete(total_share)

    own_scale = own_key_scale()
    query_weight = weight_col / totals_col

    def row_terms(i, acc):
        for k in range(several):
            d = i * several + k
            block, raw, key_scale, scale, allowed = scores(d, own_scale)
            index = split_index(dims, d)
            total_row = key_totals[index[0], index[1], index[2]][0:1]
            value = jnp.where(allowed, jnp.exp(raw * scale), 0.0)
            key_count = jnp.full((1, 1), r["counts"][d], I32).astype(F32)
            query = value * query_weight
            key = value * live_col * (share / key_count / total_row)
            query_low = (query * scale).astype(BF16)
            key_low = (key * scale).astype(BF16)
            mine = jnp.where(model == 0, block[0].astype(F32), block[1].astype(F32)).astype(BF16)
            acc = (
                acc[0] + dot(query_low, mine, NN) + dot(key_low, mine, NN),
                acc[1]
                + jnp.sum((query + key) * raw * key_scale / CONTRAST_TEMP, axis=1, keepdims=True),
            )
        return acc

    row_sum, scale_sum = lax.fori_loop(
        0, images // several, row_terms, (jnp.zeros((SLOTS, nm), F32), jnp.zeros((SLOTS, 1), F32))
    )
    norm_grad = -0.5 * own_scale * own_scale * own_scale * scale_sum
    row_grad = row_sum + 2.0 * kernel_rows.astype(F32) * norm_grad
    row_grad = row_grad + jnp.concatenate(
        [logit_rows, jnp.zeros((SLOTS - high_slots, nm), F32)], axis=0
    )
    row_low = row_grad.astype(BF16)

    for i in range(small.high // small.span):
        at = lax.broadcasted_iota(I32, (gtile, SLOTS), 0) + i * gtile
        for dv in range(3):
            chosen = (at == cells_row + (dv - 1)).astype(F32).astype(BF16)
            dg2[1 + i * small.span : 1 + (i + 1) * small.span, :, dv * nm : (dv + 1) * nm] = (
                dot(chosen, row_low, NN).astype(BF16).reshape(small.span, pad, nm)
            )
    hidden_grid = hg

    def grid_input_tile(i, carry):
        value = None
        for du in range(3):
            first = i * small.span + 2 - du
            part = dot(take(dg2, first, small.span, slice(0, 3 * nm)), grid_two(du), NT) + dot(
                take(dg2, first, small.span, slice(3 * nm, 3 * nm + 128)), class_two(du), NT
            )
            value = part if value is None else value + part
        hidden_grid[pl.ds(i * small.span + 1, small.span)] = value.astype(BF16).reshape(
            small.span, pad, 2 * ng
        )
        return carry

    lax.fori_loop(0, small.high // small.span, grid_input_tile, 0)
    hidden_grid_copy = pair_copy(
        hidden_grid.at[grid_span, :, away_g], r["dhg_in"], r["pair"].at[6]
    )
    hidden_grid_copy.start()
    for t in range(9):
        value = dot(patches[:, t * depth : (t + 1) * depth], row_low, TN)
        into = totals[3].at[..., t * nm : (t + 1) * nm]
        into[...] = value.reshape(into.shape)
    send_first(3)
    send(4)
    send(2)

    hidden_grid_copy.wait()
    hidden_grid_in = r["dhg_in"]

    def both_grid_halves(i):
        mine = take(hidden_grid, i * small.part + 1, small.part, own_g)
        return mine.astype(F32) + take(hidden_grid_in, i * small.part, small.part).astype(F32)

    gain_grid, bias_grid = norm_backward(
        small, xhg, both_grid_halves, r["spare_g"], dg1, spread_g, row(gnorms, 0),
        row(gnorms, 1), scale_grid,
    )
    weight_gradient(small, xg, dg1, totals[1], slice(0, 3 * ng))
    send_first(1)
    send(4)
    send(3)
    hidden_copy.wait()
    hidden_in = r["dhm_in"]

    def both_halves(i):
        mine = take(hidden, i * big.part + 1, big.part, own_m)
        return mine.astype(F32) + take(hidden_in, i * big.part, big.part).astype(F32)

    gain_one, bias_one = norm_backward(
        big, xh1, both_halves, r["spare"], dm, spread_m, row(norms, 0), row(norms, 1), scale_one
    )

    pieces = [gain_one, bias_one, gain_two, bias_two]
    pieces += [gain_grid[:, i : i + nm] for i in range(0, ng, nm)]
    pieces += [bias_grid[:, i : i + nm] for i in range(0, ng, nm)]
    pieces += [class_bias_sum]
    pieces += [jnp.zeros((1, 128), F32)] * (16 - len(pieces))
    small_plane, small_line = r["small_plane"], r["small_line"]
    small_plane[pos[1], pos[2]] = jnp.concatenate(pieces, axis=0)

    def plane_total(plane, cores):
        value = None
        for y in range(dims[1]):
            for x in range(dims[2]):
                for core in range(2) if cores else (None,):
                    part = plane[y, x] if core is None else plane[y, x, core]
                    value = part if value is None else value + part
        return value

    def line_total(line):
        value = line[0]
        for z in range(1, dims[0]):
            value = value + line[z]
        return value

    def small_sum_here():
        small_line[pos[0]] = plane_total(small_plane, False)

    small_share = plane_exchange(
        dims, small_plane.at[pos[1], pos[2]], small_line.at[pos[0]], False, small_sum_here,
        r["ss"], r["sr"],
    )
    advance(small_share)

    def each(du):
        send_tap_row(du)
        if du == 0:
            send(3)
            send(4)
        if du == 1:
            send(1)
            advance(small_share)

    weight_gradient(big, xm, dm, totals[0], slice(0, 3 * nm), each)
    send(3)
    send(1)
    complete(small_share)
    small_sum = line_total(small_line)
    r["small_out"][...] = small_sum
    first_model = (model == 0).astype(F32)
    loss = jnp.sum(focal_sum, keepdims=True) + first_model * (dice_sum + contrast_sum)
    if fused:
        squares = (own_image == 0).astype(F32) * jnp.sum(small_sum * small_sum, keepdims=True)

        def hand_out(i):
            complete(*out_groups[i])
            value = totals[i][pos[0], pos[1], pos[2]]
            r["out%d" % i][...] = value
            return jnp.sum(value * value, keepdims=True)

        squares += hand_out(2)
        squares += hand_out(4)
        send(0)
        squares += hand_out(3)
        send(0)
        squares += hand_out(1)
        squares += hand_out(0)
        sum_plane, sum_line = r["sum_plane"], r["sum_line"]
        at = lax.broadcasted_iota(I32, (8, 128), 0)
        sum_plane[pos[1], pos[2], model] = jnp.where(at == 0, squares, loss)

        def sums_here():
            sum_line[pos[0]] = plane_total(sum_plane, True)

        sum_share = plane_exchange(
            dims, sum_plane.at[pos[1], pos[2], model], sum_line.at[pos[0]], True, sums_here,
            r["us"], r["ur"],
        )
        complete(sum_share)
        r["sum_out"][...] = line_total(sum_line)
        sum_share.drain()
    else:
        r["sum_out"][...] = jnp.broadcast_to(loss, (8, 128))
    for shared in kernel_share + [kernel_cores, total_share, small_share]:
        shared.drain()
    for group in out_groups:
        for exchange in group:
            exchange.drain()


def run_step(cfg, inputs, weights, blocks):
    dims, fused = cfg["dims"], cfg["fused"]
    big, small = cfg["mask_map"], cfg["grid_map"]
    nm, ng = big.channels, small.channels
    rows, grid_rows = big.high * big.width, small.high * small.width
    inputs = dict(inputs, **weights)
    spaces = dict(xm_own=ANY, xg_own=ANY, masks=ANY, counts=pltpu.SMEM)
    names = list(inputs)
    specs = [pl.BlockSpec(memory_space=spaces.get(name, VMEM)) for name in names]
    outs = {"small_out": ((16, 128), F32), "sum_out": ((8, 128), F32)}
    scratch = {}
    if fused:
        for i, shape in enumerate(blocks):
            outs["out%d" % i] = (shape[3:], F32)
            scratch["w%d" % i] = VMEM(shape, BF16)
            scratch["g%d" % i] = VMEM(shape, F32)
        gather_cuts = [lane_cuts(shape[-1]) for shape in blocks]
        cuts = [tap_row_cuts(blocks[0][-1])] + gather_cuts[1:]
        lands = landing_scratch(dims, blocks, cuts)
        cfg = dict(cfg, lands=len(lands), cuts=cuts)
        for i, land in enumerate(lands):
            scratch["land%d" % i] = land
        for names_of, used in ((("gs", "gr"), gather_cuts), (("rs", "rr"), cuts)):
            for name in names_of:
                scratch[name] = DMA((flow_slots(dims, used),))
        scratch["class_stage"] = VMEM(blocks[4], BF16)
        scratch["sum_plane"] = VMEM(dims[1:] + (2, 8, 128), F32)
        scratch["sum_line"] = VMEM(dims[:1] + (8, 128), F32)
        scratch["us"], scratch["ur"] = plane_sems(dims)
    else:
        for i in range(5):
            outs["g%d" % i] = (inputs["w%d" % i].shape, F32)
    c_in = 2 * inputs["xm_own"].shape[3]
    depth = 2 * ng
    slot_rows = -(-inputs["masks"].shape[0] // 16) * 16

    def padded(m, channels):
        return VMEM((m.high + 2, m.width, channels), BF16)

    scratch.update(
        xm=padded(big, c_in),
        xg=padded(small, c_in),
        xh1=VMEM((rows, nm), F32),
        hm=padded(big, 2 * nm),
        xhg=VMEM((grid_rows, ng), F32),
        hg=padded(small, depth),
        xh2=VMEM((rows, nm), F32),
        feature=VMEM((rows, nm), BF16),
        patches=VMEM((SLOTS, 9 * depth), BF16),
        kernels=VMEM(dims + (2, SLOTS, nm), BF16),
        logits=VMEM((slot_rows, rows), BF16),
        logits_in=VMEM((slot_rows, rows), BF16),
        key_totals=VMEM(dims + (8, SLOTS), F32),
        dm=padded(big, 3 * nm),
        spare=VMEM((rows, nm), F32),
        dhm_in=VMEM((big.high, big.width, nm), BF16),
        dg2=padded(small, 3 * nm + 128),
        dhg_in=VMEM((small.high, small.width, ng), BF16),
        dg1=padded(small, 3 * ng),
        spare_g=VMEM((grid_rows, ng), F32),
        small_plane=VMEM(dims[1:] + (16, 128), F32),
        small_line=VMEM(dims[:1] + (16, 128), F32),
        table=VMEM((8, SLOTS), I32),
        bias_table=VMEM((8, 128), F32),
        local=DMA((3,)),
        mask_bits=VMEM((inputs["masks"].shape[0], rows), I32),
        pair=DMA((8, 2)),
    )
    scratch["ks"], scratch["kr"] = share_sems(dims, 2)
    for a, b in (("ls", "lr"), ("ss", "sr")):
        scratch[a], scratch[b] = plane_sems(dims)
    names += list(outs) + list(scratch)
    result = pl.pallas_call(
        partial(step_kernel, cfg, tuple(names)),
        name="step",
        out_shape=[jax.ShapeDtypeStruct(s, d) for s, d in outs.values()],
        in_specs=specs,
        out_specs=[pl.BlockSpec(memory_space=VMEM)] * len(outs),
        scratch_shapes=list(scratch.values()),
        compiler_params=params(0),
    )(*inputs.values())
    return dict(zip(outs, result))


def update_kernel(nm, ng, kc, *refs):
    reduced, small, sums = refs[:5], refs[5], refs[6]
    states, outs = refs[7:28], refs[28:]
    total = sums[0:1, 0:1]
    norm = jnp.sqrt(total)
    outs[0][...] = sums[1:2, 0:1]
    outs[1][...] = norm
    factor = jnp.minimum(1.0, CLIP_LIMIT / norm)

    def update(which, index, gradient, rate):
        old = [states[3 * which + k][index] for k in range(3)]
        new = adam_update(*old, gradient * factor, rate)
        for k in range(3):
            outs[2 + 3 * which + k][index] = new[k]

    for t in range(9):
        update(0, (0, t), reduced[0][:, t * nm : (t + 1) * nm], LEARN_RATE)
        update(0, (1, t), reduced[2][:, t * nm : (t + 1) * nm], LEARN_RATE)
        update(1, (t,), reduced[1][:, t * ng : (t + 1) * ng], LEARN_RATE)
        update(2, (t,), reduced[3][:, t * nm : (t + 1) * nm], LEARN_RATE)
        at = t // 3 * 128 + t % 3 * kc
        update(3, (t,), reduced[4][:, at : at + kc], LEARN_RATE)
    update(4, (slice(None),), small[0:4, :], SMALL_RATE)
    per = ng // nm
    for k in range(2):
        pieces = [small[4 + k * per + i : 5 + k * per + i, :] for i in range(per)]
        update(5, (slice(k, k + 1),), jnp.concatenate(pieces, axis=1), SMALL_RATE)
    at = 4 + 2 * per
    update(6, (slice(None),), small[at : at + 1, :kc], SMALL_RATE)


def run_update(nm, ng, kc, reduced, small, sums, states):
    args = list(reduced) + [small, sums] + list(states)
    shapes = [jax.ShapeDtypeStruct((1, 1), F32)] * 2
    shapes += [jax.ShapeDtypeStruct(s.shape, F32) for s in states]
    return pl.pallas_call(
        partial(update_kernel, nm, ng, kc),
        name="update",
        out_shape=shapes,
        in_specs=[pl.BlockSpec(memory_space=VMEM)] * len(args),
        out_specs=[pl.BlockSpec(memory_space=VMEM)] * len(shapes),
        compiler_params=pltpu.CompilerParams(vmem_limit_bytes=VMEM_LIMIT),
    )(*args)


def lanes_of_taps(weight):
    taps, depth, width = weight.shape
    return weight.transpose(1, 0, 2).reshape(depth, taps * width)


def class_lanes(weight):
    _, depth, width = weight.shape
    rows = weight.transpose(1, 0, 2).reshape(depth, 3, 3 * width)
    return jnp.pad(rows, ((0, 0), (0, 0), (0, 128 - 3 * width))).reshape(depth, 384)


def adam_update(weight, moment, square, gradient, rate):
    moment_new = BETA_ONE * moment + (1.0 - BETA_ONE) * gradient
    square_new = BETA_TWO * square + (1.0 - BETA_TWO) * gradient * gradient
    moment_hat = moment_new / (1.0 - BETA_ONE**STEP_TIME)
    square_hat = square_new / (1.0 - BETA_TWO**STEP_TIME)
    weight_new = weight - rate * (
        moment_hat / (jnp.sqrt(square_hat) + ADAM_EPS) + WEIGHT_DECAY * weight
    )
    return (weight_new, moment_new, square_new)


def body(
    mask_features,
    grid_features,
    instance_cells,
    instance_counts,
    instance_labels,
    instance_masks,
    *states,
):
    images = lax.axis_size("dp")
    data_index = lax.axis_index("dp")
    dims = line_lengths(images)
    mask_convs, grid_first, grid_second, class_conv = states[0:12:3]
    mask_norms, grid_norms, class_bias = states[12::3]
    _, high, wide, half = mask_features.shape
    grid = grid_features.shape[1]
    pad = -(-(grid + 1) // 16) * 16
    nm, ng, kc = mask_convs.shape[3], grid_first.shape[2], class_conv.shape[2]
    fused = grid_first.shape[1] % 16 == 0
    cfg = dict(
        dims=dims,
        images=images,
        mask_map=Map(high, wide, wide, 8, 4, nm, 2 * nm // GROUPS),
        grid_map=Map(grid, pad, grid, grid // 2, grid // 2, ng, 2 * ng // GROUPS),
        kc=kc,
        fused=fused,
    )
    inputs = dict(
        xm_own=mask_features,
        xg_own=grid_features,
        masks=instance_masks.transpose(1, 0, 2),
        counts=instance_counts,
        cells=instance_cells,
        labels=instance_labels,
        mask_norms=mask_norms,
        grid_norms=grid_norms,
        class_bias=class_bias[None, :],
    )
    if fused:
        weights = dict(
            mask_convs=mask_convs,
            grid_first=grid_first,
            grid_second=grid_second,
            class_conv=class_conv,
        )
        blocks = [
            dims + (mask_convs.shape[2], 9 * nm),
            dims + (grid_first.shape[1], 9 * ng),
            dims + (mask_convs.shape[2], 9 * nm),
            dims + (grid_second.shape[1], 9 * nm),
            dims + (class_conv.shape[1], 384),
        ]
        out = run_step(cfg, inputs, weights, blocks)
        reduced = [out["out%d" % i] for i in range(5)]
        sums = out["sum_out"]
    else:
        shards = [
            lanes_of_taps(mask_convs[0].astype(BF16)),
            lanes_of_taps(grid_first.astype(BF16)),
            lanes_of_taps(mask_convs[1].astype(BF16)),
            lanes_of_taps(grid_second.astype(BF16)),
            class_lanes(class_conv.astype(BF16)),
        ]
        gathered = gather_all(dims, shards)
        weights = {"w%d" % i: b.reshape(-1, b.shape[-1]) for i, b in enumerate(gathered)}
        out = run_step(cfg, inputs, weights, None)
        reduced = reduce_all(
            dims, [out["g%d" % i].reshape(b.shape) for i, b in enumerate(gathered)]
        )
        squares = sum(jnp.sum(jnp.square(value)) for value in reduced)
        squares += (data_index == 0).astype(F32) * jnp.sum(jnp.square(out["small_out"]))
        pair = lax.psum((squares, out["sum_out"][0, 0]), ("dp", "mp"))
        sums = jnp.broadcast_to(jnp.pad(jnp.stack(pair), (0, 6))[:, None], (8, 128))
    states = states[:18] + tuple(state[None, :] for state in states[18:])
    result = run_update(nm, ng, kc, reduced, out["small_out"], sums, states)
    result = [value.reshape(()) for value in result[:2]] + list(result[2:])
    return tuple(result[:20]) + tuple(value[0] for value in result[20:])


def solution(mesh):
    in_specs = (
        P("dp", None, None, "mp"),
        P("dp", None, None, "mp"),
        P("dp", None),
        P(),
        P("dp", None),
        P("dp", None, None),
        P(None, None, "dp", "mp"),
        P(None, None, "dp", "mp"),
        P(None, None, "dp", "mp"),
        P(None, "dp", "mp"),
        P(None, "dp", "mp"),
        P(None, "dp", "mp"),
        P(None, "dp", "mp"),
        P(None, "dp", "mp"),
        P(None, "dp", "mp"),
        P(None, "dp", "mp"),
        P(None, "dp", "mp"),
        P(None, "dp", "mp"),
        P(None, "mp"),
        P(None, "mp"),
        P(None, "mp"),
        P(None, "mp"),
        P(None, "mp"),
        P(None, "mp"),
        P("mp"),
        P("mp"),
        P("mp"),
    )
    out_specs = (
        P(),
        P(),
        P(None, None, "dp", "mp"),
        P(None, None, "dp", "mp"),
        P(None, None, "dp", "mp"),
        P(None, "dp", "mp"),
        P(None, "dp", "mp"),
        P(None, "dp", "mp"),
        P(None, "dp", "mp"),
        P(None, "dp", "mp"),
        P(None, "dp", "mp"),
        P(None, "dp", "mp"),
        P(None, "dp", "mp"),
        P(None, "dp", "mp"),
        P(None, "mp"),
        P(None, "mp"),
        P(None, "mp"),
        P(None, "mp"),
        P(None, "mp"),
        P(None, "mp"),
        P("mp"),
        P("mp"),
        P("mp"),
    )
    return jax.shard_map(body, mesh=mesh, in_specs=in_specs, out_specs=out_specs, check_vma=False)
```

```python
from functools import partial

import jax
import jax.numpy as jnp
from jax import lax
from jax.experimental import pallas as pl
from jax.experimental.pallas import tpu as pltpu
from jax.sharding import PartitionSpec as P

GROUPS = 32
GN_EPS = 1e-05
CLIP_LIMIT = 0.02
LEARN_RATE = 0.02
SMALL_RATE = 0.5
BETA_ONE = 0.9
BETA_TWO = 0.95
ADAM_EPS = 1e-08
WEIGHT_DECAY = 0.05
CONTRAST_TEMP = 0.05
FOCAL_ALPHA = 0.25
DICE_WEIGHT = 3.0
STEP_TIME = 10.0
HIGHEST = lax.Precision.HIGHEST

MESH = pl.DeviceIdType.MESH
VMEM = pltpu.VMEM
ANY = pl.ANY
VMEM_LIMIT = 67043328
F32 = jnp.float32
BF16 = jnp.bfloat16
I32 = jnp.int32
SLOTS = 128
DMA = pltpu.SemaphoreType.DMA


def line_lengths(total):
    if total & (total - 1):
        return (total, 1, 1)
    bits = total.bit_length() - 1
    last = bits // 3
    middle = (bits - last) // 2
    return (1 << (bits - last - middle), 1 << middle, 1 << last)


def place(dims):
    index = lax.axis_index("dp")
    return (index // (dims[1] * dims[2]), (index // dims[2]) % dims[1], index % dims[2])


def split_index(dims, index):
    return (
        index // (dims[1] * dims[2]),
        lax.rem(index // dims[2], dims[1]),
        lax.rem(index, dims[2]),
    )


def along(dims, axis, step):
    stride = (dims[1] * dims[2], dims[2], 1)[axis]
    return {"dp": lax.axis_index("dp") + step * stride}


def partner():
    return {"mp": 1 - lax.axis_index("mp")}


def ring_step(dims, pos, axis, offset):
    other = lax.rem(pos[axis] + offset, dims[axis])
    return along(dims, axis, other - pos[axis])


def plane_peers(dims, cores):
    pos = place(dims)
    model = lax.axis_index("mp")
    peers = []
    for y in range(dims[1]):
        for x in range(dims[2]):
            for core in range(2 if cores else 1):
                if y == x == core == 0:
                    continue
                at = (pos[0] * dims[1] + lax.rem(pos[1] + y, dims[1])) * dims[2]
                peer = {"dp": at + lax.rem(pos[2] + x, dims[2])}
                if core:
                    peer["mp"] = 1 - model
                peers.append(peer)
    return peers


def greet_start(dims):
    sem = pltpu.get_barrier_semaphore()
    pos = place(dims)
    peers = plane_peers(dims, True)
    peers += [ring_step(dims, pos, 0, offset) for offset in range(1, dims[0])]
    for peer in peers:
        pl.semaphore_signal(sem, inc=1, device_id=peer, device_id_type=MESH)
    return sem, len(peers)


def greet_end(sem, count):
    pl.semaphore_wait(sem, count)


def greet(dims):
    greet_end(*greet_start(dims))


GATHER_ORDERS = ((2, 1, 0), (0, 2, 1), (0, 1, 2))
REDUCE_ORDERS = tuple(tuple(reversed(order)) for order in GATHER_ORDERS)


def line_copies(dims):
    return sum(n - 1 for n in dims)


def lane_cuts(width):
    tiles = width // 128
    if width % 128 or tiles < 3:
        return ((0, 0, width),)
    first = max(1, round(tiles * 0.17))
    second = (tiles - first) // 2
    sizes = (first, second, tiles - first - second)
    cuts, start = [], 0
    for order, size in enumerate(sizes):
        cuts.append((order, start * 128, size * 128))
        start += size
    return tuple(cuts)


def tap_row_cuts(width):
    third = width // 3
    if third % 384:
        return lane_cuts(width)
    near = third // 384 * 128
    return ((2, 0, third), (1, third, third), (1, 2 * third, near), (2, 2 * third + near, 2 * near))


class Exchange:
    def __init__(self):
        self.stages, self.lands, self.next = [], [], 0

    def finish(self):
        if 0 < self.next <= len(self.stages):
            for copy in self.stages[self.next - 1]:
                copy.wait_recv()
            self.lands[self.next - 1]()

    def start(self):
        if self.next < len(self.stages):
            for copy in self.stages[self.next]:
                copy.start()
        self.next += 1

    def drain(self):
        for stage in self.stages:
            for copy in stage:
                copy.wait_send()


def advance(*exchanges):
    for exchange in exchanges:
        exchange.finish()
    for exchange in exchanges:
        exchange.start()


def complete(*exchanges):
    while any(e.next <= len(e.stages) for e in exchanges):
        advance(*exchanges)


def nothing():
    return None


def gather_exchange(dims, out, send_sems, recv_sems, base, lanes, order, tail=None):
    pos = place(dims)
    result, done = Exchange(), set()
    tail = (slice(None), lanes) if tail is None else tail
    for axis in order:
        view = out.at[tuple(pl.ds(0, dims[k]) if k in done else pos[k] for k in range(3)) + tail]
        copies = []
        for offset in range(1, dims[axis]):
            copies.append(
                pltpu.make_async_remote_copy(
                    src_ref=view,
                    dst_ref=view,
                    send_sem=send_sems.at[base],
                    recv_sem=recv_sems.at[base],
                    device_id=ring_step(dims, pos, axis, offset),
                    device_id_type=MESH,
                )
            )
            base += 1
        if copies:
            result.stages.append(copies)
            result.lands.append(nothing)
        done.add(axis)
    return result


def remote(view, send_sem, recv_sem, device):
    return pltpu.make_async_remote_copy(
        src_ref=view,
        dst_ref=view,
        send_sem=send_sem,
        recv_sem=recv_sem,
        device_id=device,
        device_id_type=MESH,
    )


def core_exchange(out, sems):
    result = Exchange()
    view = out.at[:, :, :, lax.axis_index("mp")]
    result.stages.append([remote(view, sems.at[0], sems.at[1], partner())])
    result.lands.append(nothing)
    return result


def plane_slots(dims):
    return 2 * dims[1] * dims[2] + dims[0]


def plane_sems(dims):
    return [DMA((plane_slots(dims),)), DMA((plane_slots(dims),))]


def plane_exchange(dims, view, line_view, cores, land, send_sems, recv_sems):
    result, pos = Exchange(), place(dims)
    first = [
        remote(view, send_sems.at[i], recv_sems.at[i], peer)
        for i, peer in enumerate(plane_peers(dims, cores))
    ]
    base = len(first)
    second = [
        remote(
            line_view,
            send_sems.at[base + offset - 1],
            recv_sems.at[base + offset - 1],
            ring_step(dims, pos, 0, offset),
        )
        for offset in range(1, dims[0])
    ]
    result.stages, result.lands = [first, second], [land, nothing]
    return result


def landing_shapes(dims, rows, width, order):
    shapes, left = [], {0, 1, 2}
    for axis in order:
        left = left - {axis}
        shapes.append(
            (max(1, dims[axis] - 1),) + tuple(dims[k] for k in sorted(left)) + (rows, width)
        )
    return shapes


def reduce_exchange(dims, total, staged, lands, send_sems, recv_sems, base, lanes, order):
    pos = place(dims)
    result = Exchange()
    axes = [axis for axis in order if dims[axis] > 1]

    def over_blocks(free, inner, body):
        outer = [k for k in free if k != inner]
        count = 1
        for k in outer:
            count *= dims[k]

        def step(i, carry):
            where, rest = {}, i
            for k in reversed(outer):
                where[k] = lax.rem(rest, dims[k])
                rest = rest // dims[k]
            for offset in range(dims[inner] if inner is not None else 1):
                here = dict(where)
                if inner is not None:
                    here[inner] = lax.rem(pos[inner] + offset, dims[inner])
                body(here, offset)
            return carry

        if count == 1:
            step(jnp.int32(0), 0)
        else:
            lax.fori_loop(0, count, step, 0)

    def index_of(where):
        return tuple(where.get(k, pos[k]) for k in range(3)) + (slice(None), lanes)

    def prepare():
        def cast(where, offset):
            if offset:
                staged[index_of(where)] = total[index_of(where)].astype(BF16)

        over_blocks(axes, axes[0], cast)

    result.prepare = prepare
    for stage, axis in enumerate(axes):
        n = dims[axis]
        free = axes[stage + 1 :]
        inner = free[0] if free else None
        copies = []
        for offset in range(1, n):
            view = tuple(
                lax.rem(pos[axis] + offset, n)
                if k == axis
                else (pl.ds(0, dims[k]) if k in free else pos[k])
                for k in range(3)
            )
            copies.append(
                pltpu.make_async_remote_copy(
                    src_ref=staged.at[view + (slice(None), lanes)],
                    dst_ref=lands[order.index(axis)].at[offset - 1],
                    send_sem=send_sems.at[base],
                    recv_sem=recv_sems.at[base],
                    device_id=ring_step(dims, pos, axis, offset),
                    device_id_type=MESH,
                )
            )
            base += 1

        def land(axis=axis, n=n, free=free, inner=inner):
            arrived = lands[order.index(axis)]
            left = sorted(free + [k for k in range(3) if dims[k] == 1 and k in later(axis)])

            def add(where, offset):
                index = index_of(where)
                value = total[index]
                for k in range(n - 1):
                    lead = tuple(where.get(j, 0) for j in left)
                    value = value + arrived[(k,) + lead].astype(F32)
                if offset:
                    staged[index] = value.astype(BF16)
                else:
                    total[index] = value

            over_blocks(free, inner, add)

        def later(axis):
            return order[order.index(axis) + 1 :]

        result.stages.append(copies)
        result.lands.append(land)
    return result


def share_sems(dims, pieces):
    return [DMA((pieces * line_copies(dims),)), DMA((pieces * line_copies(dims),))]


def pair_copy(source, target, sems):
    return pltpu.make_async_remote_copy(
        src_ref=source,
        dst_ref=target,
        send_sem=sems.at[0],
        recv_sem=sems.at[1],
        device_id=partner(),
        device_id_type=MESH,
    )


def params(collective_id):
    return pltpu.CompilerParams(
        collective_id=collective_id, has_side_effects=True, vmem_limit_bytes=VMEM_LIMIT
    )


def gather_groups(dims, outs, send_sems, recv_sems):
    groups, base = [], 0
    for out in outs:
        group = []
        for order, start, size in lane_cuts(out.shape[4]):
            group.append(
                gather_exchange(
                    dims, out, send_sems, recv_sems, base, pl.ds(start, size), GATHER_ORDERS[order]
                )
            )
            base += line_copies(dims)
        groups.append(group)
    return groups


def reduce_groups(dims, totals, staged, lands, send_sems, recv_sems, cuts):
    groups, base, lands = [], 0, list(lands)
    for total, stage, cut in zip(totals, staged, cuts):
        group = []
        for order, start, size in cut:
            group.append(
                reduce_exchange(
                    dims,
                    total,
                    stage,
                    lands[:3],
                    send_sems,
                    recv_sems,
                    base,
                    pl.ds(start, size),
                    REDUCE_ORDERS[order],
                )
            )
            lands = lands[3:]
            base += line_copies(dims)
        groups.append(group)
    return groups


def flow_slots(dims, cuts):
    return max(1, line_copies(dims) * sum(len(cut) for cut in cuts))


def landing_scratch(dims, shapes, cuts):
    scratch = []
    for shape, cut in zip(shapes, cuts):
        for order, _, size in cut:
            for land in landing_shapes(dims, shape[-2], size, REDUCE_ORDERS[order]):
                scratch.append(VMEM(land, BF16))
    return scratch


def run_all(groups):
    exchanges = [exchange for group in groups for exchange in group]
    complete(*exchanges)
    for exchange in exchanges:
        exchange.drain()


def gather_kernel(dims, count, *refs):
    shards, outs = refs[:count], refs[count : 2 * count]
    send_sems, recv_sems, local_sems = refs[2 * count :]
    pos = place(dims)
    local = [
        pltpu.make_async_copy(shards[i], outs[i].at[pos[0], pos[1], pos[2]], local_sems.at[i])
        for i in range(count)
    ]
    for copy in local:
        copy.start()
    greet(dims)
    for copy in local:
        copy.wait()
    run_all(gather_groups(dims, outs, send_sems, recv_sems))


def gather_all(dims, shards):
    count = len(shards)
    shapes = [dims + s.shape for s in shards]
    slots = flow_slots(dims, [lane_cuts(s[-1]) for s in shapes])
    return pl.pallas_call(
        partial(gather_kernel, dims, count),
        name="gather_weights",
        out_shape=[jax.ShapeDtypeStruct(s, BF16) for s in shapes],
        in_specs=[pl.BlockSpec(memory_space=VMEM)] * count,
        out_specs=[pl.BlockSpec(memory_space=VMEM)] * count,
        scratch_shapes=[DMA((slots,)), DMA((slots,)), DMA((count,))],
        compiler_params=params(1),
    )(*shards)


def reduce_kernel(dims, count, *refs):
    parts, outs = refs[:count], refs[count : 2 * count]
    send_sems, recv_sems, local_sems = refs[2 * count : 2 * count + 3]
    rest = list(refs[2 * count + 3 :])
    totals, staged, lands = rest[:count], rest[count : 2 * count], rest[2 * count :]
    pos = place(dims)
    local = [pltpu.make_async_copy(parts[i], totals[i], local_sems.at[i]) for i in range(count)]
    for copy in local:
        copy.start()
    greet(dims)
    for i in range(count):
        local[i].wait()
    cuts = [lane_cuts(total.shape[4]) for total in totals]
    groups = reduce_groups(dims, totals, staged, lands, send_sems, recv_sems, cuts)
    for group in groups:
        for exchange in group:
            exchange.prepare()
    run_all(groups)
    for i in range(count):
        outs[i][...] = totals[i][pos[0], pos[1], pos[2]]


def reduce_all(dims, parts):
    count = len(parts)
    shapes = [p.shape for p in parts]
    cuts = [lane_cuts(s[-1]) for s in shapes]
    slots = flow_slots(dims, cuts)
    scratch = [DMA((slots,)), DMA((slots,)), DMA((count,))]
    scratch += [VMEM(s, F32) for s in shapes] + [VMEM(s, BF16) for s in shapes]
    scratch += landing_scratch(dims, shapes, cuts)
    return pl.pallas_call(
        partial(reduce_kernel, dims, count),
        name="reduce_gradients",
        out_shape=[jax.ShapeDtypeStruct(s[3:], F32) for s in shapes],
        in_specs=[pl.BlockSpec(memory_space=ANY)] * count,
        out_specs=[pl.BlockSpec(memory_space=VMEM)] * count,
        scratch_shapes=scratch,
        compiler_params=params(2),
    )(*parts)


def group_sums(row, spread):
    width = row.shape[1]
    return lax.dot_general(
        jnp.broadcast_to(row, (8, width)),
        spread,
        (((1,), (0,)), ((), ())),
        precision=HIGHEST,
        preferred_element_type=F32,
    )[0:1]


def group_spread(width, group):
    rows = lax.broadcasted_iota(I32, (width, width), 0) // group
    cols = lax.broadcasted_iota(I32, (width, width), 1) // group
    return (rows == cols).astype(F32)


def dot(a, b, contract):
    return lax.dot_general(a, b, ((contract[0], contract[1]), ((), ())), preferred_element_type=F32)


NN = ((1,), (0,))
NT = ((1,), (1,))
TN = ((0,), (0,))


class Map:
    def __init__(self, high, width, live, span, part, channels, group):
        self.high, self.width, self.live = high, width, live
        self.span, self.part, self.channels = span, part, channels
        self.pixels = float(high * live * group)

    def column(self, span):
        shape = (span, self.width, self.channels)
        return lax.broadcasted_iota(I32, shape, 1).reshape(span * self.width, self.channels)

    def masked(self, value, span):
        if self.live == self.width:
            return value
        return jnp.where(self.column(span) < self.live, value, 0.0)

    def at(self, i, span):
        return pl.ds(pl.multiple_of(i * span * self.width, 16), span * self.width)


def take(source, first, count, lanes=slice(None)):
    value = source[pl.ds(first, count), :, lanes]
    return value.reshape(-1, value.shape[2])


def conv_forward(m, source, weight, raw, first=0, last=None, total=None):
    n, tile = m.channels, m.span * m.width

    def body(i, total):
        wide = None
        for du in range(3):
            part = dot(take(source, i * m.span + du, m.span), weight(du), NN)
            wide = part if wide is None else wide + part
        left = pltpu.roll(wide[:, :n], 1, 0)
        right = pltpu.roll(wide[:, 2 * n :], tile - 1, 0)
        if m.live == m.width:
            column = m.column(m.span)
            left = jnp.where(column == 0, 0.0, left)
            right = jnp.where(column == m.width - 1, 0.0, right)
        value = m.masked(left + wide[:, n : 2 * n] + right, m.span)
        raw[m.at(i, m.span), :] = value
        return total + jnp.sum(value, axis=0, keepdims=True)

    last = m.high // m.span if last is None else last
    total = jnp.zeros((1, n), F32) if total is None else total
    return lax.fori_loop(first, last, body, total)


def norm_forward(m, raw, total, spread, gain, bias, store):
    n, part = m.channels, m.part
    mean = group_sums(total, spread) / m.pixels

    def spread_of(i, acc):
        away = m.masked(raw[m.at(i, part), :] - mean, part)
        return acc + jnp.sum(away * away, axis=0, keepdims=True)

    squares = lax.fori_loop(0, m.high // part, spread_of, jnp.zeros((1, n), F32))
    scale = lax.rsqrt(group_sums(squares, spread) / m.pixels + GN_EPS)

    def normalize(i, carry):
        normed = (raw[m.at(i, part), :] - mean) * scale
        raw[m.at(i, part), :] = normed
        value = m.masked(jnp.maximum(normed * gain + bias, 0.0), part)
        store(i, value.astype(BF16))
        return carry

    lax.fori_loop(0, m.high // part, normalize, 0)
    return scale


def norm_backward(m, normed, upstream, spare, shifted, spread, gain, bias, scale):
    n, part = m.channels, m.part
    tile = part * m.width

    def first(i, sums):
        here = normed[m.at(i, part), :]
        value = m.masked(jnp.where(here * gain + bias > 0.0, upstream(i), 0.0), part)
        spare[m.at(i, part), :] = value
        return (
            sums[0] + jnp.sum(value * here, axis=0, keepdims=True),
            sums[1] + jnp.sum(value, axis=0, keepdims=True),
        )

    zero = jnp.zeros((1, n), F32)
    gain_sum, bias_sum = lax.fori_loop(0, m.high // part, first, (zero, zero))
    level = group_sums(bias_sum * gain, spread) / m.pixels
    slope = group_sums(gain_sum * gain, spread) / m.pixels

    def second(i, carry):
        value = scale * (spare[m.at(i, part), :] * gain - level - normed[m.at(i, part), :] * slope)
        value = m.masked(value, part)
        left = pltpu.roll(value, tile - 1, 0)
        right = pltpu.roll(value, 1, 0)
        if m.live == m.width:
            column = m.column(part)
            left = jnp.where(column == m.width - 1, 0.0, left)
            right = jnp.where(column == 0, 0.0, right)
        into = pl.ds(i * part + 1, part)
        for k, piece in enumerate((left, value, right)):
            shifted[into, :, k * n : (k + 1) * n] = piece.astype(BF16).reshape(part, m.width, n)
        return carry

    lax.fori_loop(0, m.high // part, second, 0)
    return gain_sum, bias_sum


def weight_gradient(m, source, shifted, total, lanes, each=None):
    width = lanes.stop - lanes.start
    for du in range(3):
        value = dot(take(source, du, m.high), take(shifted, 1, m.high, lanes), TN)
        into = total.at[..., du * width : (du + 1) * width]
        into[...] = value.reshape(into.shape)
        if each is not None:
            each(du)


def zero_edges(ref):
    blank = jnp.zeros((1,) + ref.shape[1:], ref.dtype)
    ref[0:1] = blank
    ref[ref.shape[0] - 1 : ref.shape[0]] = blank


def diagonal(n):
    return lax.broadcasted_iota(I32, (n, n), 0) == lax.broadcasted_iota(I32, (n, n), 1)


def as_row(column):
    return jnp.sum(jnp.where(diagonal(column.shape[0]), column, 0.0), axis=0, keepdims=True)


def as_column(row):
    return jnp.sum(jnp.where(diagonal(row.shape[1]), row, 0.0), axis=1, keepdims=True)


def step_kernel(cfg, names, *refs):
    r = dict(zip(names, refs))
    dims, images, fused = cfg["dims"], cfg["images"], cfg["fused"]
    big, small = cfg["mask_map"], cfg["grid_map"]
    nm, ng, kc = big.channels, small.channels, cfg["kc"]
    grid, pad = small.live, small.width
    rows, grid_rows = big.high * big.width, small.high * small.width
    gtile = small.span * small.width
    pos = place(dims)
    model = lax.axis_index("mp")
    own_image = lax.axis_index("dp")

    def lanes_of(width, side):
        return pl.ds(pl.multiple_of(side * width, width), width)

    own_m, away_m = lanes_of(nm, model), lanes_of(nm, 1 - model)
    own_g, away_g = lanes_of(ng, model), lanes_of(ng, 1 - model)
    own_x = lanes_of(r["xm_own"].shape[3], model)
    map_rows, grid_span = pl.ds(1, big.high), pl.ds(1, small.high)
    spread_m = group_spread(nm, 2 * nm // GROUPS)
    spread_g = group_spread(ng, 2 * ng // GROUPS)

    greeted = greet_start(dims)

    xm, xg, hm, hg, dm = r["xm"], r["xg"], r["hm"], r["hg"], r["dm"]
    dg1, dg2 = r["dg1"], r["dg2"]
    mask_in, grid_in = r["xm_own"].at[0], r["xg_own"].at[0]
    mask_into = xm.at[map_rows, :, own_x]
    grid_into = xg.at[grid_span, pl.ds(0, grid), own_x]
    local = [
        pltpu.make_async_copy(mask_in, mask_into, r["local"].at[0]),
        pltpu.make_async_copy(grid_in, grid_into, r["local"].at[1]),
    ]
    masks = r["mask_bits"]
    mask_copy = pltpu.make_async_copy(r["masks"].at[:, 0, :], masks, r["local"].at[2])
    for copy in local:
        copy.start()
    mask_copy.start()
    weights = [r["w%d" % i] for i in range(5)]
    groups = []
    if fused:
        for t in range(9):
            for i, value in (
                (0, r["mask_convs"][0, t]),
                (1, r["grid_first"][t]),
                (2, r["mask_convs"][1, t]),
                (3, r["grid_second"][t]),
            ):
                width = value.shape[1]
                weights[i][pos[0], pos[1], pos[2], :, t * width : (t + 1) * width] = value.astype(
                    BF16
                )
        class_in = r["class_conv"]
        for du in range(3):
            pieces = [class_in[3 * du + dv] for dv in range(3)]
            pieces.append(jnp.zeros((class_in.shape[1], 128 - 3 * kc), F32))
            weights[4][pos[0], pos[1], pos[2], :, du * 128 : (du + 1) * 128] = jnp.concatenate(
                pieces, axis=1
            ).astype(BF16)
        groups = gather_groups(dims, weights, r["gs"], r["gr"])

    def bring(*which):
        if fused:
            advance(*[exchange for i in which for exchange in groups[i]])

    greet_end(*greeted)
    bring(0)
    feature_copies = [
        pair_copy(mask_in, mask_into, r["pair"].at[0]),
        pair_copy(grid_in, grid_into, r["pair"].at[1]),
    ]
    feature_copies[0].start()
    bring(1)
    feature_copies[1].start()

    totals = [r["g%d" % i] for i in range(5)]
    out_groups = []
    if fused:
        staged = [weights[2], weights[1], weights[0], r["second_stage"], r["class_stage"]]
        lands = [r["land%d" % i] for i in range(cfg["lands"])]
        out_groups = reduce_groups(dims, totals, staged, lands, r["rs"], r["rr"], cfg["cuts"])

    def send(*which):
        if fused:
            advance(*[exchange for i in which for exchange in out_groups[i]])

    def send_first(i):
        if fused:
            for exchange in out_groups[i]:
                exchange.prepare()
            send(i)

    def send_tap_row(du):
        if not fused:
            return
        third = 3 * nm
        for (_, start, _), exchange in zip(cfg["cuts"][0], out_groups[0]):
            if len(out_groups[0]) == 1 and du == 2 or start // third == du:
                exchange.prepare()
                advance(exchange)

    for ref in (xm, xg, hm, hg, dm, dg1, dg2):
        zero_edges(ref)
    xg[:, grid:, :] = jnp.zeros((xg.shape[0], pad - grid, xg.shape[2]), BF16)
    share = jnp.float32(1.0 / images)
    table, bias_table = r["table"], r["bias_table"]
    slots = r["cells"].shape[1]
    table[...] = jnp.full(table.shape, -(1 << 20), I32)
    table[0:1, 0:slots] = r["cells"][...]
    table[1:2, 0:slots] = r["labels"][...]
    bias_table[...] = jnp.zeros(bias_table.shape, F32)
    bias_table[0:1, 0:kc] = r["class_bias"][...]
    cells = table[0:1, :].astype(F32)
    cells = cells + jnp.floor((cells + 0.5) / grid) * (pad - grid)
    cells_row = cells.astype(I32)
    cells_col = as_column(cells).astype(I32)
    labels_col = as_column(table[1:2, :].astype(F32)).astype(I32) - model * kc
    class_bias = bias_table[0:1, :]
    own_count = r["counts"][own_image]
    slot_lanes = lax.broadcasted_iota(I32, (1, SLOTS), 1)
    slot_rows = lax.broadcasted_iota(I32, (SLOTS, 1), 0)
    own_float = jnp.full((1, 1), own_count, I32).astype(F32)
    live_row = (slot_lanes < own_count).astype(F32)
    live_col = (slot_rows < own_count).astype(F32)
    weight_col = live_col * (share / own_float)
    dice_col = DICE_WEIGHT * weight_col
    focal_scale = share / (own_float + 1.0)
    bring(0)
    bring(0)
    bring(1)

    def weight(i, span):
        def part(du):
            value = weights[i][..., du * span : (du + 1) * span]
            return value.reshape(-1, span) if fused else value

        return part

    mask_one, grid_one, mask_two = weight(0, 3 * nm), weight(1, 3 * ng), weight(2, 3 * nm)
    grid_two, class_two = weight(3, 3 * nm), weight(4, 128)

    norms, gnorms = r["mask_norms"], r["grid_norms"]
    row = lambda ref, k: ref[k : k + 1, :]
    bring(2)
    for copy in local:
        copy.wait()
    feature_copies[0].wait()
    bring(0)
    xh1 = r["xh1"]
    total = conv_forward(big, xm, mask_one, xh1)
    bring(1)
    bring(2)
    bring(4)
    bring(3)

    def keep_mask(i, value):
        hm[pl.ds(i * big.part + 1, big.part), :, own_m] = value.reshape(big.part, big.width, nm)

    scale_one = norm_forward(big, xh1, total, spread_m, row(norms, 0), row(norms, 1), keep_mask)
    hm_copy = pair_copy(
        hm.at[map_rows, :, own_m], hm.at[map_rows, :, own_m], r["pair"].at[2]
    )
    hm_copy.start()
    feature_copies[1].wait()
    bring(1)
    xhg = r["xhg"]
    total = conv_forward(small, xg, grid_one, xhg, 0, 1)
    bring(2)
    bring(4)
    bring(3)
    total = conv_forward(small, xg, grid_one, xhg, 1, None, total)

    def keep_grid(i, value):
        hg[pl.ds(i * small.part + 1, small.part), :, own_g] = value.reshape(
            small.part, small.width, ng
        )

    scale_grid = norm_forward(
        small, xhg, total, spread_g, row(gnorms, 0), row(gnorms, 1), keep_grid
    )
    hg_copy = pair_copy(
        hg.at[grid_span, :, own_g], hg.at[grid_span, :, own_g], r["pair"].at[3]
    )
    hg_copy.start()

    hm_copy.wait()
    bring(2)
    xh2, feature = r["xh2"], r["feature"]
    half = big.high // big.span // 2
    total = conv_forward(big, hm, mask_two, xh2, 0, half)
    bring(4)
    bring(3)
    total = conv_forward(big, hm, mask_two, xh2, half, None, total)

    def keep_feature(i, value):
        feature[big.at(i, big.part), :] = value

    scale_two = norm_forward(
        big, xh2, total, spread_m, row(norms, 2), row(norms, 3), keep_feature
    )

    hg_copy.wait()
    patches = r["patches"]
    lane = lax.broadcasted_iota(I32, (SLOTS, grid_rows), 1)
    depth = hg.shape[2]
    for t in range(9):
        chosen = (lane == cells_col + ((t // 3 - 1) * pad + t % 3 - 1)).astype(F32).astype(BF16)
        patches[:, t * depth : (t + 1) * depth] = dot(
            chosen, take(hg, 1, small.high), NN
        ).astype(BF16)
    if fused:
        complete(*groups[4])

    class_hot = (
        (lax.broadcasted_iota(I32, (SLOTS, 128), 1) == labels_col).astype(F32).astype(BF16)
    )

    def class_tile(i, sums):
        value = None
        for du in range(3):
            part = dot(take(hg, i * small.span + du, small.span), class_two(du), NN)
            value = part if value is None else value + part
        x = (
            pltpu.roll(value, 1, 0)
            + pltpu.roll(value, 128 - kc, 1)
            + pltpu.roll(pltpu.roll(value, 128 - 2 * kc, 1), gtile - 1, 0)
            + class_bias
        )
        at = lax.broadcasted_iota(I32, (gtile, SLOTS), 0) + i * gtile
        cell_hot = jnp.where(at == cells_row, live_row, 0.0).astype(BF16)
        t = dot(cell_hot, class_hot, NN)
        lanes = lax.broadcasted_iota(I32, (gtile, 128), 1)
        column = lax.broadcasted_iota(I32, (small.span, pad, 128), 1).reshape(gtile, 128)
        real = (column < grid) & (lanes < kc)
        tiny = jnp.exp(-jnp.abs(x))
        extra = jnp.log1p(tiny)
        inverse = 1.0 / (1.0 + tiny)
        q = jnp.where(x >= 0.0, 1.0, tiny) * inverse
        p = jnp.where(x >= 0.0, tiny, 1.0) * inverse
        log_q = -(jnp.maximum(-x, 0.0) + extra)
        log_p = -(jnp.maximum(x, 0.0) + extra)
        terms = FOCAL_ALPHA * t * p * p * log_q + (1.0 - FOCAL_ALPHA) * (1.0 - t) * q * q * log_p
        slope = FOCAL_ALPHA * t * p * p * (p - 2.0 * q * log_q) + (1.0 - FOCAL_ALPHA) * (
            1.0 - t
        ) * q * q * (2.0 * p * log_p - q)
        slope = jnp.where(real, -focal_scale * slope, 0.0).astype(BF16).astype(F32)
        shifted = (
            pltpu.roll(slope, gtile - 1, 0)
            + pltpu.roll(slope, kc, 1)
            + pltpu.roll(pltpu.roll(slope, 2 * kc, 1), 1, 0)
        )
        dg2[pl.ds(i * small.span + 1, small.span), :, 3 * nm :] = shifted.astype(BF16).reshape(
            small.span, pad, 128
        )
        return (
            sums[0] + jnp.sum(jnp.where(real, -focal_scale * terms, 0.0), axis=0, keepdims=True),
            sums[1] + jnp.sum(slope, axis=0, keepdims=True),
        )

    zero = jnp.zeros((1, 128), F32)
    focal_sum, class_bias_sum = lax.fori_loop(
        0, small.high // small.span, class_tile, (zero, zero)
    )

    weight_gradient(small, hg, dg2, totals[4], slice(3 * nm, 3 * nm + 128))

    for group in groups:
        complete(*group)
        for exchange in group:
            exchange.drain()
    picked = None
    for t in range(9):
        w = grid_two(t // 3)[:, (t % 3) * nm : (t % 3 + 1) * nm]
        part = dot(patches[:, t * depth : (t + 1) * depth], w, NN)
        picked = part if picked is None else picked + part
    kernels = r["kernels"]
    kept = (slots + 15) // 16 * 16
    if kept < SLOTS:
        kernels[..., kept:, :] = jnp.zeros(dims + (2, SLOTS - kept, nm), BF16)
    kernels[pos[0], pos[1], pos[2], model, 0:kept] = picked[0:kept].astype(BF16)
    upper = kept // 32 * 16
    kernel_share = [
        gather_exchange(
            dims, kernels, r["ks"], r["kr"], i * line_copies(dims), None, order,
            (model, pl.ds(start, size)),
        )
        for i, (order, start, size) in enumerate(
            ((GATHER_ORDERS[1], 0, upper), (GATHER_ORDERS[2], upper, kept - upper))
        )
    ]
    kernel_cores = core_exchange(kernels, r["pair"].at[7])
    advance(*kernel_share)
    send_first(4)

    kernel_rows = kernels[pos[0], pos[1], pos[2], model]
    logits, logits_in = r["logits"], r["logits_in"]
    high_slots = logits.shape[0]
    tile = big.span * big.width
    for i in range(rows // tile):
        span = slice(i * tile, (i + 1) * tile)
        logits[:, span] = dot(kernel_rows[:high_slots], feature[span, :], NT).astype(BF16)
    logits_copy = pair_copy(logits, logits_in, r["pair"].at[4])
    logits_copy.start()
    advance(*kernel_share)

    logits_copy.wait()
    mask_copy.wait()
    dice_sum = jnp.zeros((1, 1), F32)
    for start in range(0, slots, 16):
        span = slice(start, start + 16)
        x = logits[span, :].astype(F32) + logits_in[span, :].astype(F32)
        s = jax.nn.sigmoid(x)
        mask = masks[start : min(start + 16, slots), :].astype(F32)
        if mask.shape[0] < 16:
            mask = jnp.concatenate([mask, jnp.zeros((16 - mask.shape[0], rows), F32)], axis=0)
        inter = jnp.sum(s * mask, axis=1, keepdims=True)
        whole = jnp.sum(s * s, axis=1, keepdims=True) + jnp.sum(mask, axis=1, keepdims=True) + 1.0
        share_here = dice_col[span]
        dice_sum += jnp.sum(share_here * (1.0 - 2.0 * inter / whole), keepdims=True)
        a = -2.0 * share_here / whole
        b = 2.0 * share_here * inter / (whole * whole)
        logits[span, :] = ((a * mask + 2.0 * b * s) * s * (1.0 - s)).astype(BF16)
    advance(*kernel_share)
    send(4)

    several = 4 if images % 4 == 0 else 1

    def key_block(d):
        index = split_index(dims, d)
        return [kernels[index[0], index[1], index[2], k] for k in range(2)]

    def squares_of(block):
        return sum(
            jnp.sum(jnp.square(part.astype(F32)), axis=1, keepdims=True) for part in block
        )

    same_slot = diagonal(SLOTS)

    def scores(d, own_scale):
        block = key_block(d)
        raw = dot(own_full[0], block[0], NT) + dot(own_full[1], block[1], NT)
        key_scale = lax.rsqrt(as_row(squares_of(block)) + 1e-06)
        scale = own_scale * key_scale / CONTRAST_TEMP
        live = slot_lanes < r["counts"][d]
        allowed = live & jnp.logical_not(same_slot & (d == own_image))
        return block, raw, key_scale, scale, allowed

    def own_key_scale():
        return lax.rsqrt(squares_of(own_full) + 1e-06)

    logit_rows = dot(logits[...], feature[...], NN)
    dlogits, part_rows = logits, big.part * big.width

    def from_logits(i):
        pixels = pl.ds(pl.multiple_of(i * part_rows, part_rows), part_rows)
        return dot(dlogits[:, pixels], kernel_rows[:high_slots], TN)

    gain_two, bias_two = norm_backward(
        big, xh2, from_logits, r["spare"], dm, spread_m, row(norms, 2), row(norms, 3), scale_two
    )
    complete(*kernel_share)
    advance(kernel_cores)
    weight_gradient(big, hm, dm, totals[2], slice(0, 3 * nm))
    send_first(2)
    send(4)
    complete(kernel_cores)
    own_full = [kernels[pos[0], pos[1], pos[2], k] for k in range(2)]
    own_scale = own_key_scale()

    def sum_keys(i, acc):
        for k in range(several):
            _, raw, _, scale, allowed = scores(i * several + k, own_scale)
            value = jnp.where(allowed, jnp.exp(raw * scale), 0.0)
            acc = acc + jnp.sum(value, axis=1, keepdims=True)
        return acc

    totals_col = lax.fori_loop(0, images // several, sum_keys, jnp.zeros((SLOTS, 1), F32))
    contrast_sum = jnp.sum(
        jnp.where(weight_col > 0.0, weight_col * jnp.log(totals_col), 0.0), keepdims=True
    )
    key_totals = r["key_totals"]
    key_totals[pos[0], pos[1], pos[2]] = jnp.broadcast_to(as_row(totals_col), (8, SLOTS))
    total_share = plane_exchange(
        dims,
        key_totals.at[pos[0], pos[1], pos[2]],
        key_totals.at[pos[0]],
        False,
        nothing,
        r["ls"],
        r["lr"],
    )
    advance(total_share)
    hidden = hm

    def input_tile(i, carry):
        value = None
        for du in range(3):
            part = dot(take(dm, i * big.span + 2 - du, big.span), mask_two(du), NT)
            value = part if value is None else value + part
        hidden[pl.ds(i * big.span + 1, big.span)] = value.astype(BF16).reshape(
            big.span, big.width, 2 * nm
        )
        return carry

    lax.fori_loop(0, big.high // big.span, input_tile, 0)
    hidden_copy = pair_copy(hidden.at[map_rows, :, away_m], r["dhm_in"], r["pair"].at[5])
    hidden_copy.start()
    send(2)
    complete(total_share)

    own_scale = own_key_scale()
    query_weight = weight_col / totals_col

    def row_terms(i, acc):
        for k in range(several):
            d = i * several + k
            block, raw, key_scale, scale, allowed = scores(d, own_scale)
            index = split_index(dims, d)
            total_row = key_totals[index[0], index[1], index[2]][0:1]
            value = jnp.where(allowed, jnp.exp(raw * scale), 0.0)
            key_count = jnp.full((1, 1), r["counts"][d], I32).astype(F32)
            query = value * query_weight
            key = value * live_col * (share / key_count / total_row)
            query_low = (query * scale).astype(BF16)
            key_low = (key * scale).astype(BF16)
            mine = jnp.where(model == 0, block[0].astype(F32), block[1].astype(F32)).astype(BF16)
            acc = (
                acc[0] + dot(query_low, mine, NN) + dot(key_low, mine, NN),
                acc[1]
                + jnp.sum((query + key) * raw * key_scale / CONTRAST_TEMP, axis=1, keepdims=True),
            )
        return acc

    row_sum, scale_sum = lax.fori_loop(
        0, images // several, row_terms, (jnp.zeros((SLOTS, nm), F32), jnp.zeros((SLOTS, 1), F32))
    )
    norm_grad = -0.5 * own_scale * own_scale * own_scale * scale_sum
    row_grad = row_sum + 2.0 * kernel_rows.astype(F32) * norm_grad
    row_grad = row_grad + jnp.concatenate(
        [logit_rows, jnp.zeros((SLOTS - high_slots, nm), F32)], axis=0
    )
    row_low = row_grad.astype(BF16)
    for t in range(9):
        value = dot(patches[:, t * depth : (t + 1) * depth], row_low, TN)
        into = totals[3].at[..., t * nm : (t + 1) * nm]
        into[...] = value.reshape(into.shape)
    send_first(3)
    send(2)
    send(4)

    for i in range(small.high // small.span):
        at = lax.broadcasted_iota(I32, (gtile, SLOTS), 0) + i * gtile
        for dv in range(3):
            chosen = (at == cells_row + (dv - 1)).astype(F32).astype(BF16)
            dg2[1 + i * small.span : 1 + (i + 1) * small.span, :, dv * nm : (dv + 1) * nm] = (
                dot(chosen, row_low, NN).astype(BF16).reshape(small.span, pad, nm)
            )
    hidden_grid = hg

    def grid_input_tile(i, carry):
        value = None
        for du in range(3):
            first = i * small.span + 2 - du
            part = dot(take(dg2, first, small.span, slice(0, 3 * nm)), grid_two(du), NT) + dot(
                take(dg2, first, small.span, slice(3 * nm, 3 * nm + 128)), class_two(du), NT
            )
            value = part if value is None else value + part
        hidden_grid[pl.ds(i * small.span + 1, small.span)] = value.astype(BF16).reshape(
            small.span, pad, 2 * ng
        )
        return carry

    lax.fori_loop(0, small.high // small.span, grid_input_tile, 0)
    hidden_grid_copy = pair_copy(
        hidden_grid.at[grid_span, :, away_g], r["dhg_in"], r["pair"].at[6]
    )
    hidden_grid_copy.start()
    send(2)

    hidden_grid_copy.wait()
    hidden_grid_in = r["dhg_in"]

    def both_grid_halves(i):
        mine = take(hidden_grid, i * small.part + 1, small.part, own_g)
        return mine.astype(F32) + take(hidden_grid_in, i * small.part, small.part).astype(F32)

    gain_grid, bias_grid = norm_backward(
        small, xhg, both_grid_halves, r["spare_g"], dg1, spread_g, row(gnorms, 0),
        row(gnorms, 1), scale_grid,
    )
    send(3)
    weight_gradient(small, xg, dg1, totals[1], slice(0, 3 * ng))
    send_first(1)
    send(3)
    hidden_copy.wait()
    hidden_in = r["dhm_in"]

    def both_halves(i):
        mine = take(hidden, i * big.part + 1, big.part, own_m)
        return mine.astype(F32) + take(hidden_in, i * big.part, big.part).astype(F32)

    gain_one, bias_one = norm_backward(
        big, xh1, both_halves, r["spare"], dm, spread_m, row(norms, 0), row(norms, 1), scale_one
    )

    pieces = [gain_one, bias_one, gain_two, bias_two]
    pieces += [gain_grid[:, i : i + nm] for i in range(0, ng, nm)]
    pieces += [bias_grid[:, i : i + nm] for i in range(0, ng, nm)]
    pieces += [class_bias_sum]
    pieces += [jnp.zeros((1, 128), F32)] * (16 - len(pieces))
    small_plane, small_line = r["small_plane"], r["small_line"]
    small_plane[pos[1], pos[2]] = jnp.concatenate(pieces, axis=0)

    def plane_total(plane, cores):
        value = None
        for y in range(dims[1]):
            for x in range(dims[2]):
                for core in range(2) if cores else (None,):
                    part = plane[y, x] if core is None else plane[y, x, core]
                    value = part if value is None else value + part
        return value

    def line_total(line):
        value = line[0]
        for z in range(1, dims[0]):
            value = value + line[z]
        return value

    def small_sum_here():
        small_line[pos[0]] = plane_total(small_plane, False)

    small_share = plane_exchange(
        dims, small_plane.at[pos[1], pos[2]], small_line.at[pos[0]], False, small_sum_here,
        r["ss"], r["sr"],
    )
    advance(small_share)

    def each(du):
        send_tap_row(du)
        if du == 1:
            advance(small_share)
            send(1)
        if du == 2:
            send(3)

    weight_gradient(big, xm, dm, totals[0], slice(0, 3 * nm), each)
    last_group = out_groups[0] if fused else []
    advance(*last_group[:2])
    send(1)
    advance(*last_group[2:])
    complete(small_share)
    small_sum = line_total(small_line)
    r["small_out"][...] = small_sum
    first_model = (model == 0).astype(F32)
    loss = jnp.sum(focal_sum, keepdims=True) + first_model * (dice_sum + contrast_sum)
    if fused:
        squares = (own_image == 0).astype(F32) * jnp.sum(small_sum * small_sum, keepdims=True)

        def hand_out(i):
            complete(*out_groups[i])
            value = totals[i][pos[0], pos[1], pos[2]]
            r["out%d" % i][...] = value
            return jnp.sum(value * value, keepdims=True)

        squares += hand_out(2)
        squares += hand_out(4)
        send(0)
        squares += hand_out(3)
        send(0)
        squares += hand_out(1)
        squares += hand_out(0)
        sum_plane, sum_line = r["sum_plane"], r["sum_line"]
        at = lax.broadcasted_iota(I32, (8, 128), 0)
        sum_plane[pos[1], pos[2], model] = jnp.where(at == 0, squares, loss)

        def sums_here():
            sum_line[pos[0]] = plane_total(sum_plane, True)

        sum_share = plane_exchange(
            dims, sum_plane.at[pos[1], pos[2], model], sum_line.at[pos[0]], True, sums_here,
            r["us"], r["ur"],
        )
        complete(sum_share)
        r["sum_out"][...] = line_total(sum_line)
        sum_share.drain()
    else:
        r["sum_out"][...] = jnp.broadcast_to(loss, (8, 128))
    for shared in kernel_share + [kernel_cores, total_share, small_share]:
        shared.drain()
    for group in out_groups:
        for exchange in group:
            exchange.drain()


def run_step(cfg, inputs, weights, blocks):
    dims, fused = cfg["dims"], cfg["fused"]
    big, small = cfg["mask_map"], cfg["grid_map"]
    nm, ng = big.channels, small.channels
    rows, grid_rows = big.high * big.width, small.high * small.width
    inputs = dict(inputs, **weights)
    spaces = dict(xm_own=ANY, xg_own=ANY, masks=ANY, counts=pltpu.SMEM)
    names = list(inputs)
    specs = [pl.BlockSpec(memory_space=spaces.get(name, VMEM)) for name in names]
    outs = {"small_out": ((16, 128), F32), "sum_out": ((8, 128), F32)}
    scratch = {}
    if fused:
        for i, shape in enumerate(blocks):
            outs["out%d" % i] = (shape[3:], F32)
            scratch["w%d" % i] = VMEM(shape, BF16)
            scratch["g%d" % i] = VMEM(shape, F32)
        gather_cuts = [lane_cuts(shape[-1]) for shape in blocks]
        cuts = [tap_row_cuts(blocks[0][-1])] + gather_cuts[1:]
        lands = landing_scratch(dims, blocks, cuts)
        cfg = dict(cfg, lands=len(lands), cuts=cuts)
        for i, land in enumerate(lands):
            scratch["land%d" % i] = land
        for names_of, used in ((("gs", "gr"), gather_cuts), (("rs", "rr"), cuts)):
            for name in names_of:
                scratch[name] = DMA((flow_slots(dims, used),))
        scratch["class_stage"] = VMEM(blocks[4], BF16)
        scratch["second_stage"] = VMEM(blocks[3], BF16)
        scratch["sum_plane"] = VMEM(dims[1:] + (2, 8, 128), F32)
        scratch["sum_line"] = VMEM(dims[:1] + (8, 128), F32)
        scratch["us"], scratch["ur"] = plane_sems(dims)
    else:
        for i in range(5):
            outs["g%d" % i] = (inputs["w%d" % i].shape, F32)
    c_in = 2 * inputs["xm_own"].shape[3]
    depth = 2 * ng
    slot_rows = -(-inputs["masks"].shape[0] // 16) * 16

    def padded(m, channels):
        return VMEM((m.high + 2, m.width, channels), BF16)

    scratch.update(
        xm=padded(big, c_in),
        xg=padded(small, c_in),
        xh1=VMEM((rows, nm), F32),
        hm=padded(big, 2 * nm),
        xhg=VMEM((grid_rows, ng), F32),
        hg=padded(small, depth),
        xh2=VMEM((rows, nm), F32),
        feature=VMEM((rows, nm), BF16),
        patches=VMEM((SLOTS, 9 * depth), BF16),
        kernels=VMEM(dims + (2, SLOTS, nm), BF16),
        logits=VMEM((slot_rows, rows), BF16),
        logits_in=VMEM((slot_rows, rows), BF16),
        key_totals=VMEM(dims + (8, SLOTS), F32),
        dm=padded(big, 3 * nm),
        spare=VMEM((rows, nm), F32),
        dhm_in=VMEM((big.high, big.width, nm), BF16),
        dg2=padded(small, 3 * nm + 128),
        dhg_in=VMEM((small.high, small.width, ng), BF16),
        dg1=padded(small, 3 * ng),
        spare_g=VMEM((grid_rows, ng), F32),
        small_plane=VMEM(dims[1:] + (16, 128), F32),
        small_line=VMEM(dims[:1] + (16, 128), F32),
        table=VMEM((8, SLOTS), I32),
        bias_table=VMEM((8, 128), F32),
        local=DMA((3,)),
        mask_bits=VMEM((inputs["masks"].shape[0], rows), I32),
        pair=DMA((8, 2)),
    )
    scratch["ks"], scratch["kr"] = share_sems(dims, 2)
    for a, b in (("ls", "lr"), ("ss", "sr")):
        scratch[a], scratch[b] = plane_sems(dims)
    names += list(outs) + list(scratch)
    result = pl.pallas_call(
        partial(step_kernel, cfg, tuple(names)),
        name="step",
        out_shape=[jax.ShapeDtypeStruct(s, d) for s, d in outs.values()],
        in_specs=specs,
        out_specs=[pl.BlockSpec(memory_space=VMEM)] * len(outs),
        scratch_shapes=list(scratch.values()),
        compiler_params=params(0),
    )(*inputs.values())
    return dict(zip(outs, result))


def update_kernel(nm, ng, kc, *refs):
    reduced, small, sums = refs[:5], refs[5], refs[6]
    states, outs = refs[7:28], refs[28:]
    total = sums[0:1, 0:1]
    norm = jnp.sqrt(total)
    outs[0][...] = sums[1:2, 0:1]
    outs[1][...] = norm
    factor = jnp.minimum(1.0, CLIP_LIMIT / norm)

    def update(which, index, gradient, rate):
        old = [states[3 * which + k][index] for k in range(3)]
        new = adam_update(*old, gradient * factor, rate)
        for k in range(3):
            outs[2 + 3 * which + k][index] = new[k]

    for t in range(9):
        update(0, (0, t), reduced[0][:, t * nm : (t + 1) * nm], LEARN_RATE)
        update(0, (1, t), reduced[2][:, t * nm : (t + 1) * nm], LEARN_RATE)
        update(1, (t,), reduced[1][:, t * ng : (t + 1) * ng], LEARN_RATE)
        update(2, (t,), reduced[3][:, t * nm : (t + 1) * nm], LEARN_RATE)
        at = t // 3 * 128 + t % 3 * kc
        update(3, (t,), reduced[4][:, at : at + kc], LEARN_RATE)
    update(4, (slice(None),), small[0:4, :], SMALL_RATE)
    per = ng // nm
    for k in range(2):
        pieces = [small[4 + k * per + i : 5 + k * per + i, :] for i in range(per)]
        update(5, (slice(k, k + 1),), jnp.concatenate(pieces, axis=1), SMALL_RATE)
    at = 4 + 2 * per
    update(6, (slice(None),), small[at : at + 1, :kc], SMALL_RATE)


def run_update(nm, ng, kc, reduced, small, sums, states):
    args = list(reduced) + [small, sums] + list(states)
    shapes = [jax.ShapeDtypeStruct((1, 1), F32)] * 2
    shapes += [jax.ShapeDtypeStruct(s.shape, F32) for s in states]
    return pl.pallas_call(
        partial(update_kernel, nm, ng, kc),
        name="update",
        out_shape=shapes,
        in_specs=[pl.BlockSpec(memory_space=VMEM)] * len(args),
        out_specs=[pl.BlockSpec(memory_space=VMEM)] * len(shapes),
        compiler_params=pltpu.CompilerParams(vmem_limit_bytes=VMEM_LIMIT),
    )(*args)


def lanes_of_taps(weight):
    taps, depth, width = weight.shape
    return weight.transpose(1, 0, 2).reshape(depth, taps * width)


def class_lanes(weight):
    _, depth, width = weight.shape
    rows = weight.transpose(1, 0, 2).reshape(depth, 3, 3 * width)
    return jnp.pad(rows, ((0, 0), (0, 0), (0, 128 - 3 * width))).reshape(depth, 384)


def adam_update(weight, moment, square, gradient, rate):
    moment_new = BETA_ONE * moment + (1.0 - BETA_ONE) * gradient
    square_new = BETA_TWO * square + (1.0 - BETA_TWO) * gradient * gradient
    moment_hat = moment_new / (1.0 - BETA_ONE**STEP_TIME)
    square_hat = square_new / (1.0 - BETA_TWO**STEP_TIME)
    weight_new = weight - rate * (
        moment_hat / (jnp.sqrt(square_hat) + ADAM_EPS) + WEIGHT_DECAY * weight
    )
    return (weight_new, moment_new, square_new)


def body(
    mask_features,
    grid_features,
    instance_cells,
    instance_counts,
    instance_labels,
    instance_masks,
    *states,
):
    images = lax.axis_size("dp")
    data_index = lax.axis_index("dp")
    dims = line_lengths(images)
    mask_convs, grid_first, grid_second, class_conv = states[0:12:3]
    mask_norms, grid_norms, class_bias = states[12::3]
    _, high, wide, half = mask_features.shape
    grid = grid_features.shape[1]
    pad = -(-(grid + 1) // 16) * 16
    nm, ng, kc = mask_convs.shape[3], grid_first.shape[2], class_conv.shape[2]
    fused = grid_first.shape[1] % 16 == 0
    cfg = dict(
        dims=dims,
        images=images,
        mask_map=Map(high, wide, wide, 8, 4, nm, 2 * nm // GROUPS),
        grid_map=Map(grid, pad, grid, grid // 2, grid // 2, ng, 2 * ng // GROUPS),
        kc=kc,
        fused=fused,
    )
    inputs = dict(
        xm_own=mask_features,
        xg_own=grid_features,
        masks=instance_masks.transpose(1, 0, 2),
        counts=instance_counts,
        cells=instance_cells,
        labels=instance_labels,
        mask_norms=mask_norms,
        grid_norms=grid_norms,
        class_bias=class_bias[None, :],
    )
    if fused:
        weights = dict(
            mask_convs=mask_convs,
            grid_first=grid_first,
            grid_second=grid_second,
            class_conv=class_conv,
        )
        blocks = [
            dims + (mask_convs.shape[2], 9 * nm),
            dims + (grid_first.shape[1], 9 * ng),
            dims + (mask_convs.shape[2], 9 * nm),
            dims + (grid_second.shape[1], 9 * nm),
            dims + (class_conv.shape[1], 384),
        ]
        out = run_step(cfg, inputs, weights, blocks)
        reduced = [out["out%d" % i] for i in range(5)]
        sums = out["sum_out"]
    else:
        shards = [
            lanes_of_taps(mask_convs[0].astype(BF16)),
            lanes_of_taps(grid_first.astype(BF16)),
            lanes_of_taps(mask_convs[1].astype(BF16)),
            lanes_of_taps(grid_second.astype(BF16)),
            class_lanes(class_conv.astype(BF16)),
        ]
        gathered = gather_all(dims, shards)
        weights = {"w%d" % i: b.reshape(-1, b.shape[-1]) for i, b in enumerate(gathered)}
        out = run_step(cfg, inputs, weights, None)
        reduced = reduce_all(
            dims, [out["g%d" % i].reshape(b.shape) for i, b in enumerate(gathered)]
        )
        squares = sum(jnp.sum(jnp.square(value)) for value in reduced)
        squares += (data_index == 0).astype(F32) * jnp.sum(jnp.square(out["small_out"]))
        pair = lax.psum((squares, out["sum_out"][0, 0]), ("dp", "mp"))
        sums = jnp.broadcast_to(jnp.pad(jnp.stack(pair), (0, 6))[:, None], (8, 128))
    states = states[:18] + tuple(state[None, :] for state in states[18:])
    result = run_update(nm, ng, kc, reduced, out["small_out"], sums, states)
    result = [value.reshape(()) for value in result[:2]] + list(result[2:])
    return tuple(result[:20]) + tuple(value[0] for value in result[20:])


def solution(mesh):
    in_specs = (
        P("dp", None, None, "mp"),
        P("dp", None, None, "mp"),
        P("dp", None),
        P(),
        P("dp", None),
        P("dp", None, None),
        P(None, None, "dp", "mp"),
        P(None, None, "dp", "mp"),
        P(None, None, "dp", "mp"),
        P(None, "dp", "mp"),
        P(None, "dp", "mp"),
        P(None, "dp", "mp"),
        P(None, "dp", "mp"),
        P(None, "dp", "mp"),
        P(None, "dp", "mp"),
        P(None, "dp", "mp"),
        P(None, "dp", "mp"),
        P(None, "dp", "mp"),
        P(None, "mp"),
        P(None, "mp"),
        P(None, "mp"),
        P(None, "mp"),
        P(None, "mp"),
        P(None, "mp"),
        P("mp"),
        P("mp"),
        P("mp"),
    )
    out_specs = (
        P(),
        P(),
        P(None, None, "dp", "mp"),
        P(None, None, "dp", "mp"),
        P(None, None, "dp", "mp"),
        P(None, "dp", "mp"),
        P(None, "dp", "mp"),
        P(None, "dp", "mp"),
        P(None, "dp", "mp"),
        P(None, "dp", "mp"),
        P(None, "dp", "mp"),
        P(None, "dp", "mp"),
        P(None, "dp", "mp"),
        P(None, "dp", "mp"),
        P(None, "mp"),
        P(None, "mp"),
        P(None, "mp"),
        P(None, "mp"),
        P(None, "mp"),
        P(None, "mp"),
        P("mp"),
        P("mp"),
        P("mp"),
    )
    return jax.shard_map(body, mesh=mesh, in_specs=in_specs, out_specs=out_specs, check_vma=False)
```

```python
from functools import partial

import jax
import jax.numpy as jnp
from jax import lax
from jax.experimental import pallas as pl
from jax.experimental.pallas import tpu as pltpu
from jax.sharding import PartitionSpec as P

GROUPS = 32
GN_EPS = 1e-05
CLIP_LIMIT = 0.02
LEARN_RATE = 0.02
SMALL_RATE = 0.5
BETA_ONE = 0.9
BETA_TWO = 0.95
ADAM_EPS = 1e-08
WEIGHT_DECAY = 0.05
CONTRAST_TEMP = 0.05
FOCAL_ALPHA = 0.25
DICE_WEIGHT = 3.0
STEP_TIME = 10.0
HIGHEST = lax.Precision.HIGHEST

MESH = pl.DeviceIdType.MESH
VMEM = pltpu.VMEM
ANY = pl.ANY
VMEM_LIMIT = 67043328
F32 = jnp.float32
BF16 = jnp.bfloat16
I32 = jnp.int32
SLOTS = 128
DMA = pltpu.SemaphoreType.DMA


def line_lengths(total):
    if total & (total - 1):
        return (total, 1, 1)
    bits = total.bit_length() - 1
    last = bits // 3
    middle = (bits - last) // 2
    return (1 << (bits - last - middle), 1 << middle, 1 << last)


def place(dims):
    index = lax.axis_index("dp")
    return (index // (dims[1] * dims[2]), (index // dims[2]) % dims[1], index % dims[2])


def split_index(dims, index):
    return (
        index // (dims[1] * dims[2]),
        lax.rem(index // dims[2], dims[1]),
        lax.rem(index, dims[2]),
    )


def along(dims, axis, step):
    stride = (dims[1] * dims[2], dims[2], 1)[axis]
    return {"dp": lax.axis_index("dp") + step * stride}


def partner():
    return {"mp": 1 - lax.axis_index("mp")}


def ring_step(dims, pos, axis, offset):
    other = lax.rem(pos[axis] + offset, dims[axis])
    return along(dims, axis, other - pos[axis])


def plane_peers(dims, cores):
    pos = place(dims)
    model = lax.axis_index("mp")
    peers = []
    for y in range(dims[1]):
        for x in range(dims[2]):
            for core in range(2 if cores else 1):
                if y == x == core == 0:
                    continue
                at = (pos[0] * dims[1] + lax.rem(pos[1] + y, dims[1])) * dims[2]
                peer = {"dp": at + lax.rem(pos[2] + x, dims[2])}
                if core:
                    peer["mp"] = 1 - model
                peers.append(peer)
    return peers


def greet_start(dims):
    sem = pltpu.get_barrier_semaphore()
    pos = place(dims)
    peers = plane_peers(dims, True)
    peers += [ring_step(dims, pos, 0, offset) for offset in range(1, dims[0])]
    for peer in peers:
        pl.semaphore_signal(sem, inc=1, device_id=peer, device_id_type=MESH)
    return sem, len(peers)


def greet_end(sem, count):
    pl.semaphore_wait(sem, count)


def greet(dims):
    greet_end(*greet_start(dims))


GATHER_ORDERS = ((2, 1, 0), (0, 2, 1), (0, 1, 2))
REDUCE_ORDERS = tuple(tuple(reversed(order)) for order in GATHER_ORDERS)


def line_copies(dims):
    return sum(n - 1 for n in dims)


def lane_cuts(width):
    tiles = width // 128
    if width % 128 or tiles < 3:
        return ((0, 0, width),)
    first = max(1, round(tiles * 0.17))
    second = (tiles - first) // 2
    sizes = (first, second, tiles - first - second)
    cuts, start = [], 0
    for order, size in enumerate(sizes):
        cuts.append((order, start * 128, size * 128))
        start += size
    return tuple(cuts)


def tap_row_cuts(width):
    third = width // 3
    if third % 384:
        return lane_cuts(width)
    near = third // 384 * 128
    return ((2, 0, third), (1, third, third), (1, 2 * third, near), (2, 2 * third + near, 2 * near))


class Exchange:
    def __init__(self):
        self.stages, self.lands, self.next = [], [], 0

    def finish(self):
        if 0 < self.next <= len(self.stages):
            for copy in self.stages[self.next - 1]:
                copy.wait_recv()
            self.lands[self.next - 1]()

    def start(self):
        if self.next < len(self.stages):
            for copy in self.stages[self.next]:
                copy.start()
        self.next += 1

    def drain(self):
        for stage in self.stages:
            for copy in stage:
                copy.wait_send()


def advance(*exchanges):
    for exchange in exchanges:
        exchange.finish()
    for exchange in exchanges:
        exchange.start()


def complete(*exchanges):
    while any(e.next <= len(e.stages) for e in exchanges):
        advance(*exchanges)


def nothing():
    return None


def gather_exchange(dims, out, send_sems, recv_sems, base, lanes, order, tail=None):
    pos = place(dims)
    result, done = Exchange(), set()
    tail = (slice(None), lanes) if tail is None else tail
    for axis in order:
        view = out.at[tuple(pl.ds(0, dims[k]) if k in done else pos[k] for k in range(3)) + tail]
        copies = []
        for offset in range(1, dims[axis]):
            copies.append(
                pltpu.make_async_remote_copy(
                    src_ref=view,
                    dst_ref=view,
                    send_sem=send_sems.at[base],
                    recv_sem=recv_sems.at[base],
                    device_id=ring_step(dims, pos, axis, offset),
                    device_id_type=MESH,
                )
            )
            base += 1
        if copies:
            result.stages.append(copies)
            result.lands.append(nothing)
        done.add(axis)
    return result


def remote(view, send_sem, recv_sem, device):
    return pltpu.make_async_remote_copy(
        src_ref=view,
        dst_ref=view,
        send_sem=send_sem,
        recv_sem=recv_sem,
        device_id=device,
        device_id_type=MESH,
    )


def core_exchange(out, sems):
    result = Exchange()
    view = out.at[:, :, :, lax.axis_index("mp")]
    result.stages.append([remote(view, sems.at[0], sems.at[1], partner())])
    result.lands.append(nothing)
    return result


def plane_slots(dims):
    return 2 * dims[1] * dims[2] + dims[0]


def plane_sems(dims):
    return [DMA((plane_slots(dims),)), DMA((plane_slots(dims),))]


def plane_exchange(dims, view, line_view, cores, land, send_sems, recv_sems):
    result, pos = Exchange(), place(dims)
    first = [
        remote(view, send_sems.at[i], recv_sems.at[i], peer)
        for i, peer in enumerate(plane_peers(dims, cores))
    ]
    base = len(first)
    second = [
        remote(
            line_view,
            send_sems.at[base + offset - 1],
            recv_sems.at[base + offset - 1],
            ring_step(dims, pos, 0, offset),
        )
        for offset in range(1, dims[0])
    ]
    result.stages, result.lands = [first, second], [land, nothing]
    return result


def landing_shapes(dims, rows, width, order):
    shapes, left = [], {0, 1, 2}
    for axis in order:
        left = left - {axis}
        shapes.append(
            (max(1, dims[axis] - 1),) + tuple(dims[k] for k in sorted(left)) + (rows, width)
        )
    return shapes


def reduce_exchange(dims, total, staged, lands, send_sems, recv_sems, base, lanes, order):
    pos = place(dims)
    result = Exchange()
    axes = [axis for axis in order if dims[axis] > 1]

    def over_blocks(free, inner, body):
        outer = [k for k in free if k != inner]
        count = 1
        for k in outer:
            count *= dims[k]

        def step(i, carry):
            where, rest = {}, i
            for k in reversed(outer):
                where[k] = lax.rem(rest, dims[k])
                rest = rest // dims[k]
            for offset in range(dims[inner] if inner is not None else 1):
                here = dict(where)
                if inner is not None:
                    here[inner] = lax.rem(pos[inner] + offset, dims[inner])
                body(here, offset)
            return carry

        if count == 1:
            step(jnp.int32(0), 0)
        else:
            lax.fori_loop(0, count, step, 0)

    def index_of(where):
        return tuple(where.get(k, pos[k]) for k in range(3)) + (slice(None), lanes)

    def prepare():
        def cast(where, offset):
            if offset:
                staged[index_of(where)] = total[index_of(where)].astype(BF16)

        over_blocks(axes, axes[0], cast)

    result.prepare = prepare
    for stage, axis in enumerate(axes):
        n = dims[axis]
        free = axes[stage + 1 :]
        inner = free[0] if free else None
        copies = []
        for offset in range(1, n):
            view = tuple(
                lax.rem(pos[axis] + offset, n)
                if k == axis
                else (pl.ds(0, dims[k]) if k in free else pos[k])
                for k in range(3)
            )
            copies.append(
                pltpu.make_async_remote_copy(
                    src_ref=staged.at[view + (slice(None), lanes)],
                    dst_ref=lands[order.index(axis)].at[offset - 1],
                    send_sem=send_sems.at[base],
                    recv_sem=recv_sems.at[base],
                    device_id=ring_step(dims, pos, axis, offset),
                    device_id_type=MESH,
                )
            )
            base += 1

        def land(axis=axis, n=n, free=free, inner=inner):
            arrived = lands[order.index(axis)]
            left = sorted(free + [k for k in range(3) if dims[k] == 1 and k in later(axis)])

            def add(where, offset):
                index = index_of(where)
                value = total[index]
                for k in range(n - 1):
                    lead = tuple(where.get(j, 0) for j in left)
                    value = value + arrived[(k,) + lead].astype(F32)
                if offset:
                    staged[index] = value.astype(BF16)
                else:
                    total[index] = value

            over_blocks(free, inner, add)

        def later(axis):
            return order[order.index(axis) + 1 :]

        result.stages.append(copies)
        result.lands.append(land)
    return result


def share_sems(dims, pieces):
    return [DMA((pieces * line_copies(dims),)), DMA((pieces * line_copies(dims),))]


def pair_copy(source, target, sems):
    return pltpu.make_async_remote_copy(
        src_ref=source,
        dst_ref=target,
        send_sem=sems.at[0],
        recv_sem=sems.at[1],
        device_id=partner(),
        device_id_type=MESH,
    )


def params(collective_id):
    return pltpu.CompilerParams(
        collective_id=collective_id, has_side_effects=True, vmem_limit_bytes=VMEM_LIMIT
    )


def gather_groups(dims, outs, send_sems, recv_sems):
    groups, base = [], 0
    for out in outs:
        group = []
        for order, start, size in lane_cuts(out.shape[4]):
            group.append(
                gather_exchange(
                    dims, out, send_sems, recv_sems, base, pl.ds(start, size), GATHER_ORDERS[order]
                )
            )
            base += line_copies(dims)
        groups.append(group)
    return groups


def reduce_groups(dims, totals, staged, lands, send_sems, recv_sems, cuts):
    groups, base, lands = [], 0, list(lands)
    for total, stage, cut in zip(totals, staged, cuts):
        group = []
        for order, start, size in cut:
            group.append(
                reduce_exchange(
                    dims,
                    total,
                    stage,
                    lands[:3],
                    send_sems,
                    recv_sems,
                    base,
                    pl.ds(start, size),
                    REDUCE_ORDERS[order],
                )
            )
            lands = lands[3:]
            base += line_copies(dims)
        groups.append(group)
    return groups


def flow_slots(dims, cuts):
    return max(1, line_copies(dims) * sum(len(cut) for cut in cuts))


def landing_scratch(dims, shapes, cuts):
    scratch = []
    for shape, cut in zip(shapes, cuts):
        for order, _, size in cut:
            for land in landing_shapes(dims, shape[-2], size, REDUCE_ORDERS[order]):
                scratch.append(VMEM(land, BF16))
    return scratch


def run_all(groups):
    exchanges = [exchange for group in groups for exchange in group]
    complete(*exchanges)
    for exchange in exchanges:
        exchange.drain()


def gather_kernel(dims, count, *refs):
    shards, outs = refs[:count], refs[count : 2 * count]
    send_sems, recv_sems, local_sems = refs[2 * count :]
    pos = place(dims)
    local = [
        pltpu.make_async_copy(shards[i], outs[i].at[pos[0], pos[1], pos[2]], local_sems.at[i])
        for i in range(count)
    ]
    for copy in local:
        copy.start()
    greet(dims)
    for copy in local:
        copy.wait()
    run_all(gather_groups(dims, outs, send_sems, recv_sems))


def gather_all(dims, shards):
    count = len(shards)
    shapes = [dims + s.shape for s in shards]
    slots = flow_slots(dims, [lane_cuts(s[-1]) for s in shapes])
    return pl.pallas_call(
        partial(gather_kernel, dims, count),
        name="gather_weights",
        out_shape=[jax.ShapeDtypeStruct(s, BF16) for s in shapes],
        in_specs=[pl.BlockSpec(memory_space=VMEM)] * count,
        out_specs=[pl.BlockSpec(memory_space=VMEM)] * count,
        scratch_shapes=[DMA((slots,)), DMA((slots,)), DMA((count,))],
        compiler_params=params(1),
    )(*shards)


def reduce_kernel(dims, count, *refs):
    parts, outs = refs[:count], refs[count : 2 * count]
    send_sems, recv_sems, local_sems = refs[2 * count : 2 * count + 3]
    rest = list(refs[2 * count + 3 :])
    totals, staged, lands = rest[:count], rest[count : 2 * count], rest[2 * count :]
    pos = place(dims)
    local = [pltpu.make_async_copy(parts[i], totals[i], local_sems.at[i]) for i in range(count)]
    for copy in local:
        copy.start()
    greet(dims)
    for i in range(count):
        local[i].wait()
    cuts = [lane_cuts(total.shape[4]) for total in totals]
    groups = reduce_groups(dims, totals, staged, lands, send_sems, recv_sems, cuts)
    for group in groups:
        for exchange in group:
            exchange.prepare()
    run_all(groups)
    for i in range(count):
        outs[i][...] = totals[i][pos[0], pos[1], pos[2]]


def reduce_all(dims, parts):
    count = len(parts)
    shapes = [p.shape for p in parts]
    cuts = [lane_cuts(s[-1]) for s in shapes]
    slots = flow_slots(dims, cuts)
    scratch = [DMA((slots,)), DMA((slots,)), DMA((count,))]
    scratch += [VMEM(s, F32) for s in shapes] + [VMEM(s, BF16) for s in shapes]
    scratch += landing_scratch(dims, shapes, cuts)
    return pl.pallas_call(
        partial(reduce_kernel, dims, count),
        name="reduce_gradients",
        out_shape=[jax.ShapeDtypeStruct(s[3:], F32) for s in shapes],
        in_specs=[pl.BlockSpec(memory_space=ANY)] * count,
        out_specs=[pl.BlockSpec(memory_space=VMEM)] * count,
        scratch_shapes=scratch,
        compiler_params=params(2),
    )(*parts)


def group_sums(row, spread):
    width = row.shape[1]
    return lax.dot_general(
        jnp.broadcast_to(row, (8, width)),
        spread,
        (((1,), (0,)), ((), ())),
        precision=HIGHEST,
        preferred_element_type=F32,
    )[0:1]


def group_spread(width, group):
    rows = lax.broadcasted_iota(I32, (width, width), 0) // group
    cols = lax.broadcasted_iota(I32, (width, width), 1) // group
    return (rows == cols).astype(F32)


def dot(a, b, contract):
    return lax.dot_general(a, b, ((contract[0], contract[1]), ((), ())), preferred_element_type=F32)


NN = ((1,), (0,))
NT = ((1,), (1,))
TN = ((0,), (0,))


class Map:
    def __init__(self, high, width, live, span, part, channels, group):
        self.high, self.width, self.live = high, width, live
        self.span, self.part, self.channels = span, part, channels
        self.pixels = float(high * live * group)

    def column(self, span):
        shape = (span, self.width, self.channels)
        return lax.broadcasted_iota(I32, shape, 1).reshape(span * self.width, self.channels)

    def masked(self, value, span):
        if self.live == self.width:
            return value
        return jnp.where(self.column(span) < self.live, value, 0.0)

    def at(self, i, span):
        return pl.ds(pl.multiple_of(i * span * self.width, 16), span * self.width)


def take(source, first, count, lanes=slice(None)):
    value = source[pl.ds(first, count), :, lanes]
    return value.reshape(-1, value.shape[2])


def conv_forward(m, source, weight, raw, first=0, last=None, total=None):
    n, tile = m.channels, m.span * m.width

    def body(i, total):
        wide = None
        for du in range(3):
            part = dot(take(source, i * m.span + du, m.span), weight(du), NN)
            wide = part if wide is None else wide + part
        left = pltpu.roll(wide[:, :n], 1, 0)
        right = pltpu.roll(wide[:, 2 * n :], tile - 1, 0)
        if m.live == m.width:
            column = m.column(m.span)
            left = jnp.where(column == 0, 0.0, left)
            right = jnp.where(column == m.width - 1, 0.0, right)
        value = m.masked(left + wide[:, n : 2 * n] + right, m.span)
        raw[m.at(i, m.span), :] = value
        return total + jnp.sum(value, axis=0, keepdims=True)

    last = m.high // m.span if last is None else last
    total = jnp.zeros((1, n), F32) if total is None else total
    return lax.fori_loop(first, last, body, total)


def norm_forward(m, raw, total, spread, gain, bias, store):
    n, part = m.channels, m.part
    mean = group_sums(total, spread) / m.pixels

    def spread_of(i, acc):
        away = m.masked(raw[m.at(i, part), :] - mean, part)
        return acc + jnp.sum(away * away, axis=0, keepdims=True)

    squares = lax.fori_loop(0, m.high // part, spread_of, jnp.zeros((1, n), F32))
    scale = lax.rsqrt(group_sums(squares, spread) / m.pixels + GN_EPS)

    def normalize(i, carry):
        normed = (raw[m.at(i, part), :] - mean) * scale
        raw[m.at(i, part), :] = normed
        value = m.masked(jnp.maximum(normed * gain + bias, 0.0), part)
        store(i, value.astype(BF16))
        return carry

    lax.fori_loop(0, m.high // part, normalize, 0)
    return scale


def norm_backward(m, normed, upstream, spare, shifted, spread, gain, bias, scale):
    n, part = m.channels, m.part
    tile = part * m.width

    def first(i, sums):
        here = normed[m.at(i, part), :]
        value = m.masked(jnp.where(here * gain + bias > 0.0, upstream(i), 0.0), part)
        spare[m.at(i, part), :] = value
        return (
            sums[0] + jnp.sum(value * here, axis=0, keepdims=True),
            sums[1] + jnp.sum(value, axis=0, keepdims=True),
        )

    zero = jnp.zeros((1, n), F32)
    gain_sum, bias_sum = lax.fori_loop(0, m.high // part, first, (zero, zero))
    level = group_sums(bias_sum * gain, spread) / m.pixels
    slope = group_sums(gain_sum * gain, spread) / m.pixels

    def second(i, carry):
        value = scale * (spare[m.at(i, part), :] * gain - level - normed[m.at(i, part), :] * slope)
        value = m.masked(value, part)
        left = pltpu.roll(value, tile - 1, 0)
        right = pltpu.roll(value, 1, 0)
        if m.live == m.width:
            column = m.column(part)
            left = jnp.where(column == m.width - 1, 0.0, left)
            right = jnp.where(column == 0, 0.0, right)
        into = pl.ds(i * part + 1, part)
        for k, piece in enumerate((left, value, right)):
            shifted[into, :, k * n : (k + 1) * n] = piece.astype(BF16).reshape(part, m.width, n)
        return carry

    lax.fori_loop(0, m.high // part, second, 0)
    return gain_sum, bias_sum


def weight_gradient(m, source, shifted, total, lanes, each=None):
    width = lanes.stop - lanes.start
    for du in range(3):
        value = dot(take(source, du, m.high), take(shifted, 1, m.high, lanes), TN)
        into = total.at[..., du * width : (du + 1) * width]
        into[...] = value.reshape(into.shape)
        if each is not None:
            each(du)


def zero_edges(ref):
    blank = jnp.zeros((1,) + ref.shape[1:], ref.dtype)
    ref[0:1] = blank
    ref[ref.shape[0] - 1 : ref.shape[0]] = blank


def diagonal(n):
    return lax.broadcasted_iota(I32, (n, n), 0) == lax.broadcasted_iota(I32, (n, n), 1)


def as_row(column):
    return jnp.sum(jnp.where(diagonal(column.shape[0]), column, 0.0), axis=0, keepdims=True)


def as_column(row):
    return jnp.sum(jnp.where(diagonal(row.shape[1]), row, 0.0), axis=1, keepdims=True)


def step_kernel(cfg, names, *refs):
    r = dict(zip(names, refs))
    dims, images, fused = cfg["dims"], cfg["images"], cfg["fused"]
    big, small = cfg["mask_map"], cfg["grid_map"]
    nm, ng, kc = big.channels, small.channels, cfg["kc"]
    grid, pad = small.live, small.width
    rows, grid_rows = big.high * big.width, small.high * small.width
    gtile = small.span * small.width
    pos = place(dims)
    model = lax.axis_index("mp")
    own_image = lax.axis_index("dp")

    def lanes_of(width, side):
        return pl.ds(pl.multiple_of(side * width, width), width)

    own_m, away_m = lanes_of(nm, model), lanes_of(nm, 1 - model)
    own_g, away_g = lanes_of(ng, model), lanes_of(ng, 1 - model)
    own_x = lanes_of(r["xm_own"].shape[3], model)
    map_rows, grid_span = pl.ds(1, big.high), pl.ds(1, small.high)
    spread_m = group_spread(nm, 2 * nm // GROUPS)
    spread_g = group_spread(ng, 2 * ng // GROUPS)

    greeted = greet_start(dims)

    xm, xg, hm, hg, dm = r["xm"], r["xg"], r["hm"], r["hg"], r["dm"]
    dg1, dg2 = r["dg1"], r["dg2"]
    mask_in, grid_in = r["xm_own"].at[0], r["xg_own"].at[0]
    mask_into = xm.at[map_rows, :, own_x]
    grid_into = xg.at[grid_span, pl.ds(0, grid), own_x]
    local = [
        pltpu.make_async_copy(mask_in, mask_into, r["local"].at[0]),
        pltpu.make_async_copy(grid_in, grid_into, r["local"].at[1]),
    ]
    masks = r["mask_bits"]
    mask_copy = pltpu.make_async_copy(r["masks"].at[:, 0, :], masks, r["local"].at[2])
    for copy in local:
        copy.start()
    mask_copy.start()
    weights = [r["w%d" % i] for i in range(5)]
    groups = []
    if fused:
        for t in range(9):
            for i, value in (
                (0, r["mask_convs"][0, t]),
                (1, r["grid_first"][t]),
                (2, r["mask_convs"][1, t]),
                (3, r["grid_second"][t]),
            ):
                width = value.shape[1]
                weights[i][pos[0], pos[1], pos[2], :, t * width : (t + 1) * width] = value.astype(
                    BF16
                )
        class_in = r["class_conv"]
        for du in range(3):
            pieces = [class_in[3 * du + dv] for dv in range(3)]
            pieces.append(jnp.zeros((class_in.shape[1], 128 - 3 * kc), F32))
            weights[4][pos[0], pos[1], pos[2], :, du * 128 : (du + 1) * 128] = jnp.concatenate(
                pieces, axis=1
            ).astype(BF16)
        groups = gather_groups(dims, weights, r["gs"], r["gr"])

    def bring(*which):
        if fused:
            advance(*[exchange for i in which for exchange in groups[i]])

    greet_end(*greeted)
    bring(0)
    feature_copies = [
        pair_copy(mask_in, mask_into, r["pair"].at[0]),
        pair_copy(grid_in, grid_into, r["pair"].at[1]),
    ]
    feature_copies[0].start()
    bring(1)
    feature_copies[1].start()

    totals = [r["g%d" % i] for i in range(5)]
    out_groups = []
    if fused:
        staged = [weights[2], weights[1], weights[0], r["second_stage"], r["class_stage"]]
        lands = [r["land%d" % i] for i in range(cfg["lands"])]
        out_groups = reduce_groups(dims, totals, staged, lands, r["rs"], r["rr"], cfg["cuts"])

    def send(*which):
        if fused:
            advance(*[exchange for i in which for exchange in out_groups[i]])

    def send_first(i):
        if fused:
            for exchange in out_groups[i]:
                exchange.prepare()
            send(i)

    def send_tap_row(du):
        if not fused:
            return
        third = 3 * nm
        for (_, start, _), exchange in zip(cfg["cuts"][0], out_groups[0]):
            if len(out_groups[0]) == 1 and du == 2 or start // third == du:
                exchange.prepare()
                advance(exchange)

    for ref in (xm, xg, hm, hg, dm, dg1, dg2):
        zero_edges(ref)
    xg[:, grid:, :] = jnp.zeros((xg.shape[0], pad - grid, xg.shape[2]), BF16)
    share = jnp.float32(1.0 / images)
    table, bias_table = r["table"], r["bias_table"]
    slots = r["cells"].shape[1]
    table[...] = jnp.full(table.shape, -(1 << 20), I32)
    table[0:1, 0:slots] = r["cells"][...]
    table[1:2, 0:slots] = r["labels"][...]
    bias_table[...] = jnp.zeros(bias_table.shape, F32)
    bias_table[0:1, 0:kc] = r["class_bias"][...]
    cells = table[0:1, :].astype(F32)
    cells = cells + jnp.floor((cells + 0.5) / grid) * (pad - grid)
    cells_row = cells.astype(I32)
    cells_col = as_column(cells).astype(I32)
    labels_col = as_column(table[1:2, :].astype(F32)).astype(I32) - model * kc
    class_bias = bias_table[0:1, :]
    own_count = r["counts"][own_image]
    slot_lanes = lax.broadcasted_iota(I32, (1, SLOTS), 1)
    slot_rows = lax.broadcasted_iota(I32, (SLOTS, 1), 0)
    own_float = jnp.full((1, 1), own_count, I32).astype(F32)
    live_row = (slot_lanes < own_count).astype(F32)
    live_col = (slot_rows < own_count).astype(F32)
    weight_col = live_col * (share / own_float)
    dice_col = DICE_WEIGHT * weight_col
    focal_scale = share / (own_float + 1.0)
    bring(0)
    bring(0)
    bring(1)

    def weight(i, span):
        def part(du):
            value = weights[i][..., du * span : (du + 1) * span]
            return value.reshape(-1, span) if fused else value

        return part

    mask_one, grid_one, mask_two = weight(0, 3 * nm), weight(1, 3 * ng), weight(2, 3 * nm)
    grid_two, class_two = weight(3, 3 * nm), weight(4, 128)

    norms, gnorms = r["mask_norms"], r["grid_norms"]
    row = lambda ref, k: ref[k : k + 1, :]
    bring(2)
    for copy in local:
        copy.wait()
    feature_copies[0].wait()
    bring(0)
    xh1 = r["xh1"]
    half = big.high // big.span // 2
    total = conv_forward(big, xm, mask_one, xh1, 0, half)
    bring(1)
    total = conv_forward(big, xm, mask_one, xh1, half, None, total)
    bring(2)
    bring(4)
    bring(3)

    def keep_mask(i, value):
        hm[pl.ds(i * big.part + 1, big.part), :, own_m] = value.reshape(big.part, big.width, nm)

    scale_one = norm_forward(big, xh1, total, spread_m, row(norms, 0), row(norms, 1), keep_mask)
    hm_copy = pair_copy(
        hm.at[map_rows, :, own_m], hm.at[map_rows, :, own_m], r["pair"].at[2]
    )
    hm_copy.start()
    feature_copies[1].wait()
    bring(1)
    xhg = r["xhg"]
    total = conv_forward(small, xg, grid_one, xhg, 0, 1)
    bring(2)
    bring(4)
    bring(3)
    total = conv_forward(small, xg, grid_one, xhg, 1, None, total)

    def keep_grid(i, value):
        hg[pl.ds(i * small.part + 1, small.part), :, own_g] = value.reshape(
            small.part, small.width, ng
        )

    scale_grid = norm_forward(
        small, xhg, total, spread_g, row(gnorms, 0), row(gnorms, 1), keep_grid
    )
    hg_copy = pair_copy(
        hg.at[grid_span, :, own_g], hg.at[grid_span, :, own_g], r["pair"].at[3]
    )
    hg_copy.start()

    hm_copy.wait()
    bring(2)
    xh2, feature = r["xh2"], r["feature"]
    half = big.high // big.span // 2
    total = conv_forward(big, hm, mask_two, xh2, 0, half)
    bring(4)
    bring(3)
    total = conv_forward(big, hm, mask_two, xh2, half, None, total)

    def keep_feature(i, value):
        feature[big.at(i, big.part), :] = value

    scale_two = norm_forward(
        big, xh2, total, spread_m, row(norms, 2), row(norms, 3), keep_feature
    )

    hg_copy.wait()
    patches = r["patches"]
    lane = lax.broadcasted_iota(I32, (SLOTS, grid_rows), 1)
    depth = hg.shape[2]
    for t in range(9):
        chosen = (lane == cells_col + ((t // 3 - 1) * pad + t % 3 - 1)).astype(F32).astype(BF16)
        patches[:, t * depth : (t + 1) * depth] = dot(
            chosen, take(hg, 1, small.high), NN
        ).astype(BF16)
    if fused:
        complete(*groups[4])

    class_hot = (
        (lax.broadcasted_iota(I32, (SLOTS, 128), 1) == labels_col).astype(F32).astype(BF16)
    )

    def class_tile(i, sums):
        value = None
        for du in range(3):
            part = dot(take(hg, i * small.span + du, small.span), class_two(du), NN)
            value = part if value is None else value + part
        x = (
            pltpu.roll(value, 1, 0)
            + pltpu.roll(value, 128 - kc, 1)
            + pltpu.roll(pltpu.roll(value, 128 - 2 * kc, 1), gtile - 1, 0)
            + class_bias
        )
        at = lax.broadcasted_iota(I32, (gtile, SLOTS), 0) + i * gtile
        cell_hot = jnp.where(at == cells_row, live_row, 0.0).astype(BF16)
        t = dot(cell_hot, class_hot, NN)
        lanes = lax.broadcasted_iota(I32, (gtile, 128), 1)
        column = lax.broadcasted_iota(I32, (small.span, pad, 128), 1).reshape(gtile, 128)
        real = (column < grid) & (lanes < kc)
        tiny = jnp.exp(-jnp.abs(x))
        extra = jnp.log1p(tiny)
        inverse = 1.0 / (1.0 + tiny)
        q = jnp.where(x >= 0.0, 1.0, tiny) * inverse
        p = jnp.where(x >= 0.0, tiny, 1.0) * inverse
        log_q = -(jnp.maximum(-x, 0.0) + extra)
        log_p = -(jnp.maximum(x, 0.0) + extra)
        terms = FOCAL_ALPHA * t * p * p * log_q + (1.0 - FOCAL_ALPHA) * (1.0 - t) * q * q * log_p
        slope = FOCAL_ALPHA * t * p * p * (p - 2.0 * q * log_q) + (1.0 - FOCAL_ALPHA) * (
            1.0 - t
        ) * q * q * (2.0 * p * log_p - q)
        slope = jnp.where(real, -focal_scale * slope, 0.0).astype(BF16).astype(F32)
        shifted = (
            pltpu.roll(slope, gtile - 1, 0)
            + pltpu.roll(slope, kc, 1)
            + pltpu.roll(pltpu.roll(slope, 2 * kc, 1), 1, 0)
        )
        dg2[pl.ds(i * small.span + 1, small.span), :, 3 * nm :] = shifted.astype(BF16).reshape(
            small.span, pad, 128
        )
        return (
            sums[0] + jnp.sum(jnp.where(real, -focal_scale * terms, 0.0), axis=0, keepdims=True),
            sums[1] + jnp.sum(slope, axis=0, keepdims=True),
        )

    zero = jnp.zeros((1, 128), F32)
    focal_sum, class_bias_sum = lax.fori_loop(
        0, small.high // small.span, class_tile, (zero, zero)
    )

    weight_gradient(small, hg, dg2, totals[4], slice(3 * nm, 3 * nm + 128))

    for group in groups:
        complete(*group)
        for exchange in group:
            exchange.drain()
    picked = None
    for t in range(9):
        w = grid_two(t // 3)[:, (t % 3) * nm : (t % 3 + 1) * nm]
        part = dot(patches[:, t * depth : (t + 1) * depth], w, NN)
        picked = part if picked is None else picked + part
    kernels = r["kernels"]
    kept = (slots + 15) // 16 * 16
    if kept < SLOTS:
        kernels[..., kept:, :] = jnp.zeros(dims + (2, SLOTS - kept, nm), BF16)
    kernels[pos[0], pos[1], pos[2], model, 0:kept] = picked[0:kept].astype(BF16)
    upper = kept // 32 * 16
    kernel_share = [
        gather_exchange(
            dims, kernels, r["ks"], r["kr"], i * line_copies(dims), None, order,
            (model, pl.ds(start, size)),
        )
        for i, (order, start, size) in enumerate(
            ((GATHER_ORDERS[1], 0, upper), (GATHER_ORDERS[2], upper, kept - upper))
        )
    ]
    kernel_cores = core_exchange(kernels, r["pair"].at[7])
    advance(*kernel_share)
    send_first(4)

    kernel_rows = kernels[pos[0], pos[1], pos[2], model]
    logits, logits_in = r["logits"], r["logits_in"]
    high_slots = logits.shape[0]
    tile = big.span * big.width
    for i in range(rows // tile):
        span = slice(i * tile, (i + 1) * tile)
        logits[:, span] = dot(kernel_rows[:high_slots], feature[span, :], NT).astype(BF16)
    logits_copy = pair_copy(logits, logits_in, r["pair"].at[4])
    logits_copy.start()
    advance(*kernel_share)

    logits_copy.wait()
    mask_copy.wait()
    dice_sum = jnp.zeros((1, 1), F32)
    for start in range(0, slots, 16):
        span = slice(start, start + 16)
        x = logits[span, :].astype(F32) + logits_in[span, :].astype(F32)
        s = jax.nn.sigmoid(x)
        mask = masks[start : min(start + 16, slots), :].astype(F32)
        if mask.shape[0] < 16:
            mask = jnp.concatenate([mask, jnp.zeros((16 - mask.shape[0], rows), F32)], axis=0)
        inter = jnp.sum(s * mask, axis=1, keepdims=True)
        whole = jnp.sum(s * s, axis=1, keepdims=True) + jnp.sum(mask, axis=1, keepdims=True) + 1.0
        share_here = dice_col[span]
        dice_sum += jnp.sum(share_here * (1.0 - 2.0 * inter / whole), keepdims=True)
        a = -2.0 * share_here / whole
        b = 2.0 * share_here * inter / (whole * whole)
        logits[span, :] = ((a * mask + 2.0 * b * s) * s * (1.0 - s)).astype(BF16)
    advance(*kernel_share)
    send(4)

    several = 4 if images % 4 == 0 else 1

    def key_block(d):
        index = split_index(dims, d)
        return [kernels[index[0], index[1], index[2], k] for k in range(2)]

    def squares_of(block):
        return sum(
            jnp.sum(jnp.square(part.astype(F32)), axis=1, keepdims=True) for part in block
        )

    same_slot = diagonal(SLOTS)

    def scores(d, own_scale):
        block = key_block(d)
        raw = dot(own_full[0], block[0], NT) + dot(own_full[1], block[1], NT)
        key_scale = lax.rsqrt(as_row(squares_of(block)) + 1e-06)
        scale = own_scale * key_scale / CONTRAST_TEMP
        live = slot_lanes < r["counts"][d]
        allowed = live & jnp.logical_not(same_slot & (d == own_image))
        return block, raw, key_scale, scale, allowed

    def own_key_scale():
        return lax.rsqrt(squares_of(own_full) + 1e-06)

    logit_rows = dot(logits[...], feature[...], NN)
    dlogits, part_rows = logits, big.part * big.width

    def from_logits(i):
        pixels = pl.ds(pl.multiple_of(i * part_rows, part_rows), part_rows)
        return dot(dlogits[:, pixels], kernel_rows[:high_slots], TN)

    gain_two, bias_two = norm_backward(
        big, xh2, from_logits, r["spare"], dm, spread_m, row(norms, 2), row(norms, 3), scale_two
    )
    complete(*kernel_share)
    advance(kernel_cores)
    weight_gradient(big, hm, dm, totals[2], slice(0, 3 * nm))
    send_first(2)
    send(4)
    complete(kernel_cores)
    own_full = [kernels[pos[0], pos[1], pos[2], k] for k in range(2)]
    own_scale = own_key_scale()

    def sum_keys(i, acc):
        for k in range(several):
            _, raw, _, scale, allowed = scores(i * several + k, own_scale)
            value = jnp.where(allowed, jnp.exp(raw * scale), 0.0)
            acc = acc + jnp.sum(value, axis=1, keepdims=True)
        return acc

    totals_col = lax.fori_loop(0, images // several, sum_keys, jnp.zeros((SLOTS, 1), F32))
    contrast_sum = jnp.sum(
        jnp.where(weight_col > 0.0, weight_col * jnp.log(totals_col), 0.0), keepdims=True
    )
    key_totals = r["key_totals"]
    key_totals[pos[0], pos[1], pos[2]] = jnp.broadcast_to(as_row(totals_col), (8, SLOTS))
    total_share = plane_exchange(
        dims,
        key_totals.at[pos[0], pos[1], pos[2]],
        key_totals.at[pos[0]],
        False,
        nothing,
        r["ls"],
        r["lr"],
    )
    advance(total_share)
    hidden = hm

    def input_tile(i, carry):
        value = None
        for du in range(3):
            part = dot(take(dm, i * big.span + 2 - du, big.span), mask_two(du), NT)
            value = part if value is None else value + part
        hidden[pl.ds(i * big.span + 1, big.span)] = value.astype(BF16).reshape(
            big.span, big.width, 2 * nm
        )
        return carry

    lax.fori_loop(0, big.high // big.span, input_tile, 0)
    hidden_copy = pair_copy(hidden.at[map_rows, :, away_m], r["dhm_in"], r["pair"].at[5])
    hidden_copy.start()
    send(2)
    complete(total_share)

    own_scale = own_key_scale()
    query_weight = weight_col / totals_col

    def row_terms(i, acc):
        for k in range(several):
            d = i * several + k
            block, raw, key_scale, scale, allowed = scores(d, own_scale)
            index = split_index(dims, d)
            total_row = key_totals[index[0], index[1], index[2]][0:1]
            value = jnp.where(allowed, jnp.exp(raw * scale), 0.0)
            key_count = jnp.full((1, 1), r["counts"][d], I32).astype(F32)
            query = value * query_weight
            key = value * live_col * (share / key_count / total_row)
            query_low = (query * scale).astype(BF16)
            key_low = (key * scale).astype(BF16)
            mine = jnp.where(model == 0, block[0].astype(F32), block[1].astype(F32)).astype(BF16)
            acc = (
                acc[0] + dot(query_low, mine, NN) + dot(key_low, mine, NN),
                acc[1]
                + jnp.sum((query + key) * raw * key_scale / CONTRAST_TEMP, axis=1, keepdims=True),
            )
        return acc

    row_sum, scale_sum = lax.fori_loop(
        0, images // several, row_terms, (jnp.zeros((SLOTS, nm), F32), jnp.zeros((SLOTS, 1), F32))
    )
    norm_grad = -0.5 * own_scale * own_scale * own_scale * scale_sum
    row_grad = row_sum + 2.0 * kernel_rows.astype(F32) * norm_grad
    row_grad = row_grad + jnp.concatenate(
        [logit_rows, jnp.zeros((SLOTS - high_slots, nm), F32)], axis=0
    )
    row_low = row_grad.astype(BF16)
    for t in range(9):
        value = dot(patches[:, t * depth : (t + 1) * depth], row_low, TN)
        into = totals[3].at[..., t * nm : (t + 1) * nm]
        into[...] = value.reshape(into.shape)
    send_first(3)
    send(2)
    send(4)

    for i in range(small.high // small.span):
        at = lax.broadcasted_iota(I32, (gtile, SLOTS), 0) + i * gtile
        for dv in range(3):
            chosen = (at == cells_row + (dv - 1)).astype(F32).astype(BF16)
            dg2[1 + i * small.span : 1 + (i + 1) * small.span, :, dv * nm : (dv + 1) * nm] = (
                dot(chosen, row_low, NN).astype(BF16).reshape(small.span, pad, nm)
            )
    hidden_grid = hg

    def grid_input_tile(i, carry):
        value = None
        for du in range(3):
            first = i * small.span + 2 - du
            part = dot(take(dg2, first, small.span, slice(0, 3 * nm)), grid_two(du), NT) + dot(
                take(dg2, first, small.span, slice(3 * nm, 3 * nm + 128)), class_two(du), NT
            )
            value = part if value is None else value + part
        hidden_grid[pl.ds(i * small.span + 1, small.span)] = value.astype(BF16).reshape(
            small.span, pad, 2 * ng
        )
        return carry

    lax.fori_loop(0, small.high // small.span, grid_input_tile, 0)
    hidden_grid_copy = pair_copy(
        hidden_grid.at[grid_span, :, away_g], r["dhg_in"], r["pair"].at[6]
    )
    hidden_grid_copy.start()
    send(2)

    hidden_grid_copy.wait()
    hidden_grid_in = r["dhg_in"]

    def both_grid_halves(i):
        mine = take(hidden_grid, i * small.part + 1, small.part, own_g)
        return mine.astype(F32) + take(hidden_grid_in, i * small.part, small.part).astype(F32)

    gain_grid, bias_grid = norm_backward(
        small, xhg, both_grid_halves, r["spare_g"], dg1, spread_g, row(gnorms, 0),
        row(gnorms, 1), scale_grid,
    )
    send(3)
    weight_gradient(small, xg, dg1, totals[1], slice(0, 3 * ng))
    send_first(1)
    send(3)
    hidden_copy.wait()
    hidden_in = r["dhm_in"]

    def both_halves(i):
        mine = take(hidden, i * big.part + 1, big.part, own_m)
        return mine.astype(F32) + take(hidden_in, i * big.part, big.part).astype(F32)

    gain_one, bias_one = norm_backward(
        big, xh1, both_halves, r["spare"], dm, spread_m, row(norms, 0), row(norms, 1), scale_one
    )

    pieces = [gain_one, bias_one, gain_two, bias_two]
    pieces += [gain_grid[:, i : i + nm] for i in range(0, ng, nm)]
    pieces += [bias_grid[:, i : i + nm] for i in range(0, ng, nm)]
    pieces += [class_bias_sum]
    pieces += [jnp.zeros((1, 128), F32)] * (16 - len(pieces))
    small_plane, small_line = r["small_plane"], r["small_line"]
    small_plane[pos[1], pos[2]] = jnp.concatenate(pieces, axis=0)

    def plane_total(plane, cores):
        value = None
        for y in range(dims[1]):
            for x in range(dims[2]):
                for core in range(2) if cores else (None,):
                    part = plane[y, x] if core is None else plane[y, x, core]
                    value = part if value is None else value + part
        return value

    def line_total(line):
        value = line[0]
        for z in range(1, dims[0]):
            value = value + line[z]
        return value

    def small_sum_here():
        small_line[pos[0]] = plane_total(small_plane, False)

    small_share = plane_exchange(
        dims, small_plane.at[pos[1], pos[2]], small_line.at[pos[0]], False, small_sum_here,
        r["ss"], r["sr"],
    )
    advance(small_share)

    def each(du):
        send_tap_row(du)
        if du == 1:
            advance(small_share)
            send(1)
        if du == 2:
            send(3)

    weight_gradient(big, xm, dm, totals[0], slice(0, 3 * nm), each)
    last_group = out_groups[0] if fused else []
    advance(*last_group[:2])
    send(1)
    advance(*last_group[2:])
    complete(small_share)
    small_sum = line_total(small_line)
    r["small_out"][...] = small_sum
    first_model = (model == 0).astype(F32)
    loss = jnp.sum(focal_sum, keepdims=True) + first_model * (dice_sum + contrast_sum)
    if fused:
        squares = (own_image == 0).astype(F32) * jnp.sum(small_sum * small_sum, keepdims=True)

        def hand_out(i):
            complete(*out_groups[i])
            value = totals[i][pos[0], pos[1], pos[2]]
            r["out%d" % i][...] = value
            return jnp.sum(value * value, keepdims=True)

        squares += hand_out(2)
        squares += hand_out(4)
        send(0)
        squares += hand_out(3)
        send(0)
        squares += hand_out(1)
        squares += hand_out(0)
        sum_plane, sum_line = r["sum_plane"], r["sum_line"]
        at = lax.broadcasted_iota(I32, (8, 128), 0)
        sum_plane[pos[1], pos[2], model] = jnp.where(at == 0, squares, loss)

        def sums_here():
            sum_line[pos[0]] = plane_total(sum_plane, True)

        sum_share = plane_exchange(
            dims, sum_plane.at[pos[1], pos[2], model], sum_line.at[pos[0]], True, sums_here,
            r["us"], r["ur"],
        )
        complete(sum_share)
        r["sum_out"][...] = line_total(sum_line)
        sum_share.drain()
    else:
        r["sum_out"][...] = jnp.broadcast_to(loss, (8, 128))
    for shared in kernel_share + [kernel_cores, total_share, small_share]:
        shared.drain()
    for group in out_groups:
        for exchange in group:
            exchange.drain()


def run_step(cfg, inputs, weights, blocks):
    dims, fused = cfg["dims"], cfg["fused"]
    big, small = cfg["mask_map"], cfg["grid_map"]
    nm, ng = big.channels, small.channels
    rows, grid_rows = big.high * big.width, small.high * small.width
    inputs = dict(inputs, **weights)
    spaces = dict(xm_own=ANY, xg_own=ANY, masks=ANY, counts=pltpu.SMEM)
    names = list(inputs)
    specs = [pl.BlockSpec(memory_space=spaces.get(name, VMEM)) for name in names]
    outs = {"small_out": ((16, 128), F32), "sum_out": ((8, 128), F32)}
    scratch = {}
    if fused:
        for i, shape in enumerate(blocks):
            outs["out%d" % i] = (shape[3:], F32)
            scratch["w%d" % i] = VMEM(shape, BF16)
            scratch["g%d" % i] = VMEM(shape, F32)
        gather_cuts = [lane_cuts(shape[-1]) for shape in blocks]
        cuts = [tap_row_cuts(blocks[0][-1])] + gather_cuts[1:]
        lands = landing_scratch(dims, blocks, cuts)
        cfg = dict(cfg, lands=len(lands), cuts=cuts)
        for i, land in enumerate(lands):
            scratch["land%d" % i] = land
        for names_of, used in ((("gs", "gr"), gather_cuts), (("rs", "rr"), cuts)):
            for name in names_of:
                scratch[name] = DMA((flow_slots(dims, used),))
        scratch["class_stage"] = VMEM(blocks[4], BF16)
        scratch["second_stage"] = VMEM(blocks[3], BF16)
        scratch["sum_plane"] = VMEM(dims[1:] + (2, 8, 128), F32)
        scratch["sum_line"] = VMEM(dims[:1] + (8, 128), F32)
        scratch["us"], scratch["ur"] = plane_sems(dims)
    else:
        for i in range(5):
            outs["g%d" % i] = (inputs["w%d" % i].shape, F32)
    c_in = 2 * inputs["xm_own"].shape[3]
    depth = 2 * ng
    slot_rows = -(-inputs["masks"].shape[0] // 16) * 16

    def padded(m, channels):
        return VMEM((m.high + 2, m.width, channels), BF16)

    scratch.update(
        xm=padded(big, c_in),
        xg=padded(small, c_in),
        xh1=VMEM((rows, nm), F32),
        hm=padded(big, 2 * nm),
        xhg=VMEM((grid_rows, ng), F32),
        hg=padded(small, depth),
        xh2=VMEM((rows, nm), F32),
        feature=VMEM((rows, nm), BF16),
        patches=VMEM((SLOTS, 9 * depth), BF16),
        kernels=VMEM(dims + (2, SLOTS, nm), BF16),
        logits=VMEM((slot_rows, rows), BF16),
        logits_in=VMEM((slot_rows, rows), BF16),
        key_totals=VMEM(dims + (8, SLOTS), F32),
        dm=padded(big, 3 * nm),
        spare=VMEM((rows, nm), F32),
        dhm_in=VMEM((big.high, big.width, nm), BF16),
        dg2=padded(small, 3 * nm + 128),
        dhg_in=VMEM((small.high, small.width, ng), BF16),
        dg1=padded(small, 3 * ng),
        spare_g=VMEM((grid_rows, ng), F32),
        small_plane=VMEM(dims[1:] + (16, 128), F32),
        small_line=VMEM(dims[:1] + (16, 128), F32),
        table=VMEM((8, SLOTS), I32),
        bias_table=VMEM((8, 128), F32),
        local=DMA((3,)),
        mask_bits=VMEM((inputs["masks"].shape[0], rows), I32),
        pair=DMA((8, 2)),
    )
    scratch["ks"], scratch["kr"] = share_sems(dims, 2)
    for a, b in (("ls", "lr"), ("ss", "sr")):
        scratch[a], scratch[b] = plane_sems(dims)
    names += list(outs) + list(scratch)
    result = pl.pallas_call(
        partial(step_kernel, cfg, tuple(names)),
        name="step",
        out_shape=[jax.ShapeDtypeStruct(s, d) for s, d in outs.values()],
        in_specs=specs,
        out_specs=[pl.BlockSpec(memory_space=VMEM)] * len(outs),
        scratch_shapes=list(scratch.values()),
        compiler_params=params(0),
    )(*inputs.values())
    return dict(zip(outs, result))


def update_kernel(nm, ng, kc, *refs):
    reduced, small, sums = refs[:5], refs[5], refs[6]
    states, outs = refs[7:28], refs[28:]
    total = sums[0:1, 0:1]
    norm = jnp.sqrt(total)
    outs[0][...] = sums[1:2, 0:1]
    outs[1][...] = norm
    factor = jnp.minimum(1.0, CLIP_LIMIT / norm)

    def update(which, index, gradient, rate):
        old = [states[3 * which + k][index] for k in range(3)]
        new = adam_update(*old, gradient * factor, rate)
        for k in range(3):
            outs[2 + 3 * which + k][index] = new[k]

    for t in range(9):
        update(0, (0, t), reduced[0][:, t * nm : (t + 1) * nm], LEARN_RATE)
        update(0, (1, t), reduced[2][:, t * nm : (t + 1) * nm], LEARN_RATE)
        update(1, (t,), reduced[1][:, t * ng : (t + 1) * ng], LEARN_RATE)
        update(2, (t,), reduced[3][:, t * nm : (t + 1) * nm], LEARN_RATE)
        at = t // 3 * 128 + t % 3 * kc
        update(3, (t,), reduced[4][:, at : at + kc], LEARN_RATE)
    update(4, (slice(None),), small[0:4, :], SMALL_RATE)
    per = ng // nm
    for k in range(2):
        pieces = [small[4 + k * per + i : 5 + k * per + i, :] for i in range(per)]
        update(5, (slice(k, k + 1),), jnp.concatenate(pieces, axis=1), SMALL_RATE)
    at = 4 + 2 * per
    update(6, (slice(None),), small[at : at + 1, :kc], SMALL_RATE)


def run_update(nm, ng, kc, reduced, small, sums, states):
    args = list(reduced) + [small, sums] + list(states)
    shapes = [jax.ShapeDtypeStruct((1, 1), F32)] * 2
    shapes += [jax.ShapeDtypeStruct(s.shape, F32) for s in states]
    return pl.pallas_call(
        partial(update_kernel, nm, ng, kc),
        name="update",
        out_shape=shapes,
        in_specs=[pl.BlockSpec(memory_space=VMEM)] * len(args),
        out_specs=[pl.BlockSpec(memory_space=VMEM)] * len(shapes),
        compiler_params=pltpu.CompilerParams(vmem_limit_bytes=VMEM_LIMIT),
    )(*args)


def lanes_of_taps(weight):
    taps, depth, width = weight.shape
    return weight.transpose(1, 0, 2).reshape(depth, taps * width)


def class_lanes(weight):
    _, depth, width = weight.shape
    rows = weight.transpose(1, 0, 2).reshape(depth, 3, 3 * width)
    return jnp.pad(rows, ((0, 0), (0, 0), (0, 128 - 3 * width))).reshape(depth, 384)


def adam_update(weight, moment, square, gradient, rate):
    moment_new = BETA_ONE * moment + (1.0 - BETA_ONE) * gradient
    square_new = BETA_TWO * square + (1.0 - BETA_TWO) * gradient * gradient
    moment_hat = moment_new / (1.0 - BETA_ONE**STEP_TIME)
    square_hat = square_new / (1.0 - BETA_TWO**STEP_TIME)
    weight_new = weight - rate * (
        moment_hat / (jnp.sqrt(square_hat) + ADAM_EPS) + WEIGHT_DECAY * weight
    )
    return (weight_new, moment_new, square_new)


def body(
    mask_features,
    grid_features,
    instance_cells,
    instance_counts,
    instance_labels,
    instance_masks,
    *states,
):
    images = lax.axis_size("dp")
    data_index = lax.axis_index("dp")
    dims = line_lengths(images)
    mask_convs, grid_first, grid_second, class_conv = states[0:12:3]
    mask_norms, grid_norms, class_bias = states[12::3]
    _, high, wide, half = mask_features.shape
    grid = grid_features.shape[1]
    pad = -(-(grid + 1) // 16) * 16
    nm, ng, kc = mask_convs.shape[3], grid_first.shape[2], class_conv.shape[2]
    fused = grid_first.shape[1] % 16 == 0
    cfg = dict(
        dims=dims,
        images=images,
        mask_map=Map(high, wide, wide, 8, 4, nm, 2 * nm // GROUPS),
        grid_map=Map(grid, pad, grid, grid // 2, grid // 2, ng, 2 * ng // GROUPS),
        kc=kc,
        fused=fused,
    )
    inputs = dict(
        xm_own=mask_features,
        xg_own=grid_features,
        masks=instance_masks.transpose(1, 0, 2),
        counts=instance_counts,
        cells=instance_cells,
        labels=instance_labels,
        mask_norms=mask_norms,
        grid_norms=grid_norms,
        class_bias=class_bias[None, :],
    )
    if fused:
        weights = dict(
            mask_convs=mask_convs,
            grid_first=grid_first,
            grid_second=grid_second,
            class_conv=class_conv,
        )
        blocks = [
            dims + (mask_convs.shape[2], 9 * nm),
            dims + (grid_first.shape[1], 9 * ng),
            dims + (mask_convs.shape[2], 9 * nm),
            dims + (grid_second.shape[1], 9 * nm),
            dims + (class_conv.shape[1], 384),
        ]
        out = run_step(cfg, inputs, weights, blocks)
        reduced = [out["out%d" % i] for i in range(5)]
        sums = out["sum_out"]
    else:
        shards = [
            lanes_of_taps(mask_convs[0].astype(BF16)),
            lanes_of_taps(grid_first.astype(BF16)),
            lanes_of_taps(mask_convs[1].astype(BF16)),
            lanes_of_taps(grid_second.astype(BF16)),
            class_lanes(class_conv.astype(BF16)),
        ]
        gathered = gather_all(dims, shards)
        weights = {"w%d" % i: b.reshape(-1, b.shape[-1]) for i, b in enumerate(gathered)}
        out = run_step(cfg, inputs, weights, None)
        reduced = reduce_all(
            dims, [out["g%d" % i].reshape(b.shape) for i, b in enumerate(gathered)]
        )
        squares = sum(jnp.sum(jnp.square(value)) for value in reduced)
        squares += (data_index == 0).astype(F32) * jnp.sum(jnp.square(out["small_out"]))
        pair = lax.psum((squares, out["sum_out"][0, 0]), ("dp", "mp"))
        sums = jnp.broadcast_to(jnp.pad(jnp.stack(pair), (0, 6))[:, None], (8, 128))
    states = states[:18] + tuple(state[None, :] for state in states[18:])
    result = run_update(nm, ng, kc, reduced, out["small_out"], sums, states)
    result = [value.reshape(()) for value in result[:2]] + list(result[2:])
    return tuple(result[:20]) + tuple(value[0] for value in result[20:])


def solution(mesh):
    in_specs = (
        P("dp", None, None, "mp"),
        P("dp", None, None, "mp"),
        P("dp", None),
        P(),
        P("dp", None),
        P("dp", None, None),
        P(None, None, "dp", "mp"),
        P(None, None, "dp", "mp"),
        P(None, None, "dp", "mp"),
        P(None, "dp", "mp"),
        P(None, "dp", "mp"),
        P(None, "dp", "mp"),
        P(None, "dp", "mp"),
        P(None, "dp", "mp"),
        P(None, "dp", "mp"),
        P(None, "dp", "mp"),
        P(None, "dp", "mp"),
        P(None, "dp", "mp"),
        P(None, "mp"),
        P(None, "mp"),
        P(None, "mp"),
        P(None, "mp"),
        P(None, "mp"),
        P(None, "mp"),
        P("mp"),
        P("mp"),
        P("mp"),
    )
    out_specs = (
        P(),
        P(),
        P(None, None, "dp", "mp"),
        P(None, None, "dp", "mp"),
        P(None, None, "dp", "mp"),
        P(None, "dp", "mp"),
        P(None, "dp", "mp"),
        P(None, "dp", "mp"),
        P(None, "dp", "mp"),
        P(None, "dp", "mp"),
        P(None, "dp", "mp"),
        P(None, "dp", "mp"),
        P(None, "dp", "mp"),
        P(None, "dp", "mp"),
        P(None, "mp"),
        P(None, "mp"),
        P(None, "mp"),
        P(None, "mp"),
        P(None, "mp"),
        P(None, "mp"),
        P("mp"),
        P("mp"),
        P("mp"),
    )
    return jax.shard_map(body, mesh=mesh, in_specs=in_specs, out_specs=out_specs, check_vma=False)
```
